32 devices in a mesh: dp: 8 (over z, core), mp: 4 (over y, x).
Axes of the slice: x: 2, y: 2, z: 4, core: 2. Of those that a mesh axis runs over, the one named last changes fastest.
Arguments:
- tokens: bfloat16 [2048, 3072], P('dp'), may hold values from -60 to 60
- ln_gain: float32 [3072], replicated, may hold values from 0.25 to 1.75
- q_weight: bfloat16 [3072, 4096], P('dp', 'mp'), may hold values from -1 to 1
- k_weight: bfloat16 [3072, 4096], P('dp', 'mp'), may hold values from -1 to 1
- v_weight: bfloat16 [3072, 4096], P('dp', 'mp'), may hold values from -0.109375 to 0.109375
- q_gain: float32 [4096], P('mp'), may hold values from 0.6 to 6
- k_gain: float32 [4096], P('mp'), may hold values from 0.6 to 6
- out_weight: bfloat16 [3072, 4096], P('dp', 'mp'), may hold values from -0.25 to 0.25
Outputs:
- mixed: bfloat16 [2048, 3072], P(('dp', 'mp'))
The draws below stay inside these ranges and needn't reach their ends.
All inputs are finite; a program needn't handle non-finite values.
Results may differ from the reference program's by a relative error of at most 0.018.
Values may be sent and summed in bfloat16 or wider, within the bound.
A program may use at most 128 MiB of HBM per device.

```python
import math
import jax
import jax.numpy as jnp
from jax import lax

D = 3072
HEADS = 32
HEAD_DIM = 128
IMG_TOKENS = 256
TOKENS = 2048
N_MP = 4


def draw_tokens(key, part):
    base = jax.random.normal(jax.random.fold_in(key, 21), (TOKENS, D), jnp.float32)
    result = base
    return jnp.clip(result, -60.0, 60.0).astype(jnp.bfloat16)


def weight_pair(key):
    shape = (D, HEADS * HEAD_DIM)
    first = jnp.clip(jax.random.normal(jax.random.fold_in(key, 31), shape, jnp.float32), -4.0, 4.0) * D ** (-0.5)
    second = jnp.clip(jax.random.normal(jax.random.fold_in(key, 32), shape, jnp.float32), -4.0, 4.0) * D ** (-0.5)
    return (first, second)


def draw_q_weight(key, part):
    return weight_pair(key)[0].astype(jnp.bfloat16)


def draw_k_weight(key, part):
    return weight_pair(key)[1].astype(jnp.bfloat16)


def gain_draw(key):
    return jax.random.uniform(key, (HEADS * HEAD_DIM,), jnp.float32, 0.6, 1.4)


def draw_q_gain(key, part):
    return gain_draw(jax.random.fold_in(key, 41))


def draw_k_gain(key, part):
    return gain_draw(jax.random.fold_in(key, 42))


def steps_of(own_key, shape, shards, smallest, largest):
    loudness = 1.0
    for axis_at, parts in shards:
        heights = jax.random.uniform(jax.random.fold_in(jax.random.fold_in(own_key, 6), axis_at), (parts,), jnp.float32, smallest / len(shards), largest / len(shards))
        loudness = loudness * jnp.repeat(jnp.exp(heights), shape[axis_at] // parts).reshape((-1,) + (1,) * (len(shape) - 1 - axis_at))
    return loudness


def gaussian(own_key, dims, width, reach, cuts=(), kind=jnp.bfloat16):
    entries = jax.random.normal(own_key, dims, jnp.float32) * width
    if len(cuts) > 0:
        entries = steps_of(own_key, dims, cuts, -0.22, 0.18) * entries
    return jnp.clip(entries, min=-reach, max=reach).astype(kind)


def setup_inputs(seed: int = 0) -> dict:
    splits = jax.random.split(jax.random.key(seed), 9)
    return {
        "tokens": draw_tokens(jax.random.fold_in(splits[8], 71), 0),
        "ln_gain": jnp.clip(1.0 + 0.15 * jax.random.normal(splits[1], (D,), jnp.float32), 0.25, 1.75),
        "q_weight": draw_q_weight(jax.random.fold_in(splits[8], 71), 0),
        "k_weight": draw_k_weight(jax.random.fold_in(splits[8], 71), 0),
        "v_weight": gaussian(splits[4], (D, HEADS * HEAD_DIM), D ** -0.5, 0.109375, ((0, 8), (1, 4))),
        "q_gain": draw_q_gain(jax.random.fold_in(splits[8], 71), 0),
        "k_gain": draw_k_gain(jax.random.fold_in(splits[8], 71), 0),
        "out_weight": gaussian(splits[7], (D, HEADS * HEAD_DIM), (HEADS * HEAD_DIM // 8) ** -0.5, 0.25, ((0, 8), (1, 4))),
    }


epsilon = 1e-06

def layer_norm(values, scale_gain):
    average = lax.optimization_barrier(jnp.mean(values, axis=-1, keepdims=True))
    centred = values - average
    variance = lax.optimization_barrier(jnp.mean(centred * centred, axis=-1, keepdims=True))
    return centred * lax.rsqrt(variance + epsilon) * scale_gain

def head_norm(projected, scale_gain):
    heads_count = projected.shape[1] // HEAD_DIM
    shaped = projected.reshape(projected.shape[0], heads_count, HEAD_DIM)
    normed = layer_norm(shaped, scale_gain.reshape(heads_count, HEAD_DIM))
    return normed.reshape(projected.shape).astype(jnp.bfloat16)

def attend_image(triple):
    queries = triple[0].astype(jnp.float32)
    key_rows = triple[1].astype(jnp.float32)
    value_rows = triple[2].astype(jnp.float32)
    scores = jnp.einsum('qhd,khd->hqk', queries, key_rows) * (1.0 / math.sqrt(HEAD_DIM))
    highest = lax.optimization_barrier(jnp.max(scores, axis=-1, keepdims=True))
    weights = jnp.exp(scores - highest)
    probs = (weights / lax.optimization_barrier(jnp.sum(weights, axis=-1, keepdims=True))).astype(jnp.bfloat16)
    context = jnp.einsum('hqk,khd->qhd', probs.astype(jnp.float32), value_rows)
    return context.astype(jnp.bfloat16)

def reference(tokens, ln_gain, q_weight, k_weight, v_weight, q_gain, k_gain, out_weight):
    normed = layer_norm(tokens.astype(jnp.float32), ln_gain).astype(jnp.bfloat16)
    queries = jnp.dot(normed, q_weight, preferred_element_type=jnp.float32)
    key_rows = jnp.dot(normed, k_weight, preferred_element_type=jnp.float32)
    value_rows = jnp.dot(normed, v_weight, preferred_element_type=jnp.float32).astype(jnp.bfloat16)
    query_normed = head_norm(queries, q_gain)
    key_normed = head_norm(key_rows, k_gain)
    images = TOKENS // IMG_TOKENS
    shaped = (images, IMG_TOKENS, HEADS, HEAD_DIM)
    context = lax.map(attend_image, (query_normed.reshape(shaped), key_normed.reshape(shaped), value_rows.reshape(shaped)))
    context = context.reshape(TOKENS, HEADS * HEAD_DIM)
    group_width = HEADS * HEAD_DIM // N_MP
    context_groups = context.reshape(TOKENS, N_MP, group_width).transpose(1, 0, 2)
    weight_groups = out_weight.reshape(D, N_MP, group_width).transpose(1, 0, 2)

    def add_group(total, paired):
        partial_sum = lax.dot_general(paired[0], paired[1], (((1,), (1,)), ((), ())), preferred_element_type=jnp.float32)
        rounded = lax.optimization_barrier(partial_sum.astype(jnp.bfloat16))
        return (total + rounded.astype(jnp.float32), None)
    total, unused = lax.scan(add_group, jnp.zeros((TOKENS, D), jnp.float32), (context_groups, weight_groups))
    return total.astype(jnp.bfloat16)
```

```python
import functools
import math

import jax
import jax.numpy as jnp
from jax import lax
from jax.experimental import pallas as pl
from jax.experimental.pallas import tpu as pltpu
from jax.sharding import PartitionSpec as P

HEAD_DIM = 128
IMG_TOKENS = 256


epsilon = 1e-06


def layer_norm(values, scale_gain):
    average = jnp.mean(values, axis=-1, keepdims=True)
    centred = values - average
    variance = jnp.mean(centred * centred, axis=-1, keepdims=True)
    return centred * lax.rsqrt(variance + epsilon) * scale_gain


def head_norm(projected, scale_gain):
    heads_count = projected.shape[1] // HEAD_DIM
    shaped = projected.reshape(projected.shape[0], heads_count, HEAD_DIM)
    normed = layer_norm(shaped, scale_gain.reshape(heads_count, HEAD_DIM))
    return normed.reshape(projected.shape).astype(jnp.bfloat16)


def attend(queries, key_rows, value_rows):
    scores = jnp.einsum(
        "bqhd,bkhd->bhqk", queries, key_rows, preferred_element_type=jnp.float32
    ) * (1.0 / math.sqrt(HEAD_DIM))
    highest = jnp.max(scores, axis=-1, keepdims=True)
    weights = jnp.exp(scores - highest)
    probs = (weights / jnp.sum(weights, axis=-1, keepdims=True)).astype(jnp.bfloat16)
    context = jnp.einsum("bhqk,bkhd->bqhd", probs, value_rows, preferred_element_type=jnp.float32)
    return context.astype(jnp.bfloat16)


def place_three(holder, pieces, offset, local_width):
    holder = lax.dynamic_update_slice(holder, pieces[0], (offset, 0))
    holder = lax.dynamic_update_slice(holder, pieces[1], (offset, local_width))
    return lax.dynamic_update_slice(holder, pieces[2], (offset, 2 * local_width))


def gathered_weights(tokens, ln_gain, q_weight, k_weight, v_weight, q_gain, k_gain, out_weight):
    normed = layer_norm(tokens.astype(jnp.float32), ln_gain).astype(jnp.bfloat16)
    token_count = normed.shape[0]
    local_width = q_weight.shape[1]
    feature_count = normed.shape[1]
    stacked = jnp.zeros((feature_count, 3 * local_width), jnp.bfloat16)
    projections = place_three(
        stacked,
        (
            lax.all_gather(q_weight, "dp", axis=0, tiled=True),
            lax.all_gather(k_weight, "dp", axis=0, tiled=True),
            lax.all_gather(v_weight, "dp", axis=0, tiled=True),
        ),
        jnp.int32(0),
        local_width,
    )
    combined = jnp.dot(normed, projections, preferred_element_type=jnp.float32)
    queries = combined[:, :local_width]
    key_rows = combined[:, local_width : 2 * local_width]
    value_cast = combined[:, 2 * local_width :].astype(jnp.bfloat16)
    query_normed = head_norm(queries, q_gain)
    key_normed = head_norm(key_rows, k_gain)
    images = token_count // IMG_TOKENS
    shaped = (images, IMG_TOKENS, local_width // HEAD_DIM, HEAD_DIM)
    context = attend(
        query_normed.reshape(shaped), key_normed.reshape(shaped), value_cast.reshape(shaped)
    )
    context = context.reshape(token_count, local_width)
    out_full = lax.all_gather(out_weight, "dp", axis=0, tiled=True)
    return lax.psum_scatter(
        lax.dot_general(
            context, out_full, (((1,), (1,)), ((), ())), preferred_element_type=jnp.float32
        ).astype(jnp.bfloat16),
        "mp",
        scatter_dimension=0,
        tiled=True,
    )


MESH = pl.DeviceIdType.MESH

CHUNKS = 4


def exchange_kernel(
    pairs, groups, chunks, tokens, ln_gain, q_w, k_w, v_w, q_gain, k_gain, out_w, result,
    raw, normed, weights, out_rows, context, partial, arrived, summed, final,
    local_sem, token_send, token_recv, peer_send, peer_recv,
    w_send, w_recv, own_send, own_recv, pass_send, pass_recv, out_send, out_recv,
    c_send, c_recv, p_send, p_recv, f_send, f_recv,
):
    dp = lax.axis_index("dp")
    group = lax.axis_index("mp")
    pair = dp // 2
    core = dp % 2
    rows = tokens.shape[0]
    part = rows // groups
    piece_rows = part // chunks
    shard = q_w.shape[0]
    width = q_w.shape[1] // pairs
    span = 2 * shard
    heads = width // HEAD_DIM
    has_up = pair + 1 < pairs
    has_down = pair > 0

    def at_pair(other):
        return (other * 2 + core, group)

    partner = (pair * 2 + (1 - core), group)

    def at_group(other):
        return (dp, other)

    def remote(source, target, send, recv, device):
        return pltpu.make_async_remote_copy(
            src_ref=source, dst_ref=target, send_sem=send, recv_sem=recv,
            device_id=device, device_id_type=MESH,
        )

    def quarter_of(owner):
        return pl.ds(pl.multiple_of(owner * part, part), part)

    token_quarters = []
    for j in range(groups):
        place = quarter_of((group + j) % groups)
        token_quarters.append(
            pltpu.make_async_copy(tokens.at[place, :], raw.at[place, :], local_sem.at[j])
        )
        token_quarters[j].start()

    projections = (q_w, k_w, v_w)

    def columns(other, h, t):
        start = pl.multiple_of(other * width + h * HEAD_DIM, HEAD_DIM)
        return projections[t].at[:, pl.ds(start, HEAD_DIM)]

    def slot(h, block, side, t):
        return weights.at[h, block, side, :, pl.ds(t * HEAD_DIM, HEAD_DIM)]

    greeted = pltpu.get_barrier_semaphore()
    for step in range(1, pairs):
        pl.semaphore_signal(
            greeted, inc=1, device_id=at_pair((pair + step) % pairs), device_id_type=MESH
        )
    for step in range(1, groups):
        pl.semaphore_signal(
            greeted, inc=1, device_id=at_group((group + step) % groups), device_id_type=MESH
        )
    pl.semaphore_signal(greeted, inc=1, device_id=partner, device_id_type=MESH)

    locals_ = [pltpu.make_async_copy(out_w, out_rows.at[core], local_sem.at[groups])]
    for h in range(heads):
        for t in range(3):
            locals_.append(
                pltpu.make_async_copy(
                    columns(pair, h, t), slot(h, pair, core, t),
                    local_sem.at[groups + 1 + 3 * h + t],
                )
            )
    for copy in locals_:
        copy.start()

    def normalise(first_row, count):
        @pl.loop(0, count // 16)
        def _(step):
            place = pl.ds(pl.multiple_of(first_row + step * 16, 16), 16)
            values = raw[place, :].astype(jnp.float32)
            average = jnp.mean(values, axis=-1, keepdims=True)
            centred = values - average
            variance = jnp.mean(centred * centred, axis=-1, keepdims=True)
            scaled = centred * lax.rsqrt(variance + epsilon) * ln_gain[...]
            normed[pair, place, :] = scaled.astype(jnp.bfloat16)

    token_quarters[0].wait()
    normalise(group * part, part)

    def piece(block, owner, k):
        start = pl.multiple_of(owner * part + k * piece_rows, 16)
        return normed.at[block, pl.ds(start, piece_rows), :]

    def z_hop(block, k, up):
        there = piece(block, group, k)
        return remote(
            there, there, token_send.at[0 if up else 1, block], token_recv.at[block, k],
            at_pair(pair + 1 if up else pair - 1),
        )

    beside = group + 1 - 2 * (group % 2)
    across = (group + 2) % 4
    first = jnp.where(core == 0, beside, across)
    second = jnp.where(core == 0, across, beside)
    opposite = 3 - group

    def peer_copy(block, owner, place, k, other):
        there = piece(block, owner, k)
        return remote(
            there, there, peer_send.at[block, place], peer_recv.at[block, owner, k], at_group(other)
        )

    def weight_to(other, h, t):
        return remote(
            columns(other, h, t), slot(h, pair, core, t),
            w_send.at[other, h], w_recv.at[pair, h], at_pair(other),
        )

    def send_weights(up, some):
        for h in some:
            for distance in range(1, pairs):
                other = pair + distance if up else pair - distance

                @pl.when(other < pairs if up else other >= 0)
                def _():
                    for t in range(3):
                        weight_to(other, h, t).start()

    def own_weight(h, t):
        return remote(
            columns(pair, h, t), slot(h, pair, core, t), own_send, own_recv, partner
        )

    def out_over():
        return remote(out_w, out_rows.at[core], out_send, out_recv, partner)

    with jax.named_scope("greet"):
        pl.semaphore_wait(greeted, pairs + groups - 1)

    @pl.loop(0, chunks)
    def _(k):
        @pl.when(has_up)
        def _():
            z_hop(pair, k, True).start()

        @pl.when(has_down)
        def _():
            z_hop(pair, k, False).start()

    @pl.when(pair == 0)
    def _():
        send_weights(True, range(heads))

    @pl.when(pair == pairs - 1)
    def _():
        send_weights(False, range(heads))

    for h in range(heads):
        for t in range(3):
            own_weight(h, t).start()
    out_over().start()
    for j in range(1, groups):
        token_quarters[j].wait()

    def relay(block, k, up):
        with jax.named_scope("relaywait"):
            z_hop(block, k, up).wait_recv()

        @pl.when(has_up if up else has_down)
        def _():
            z_hop(block, k, up).start()

        peer_copy(block, group, 0, k, first).start()
        peer_copy(block, group, 1, k, second).start()

    others = rows - part
    for distance in range(1, pairs):
        @pl.loop(0, chunks)
        def _(k):
            @pl.when(pair - distance >= 0)
            def _():
                relay(pair - distance, k, True)

            @pl.when(pair + distance < pairs)
            def _():
                relay(pair + distance, k, False)

            if distance == 1:
                for j in range(1, groups):
                    normalise(((group + j) % groups) * part + k * piece_rows, piece_rows)

        @pl.when(has_up & (pair == distance))
        def _():
            send_weights(True, range(1))

            @pl.when(pair + 2 < pairs)
            def _():
                send_weights(True, range(1, heads))

        @pl.when(has_down & (pair == pairs - 1 - distance))
        def _():
            send_weights(False, range(1))

            @pl.when(pair - 2 >= 0)
            def _():
                send_weights(False, range(1, heads))

    def cross_tokens(block, k):
        with jax.named_scope("crosswait"):
            peer_copy(block, first, 0, k, first).wait_recv()
        peer_copy(block, first, 2, k, second).start()

    for distance in range(1, pairs):
        @pl.loop(0, chunks)
        def _(k):
            @pl.when(pair - distance >= 0)
            def _():
                cross_tokens(pair - distance, k)

            @pl.when(pair + distance < pairs)
            def _():
                cross_tokens(pair + distance, k)

    @pl.when(has_up & (pair == pairs - 2))
    def _():
        send_weights(True, range(1, heads))

    @pl.when(has_down & (pair == 1))
    def _():
        send_weights(False, range(1, heads))

    def pass_on(other, h):
        there = weights.at[h, other, core]
        return remote(there, there, pass_send.at[h], pass_recv.at[h], partner)

    def pass_weights(h):
        for distance in range(1, pairs):
            for up in (True, False):
                other = pair - distance if up else pair + distance

                @pl.when(other >= 0 if up else other < pairs)
                def _():
                    there = weights.at[h, other, core]
                    with jax.named_scope("wwait"):
                        remote(
                            there, there, w_send.at[other, h], w_recv.at[other, h], at_pair(other)
                        ).wait_recv()
                    pass_on(other, h).start()

    def all_passed(h):
        there = weights.at[h, pl.ds(0, pairs - 1), 1 - core]
        return remote(there, there, pass_send.at[h], pass_recv.at[h], partner)

    def all_own():
        there = weights.at[:, pair, 1 - core]
        return remote(there, there, own_send, own_recv, partner)

    pass_weights(0)
    for copy in locals_:
        copy.wait()
    all_own().wait_recv()
    for distance in range(1, pairs):
        for below in (True, False):
            block = pair - distance if below else pair + distance

            @pl.when(block >= 0 if below else block < pairs)
            def _():
                with jax.named_scope("tokwait"):
                    @pl.loop(0, chunks)
                    def _(k):
                        peer_copy(block, second, 0, k, second).wait_recv()
                        peer_copy(block, opposite, 0, k, second).wait_recv()

    def head_layer_norm(values, scale_gain):
        average = jnp.mean(values, axis=-1, keepdims=True)
        centred = values - average
        variance = jnp.mean(centred * centred, axis=-1, keepdims=True)
        return (centred * lax.rsqrt(variance + epsilon) * scale_gain).astype(jnp.bfloat16)

    def head_place(block, h):
        return pl.ds(pl.multiple_of(block * width + h * HEAD_DIM, HEAD_DIM), HEAD_DIM)

    def context_hop(block, image, h, up):
        there = context.at[image, :, head_place(block, h)]
        return remote(
            there, there,
            c_send.at[0 if up else 1, block, h], c_recv.at[block, image, h],
            at_pair(pair + 1 if up else pair - 1),
        )

    def pass_context(image, h, distance):
        for up in (True, False):
            block = pair - distance if up else pair + distance

            @pl.when(block >= 0 if up else block < pairs)
            def _():
                with jax.named_scope("ctxwait"):
                    context_hop(block, image, h, up).wait_recv()

                @pl.when(has_up if up else has_down)
                def _():
                    context_hop(block, image, h, up).start()

    def attend_head(image, h):
        lanes = slice(h * HEAD_DIM, (h + 1) * HEAD_DIM)
        with jax.named_scope("attend"):
            total = jnp.dot(
                normed[image], weights[h].reshape(pairs * span, 3 * HEAD_DIM),
                preferred_element_type=jnp.float32,
            )
            queries = head_layer_norm(total[:, :HEAD_DIM], q_gain[pair, :, lanes])
            key_rows = head_layer_norm(total[:, HEAD_DIM : 2 * HEAD_DIM], k_gain[pair, :, lanes])
            value_rows = total[:, 2 * HEAD_DIM :].astype(jnp.bfloat16)
            scores = lax.dot_general(
                queries, key_rows, (((1,), (1,)), ((), ())), preferred_element_type=jnp.float32
            ) * (1.0 / math.sqrt(HEAD_DIM))
            highest = jnp.max(scores, axis=-1, keepdims=True)
            spread = jnp.exp(scores - highest)
            probs = (spread / jnp.sum(spread, axis=-1, keepdims=True)).astype(jnp.bfloat16)
            mixed = jnp.dot(probs, value_rows, preferred_element_type=jnp.float32)
            context[image, :, head_place(pair, h)] = mixed.astype(jnp.bfloat16)

        @pl.when(has_up)
        def _():
            context_hop(pair, image, h, True).start()

        @pl.when(has_down)
        def _():
            context_hop(pair, image, h, False).start()

    for h in range(heads):
        if h > 0:
            pass_weights(h)
        with jax.named_scope("passedwait"):
            all_passed(h).wait_recv()

        @pl.loop(0, pairs)
        def _(image):
            attend_head(image, h)
            if h > 0:
                pass_context(image, h - 1, 1)

        if h == 0:
            with jax.named_scope("sends"):
                for distance in range(pairs):
                    for up in (True, False):
                        if distance == 0 and not up:
                            continue
                        block = pair - distance if up else pair + distance

                        @pl.when(block >= 0 if up else block < pairs)
                        def _():
                            quarter = normed.at[block, quarter_of(group), :]
                            for way, there in ((0, has_up), (1, has_down)):
                                if distance > 0 and way != (0 if up else 1):
                                    continue

                                @pl.when(there)
                                def _():
                                    remote(
                                        quarter, quarter, token_send.at[way, block],
                                        token_recv.at[block, 0], partner,
                                    ).wait_send()

                            if distance > 0:
                                for place in range(3):
                                    remote(
                                        quarter, quarter, peer_send.at[block, place],
                                        peer_recv.at[block, 0, 0], partner,
                                    ).wait_send()
                all_own().wait_send()
                out_back = remote(out_rows.at[1 - core], out_rows.at[1 - core], out_send, out_recv, partner)
                out_back.wait_recv()
                out_back.wait_send()

    for distance in range(2, pairs):
        for h in range(heads - 1):
            @pl.loop(0, pairs)
            def _(image):
                pass_context(image, h, distance)

    def partial_to(image, step):
        other = (group + step) % groups
        return remote(
            partial.at[image, quarter_of(other), :], arrived.at[image, step - 1],
            p_send.at[image], p_recv.at[image], at_group(other),
        )

    def partials(image):
        there = arrived.at[image]
        return remote(there, there, p_send.at[image], p_recv.at[image], partner)

    def final_to(image):
        return remote(summed.at[image], final.at[pair], f_send, f_recv, at_pair(image))

    def finals():
        there = final.at[pl.ds(0, pairs - 1)]
        return remote(there, there, f_send, f_recv, partner)

    def finish(image):
        with jax.named_scope("partwait"):
            partials(image).wait_recv()
        total = partial[image, quarter_of(group), :].astype(jnp.float32)
        for step in range(1, groups):
            total = total + arrived[image, step - 1].astype(jnp.float32)
        summed[image] = total.astype(jnp.bfloat16)

        @pl.when(image != pair)
        def _():
            final_to(image).start()

        @pl.when(image == pair)
        def _():
            final[pair] = summed[image]

    @pl.loop(0, pairs)
    def _(image):
        for distance in range(1, pairs):
            pass_context(image, heads - 1, distance)

        with jax.named_scope("outproj"):
            for c in range(2):
                product = lax.dot_general(
                    context[image], out_rows[c], (((1,), (1,)), ((), ())),
                    preferred_element_type=jnp.float32,
                )
                partial[image, :, c * shard : (c + 1) * shard] = product.astype(jnp.bfloat16)
        for step in range(1, groups):
            partial_to(image, step).start()

        @pl.when(image > 0)
        def _():
            finish(image - 1)

    with jax.named_scope("sends2"):
        for h in range(heads):
            own = weights.at[h, pl.ds(0, pairs - 1), core]
            remote(own, own, pass_send.at[h], pass_recv.at[h], partner).wait_send()
        for distance in range(1, pairs):
            for below in (True, False):
                other = pair - distance if below else pair + distance

                @pl.when(other >= 0 if below else other < pairs)
                def _():
                    for h in range(heads):
                        there = weights.at[h, pair, core]
                        remote(
                            there, there, w_send.at[other, h], w_recv.at[other, h], partner
                        ).wait_send()

    finish(pairs - 1)

    with jax.named_scope("sends3"):
        for distance in range(pairs):
            for up in (True, False):
                block = pair - distance if up else pair + distance

                @pl.when((block >= 0 if up else block < pairs) & (has_up if up else has_down))
                def _():
                    for h in range(heads):
                        there = context.at[:, :, head_place(block, h)]
                        remote(
                            there, there, c_send.at[0 if up else 1, block, h],
                            c_recv.at[block, 0, h], partner,
                        ).wait_send()

        @pl.loop(0, pairs)
        def _(image):
            partials(image).wait_send()

    with jax.named_scope("finalwait"):
        finals().wait_recv()
    for p in range(pairs):
        result[:, p * span : (p + 1) * span] = final[p]
    with jax.named_scope("sends4"):
        finals().wait_send()


def exchanged_heads(pairs, groups, tokens, ln_gain, q_w, k_w, v_w, q_gain, k_gain, out_w):
    rows, features = tokens.shape
    shard, local_width = q_w.shape
    width = local_width // pairs
    heads = width // HEAD_DIM
    part = rows // groups
    chunks = min(CHUNKS, part // 16)
    dma = pltpu.SemaphoreType.DMA
    in_hbm = pl.BlockSpec(memory_space=pl.ANY)
    in_vmem = pl.BlockSpec(memory_space=pltpu.VMEM)
    bf16 = jnp.bfloat16
    return pl.pallas_call(
        functools.partial(exchange_kernel, pairs, groups, chunks),
        out_shape=jax.ShapeDtypeStruct((part, features), bf16),
        in_specs=[in_hbm, in_vmem, in_hbm, in_hbm, in_hbm, in_vmem, in_vmem, in_hbm],
        out_specs=in_vmem,
        scratch_shapes=[
            pltpu.VMEM((rows, features), bf16),
            pltpu.VMEM((pairs, rows, features), bf16),
            pltpu.VMEM((heads, pairs, 2, shard, 3 * HEAD_DIM), bf16),
            pltpu.VMEM((2, shard, local_width), bf16),
            pltpu.VMEM((pairs, rows, local_width), bf16),
            pltpu.VMEM((pairs, rows, 2 * shard), bf16),
            pltpu.VMEM((pairs, groups - 1, part, 2 * shard), bf16),
            pltpu.VMEM((pairs, part, 2 * shard), bf16),
            pltpu.VMEM((pairs, part, 2 * shard), bf16),
            dma((groups + 1 + 3 * heads,)), dma((2, pairs)), dma((pairs, chunks)),
            dma((pairs, 3)), dma((pairs, groups, chunks)),
            dma((pairs, heads)), dma((pairs, heads)), dma, dma,
            dma((heads,)), dma((heads,)), dma, dma,
            dma((2, pairs, heads)), dma((pairs, pairs, heads)),
            dma((pairs,)), dma((pairs,)), dma, dma,
        ],
        compiler_params=pltpu.CompilerParams(
            collective_id=0, has_side_effects=True, vmem_limit_bytes=60 * 1024 * 1024
        ),
    )(
        tokens, ln_gain.reshape(1, features), q_w, k_w, v_w,
        q_gain.reshape(pairs, 1, width), k_gain.reshape(pairs, 1, width), out_w,
    )


def on_device(tokens, ln_gain, q_w, k_w, v_w, q_gain, k_gain, out_w):
    devices = lax.axis_size("dp")
    groups = lax.axis_size("mp")
    pairs = devices // 2
    fits = (
        devices % 2 == 0
        and pairs > 1
        and groups == 4
        and q_w.shape[1] % (pairs * HEAD_DIM) == 0
        and q_w.shape[0] % 128 == 0
        and tokens.shape[0] == IMG_TOKENS
        and tokens.shape[0] % (16 * groups) == 0
        and pairs <= 4
        and q_w.shape[1] <= 2 * pairs * HEAD_DIM
    )
    if fits:
        return exchanged_heads(pairs, groups, tokens, ln_gain, q_w, k_w, v_w, q_gain, k_gain, out_w)
    return gathered_weights(tokens, ln_gain, q_w, k_w, v_w, q_gain, k_gain, out_w)


def solution(mesh):
    in_specs = (
        P("dp", None),
        P(),
        P("dp", "mp"),
        P("dp", "mp"),
        P("dp", "mp"),
        P("mp"),
        P("mp"),
        P("dp", "mp"),
    )
    out_specs = P(("dp", "mp"), None)
    return jax.shard_map(
        on_device, mesh=mesh, in_specs=in_specs, out_specs=out_specs, check_vma=False
    )
```

```python
import functools
import math

import jax
import jax.numpy as jnp
from jax import lax
from jax.experimental import pallas as pl
from jax.experimental.pallas import tpu as pltpu
from jax.sharding import PartitionSpec as P

HEAD_DIM = 128
IMG_TOKENS = 256


epsilon = 1e-06


def layer_norm(values, scale_gain):
    average = jnp.mean(values, axis=-1, keepdims=True)
    centred = values - average
    variance = jnp.mean(centred * centred, axis=-1, keepdims=True)
    return centred * lax.rsqrt(variance + epsilon) * scale_gain


def head_norm(projected, scale_gain):
    heads_count = projected.shape[1] // HEAD_DIM
    shaped = projected.reshape(projected.shape[0], heads_count, HEAD_DIM)
    normed = layer_norm(shaped, scale_gain.reshape(heads_count, HEAD_DIM))
    return normed.reshape(projected.shape).astype(jnp.bfloat16)


def attend(queries, key_rows, value_rows):
    scores = jnp.einsum(
        "bqhd,bkhd->bhqk", queries, key_rows, preferred_element_type=jnp.float32
    ) * (1.0 / math.sqrt(HEAD_DIM))
    highest = jnp.max(scores, axis=-1, keepdims=True)
    weights = jnp.exp(scores - highest)
    probs = (weights / jnp.sum(weights, axis=-1, keepdims=True)).astype(jnp.bfloat16)
    context = jnp.einsum("bhqk,bkhd->bqhd", probs, value_rows, preferred_element_type=jnp.float32)
    return context.astype(jnp.bfloat16)


def place_three(holder, pieces, offset, local_width):
    holder = lax.dynamic_update_slice(holder, pieces[0], (offset, 0))
    holder = lax.dynamic_update_slice(holder, pieces[1], (offset, local_width))
    return lax.dynamic_update_slice(holder, pieces[2], (offset, 2 * local_width))


def gathered_weights(tokens, ln_gain, q_weight, k_weight, v_weight, q_gain, k_gain, out_weight):
    normed = layer_norm(tokens.astype(jnp.float32), ln_gain).astype(jnp.bfloat16)
    token_count = normed.shape[0]
    local_width = q_weight.shape[1]
    feature_count = normed.shape[1]
    stacked = jnp.zeros((feature_count, 3 * local_width), jnp.bfloat16)
    projections = place_three(
        stacked,
        (
            lax.all_gather(q_weight, "dp", axis=0, tiled=True),
            lax.all_gather(k_weight, "dp", axis=0, tiled=True),
            lax.all_gather(v_weight, "dp", axis=0, tiled=True),
        ),
        jnp.int32(0),
        local_width,
    )
    combined = jnp.dot(normed, projections, preferred_element_type=jnp.float32)
    queries = combined[:, :local_width]
    key_rows = combined[:, local_width : 2 * local_width]
    value_cast = combined[:, 2 * local_width :].astype(jnp.bfloat16)
    query_normed = head_norm(queries, q_gain)
    key_normed = head_norm(key_rows, k_gain)
    images = token_count // IMG_TOKENS
    shaped = (images, IMG_TOKENS, local_width // HEAD_DIM, HEAD_DIM)
    context = attend(
        query_normed.reshape(shaped), key_normed.reshape(shaped), value_cast.reshape(shaped)
    )
    context = context.reshape(token_count, local_width)
    out_full = lax.all_gather(out_weight, "dp", axis=0, tiled=True)
    return lax.psum_scatter(
        lax.dot_general(
            context, out_full, (((1,), (1,)), ((), ())), preferred_element_type=jnp.float32
        ).astype(jnp.bfloat16),
        "mp",
        scatter_dimension=0,
        tiled=True,
    )


MESH = pl.DeviceIdType.MESH

CHUNKS = 4


def exchange_kernel(
    pairs, groups, chunks, tokens, ln_gain, q_w, k_w, v_w, q_gain, k_gain, out_w, result,
    raw, normed, weights, out_rows, end_rows, context, partial, arrived, halves, summed, final,
    local_sem, token_send, token_recv, peer_send, peer_recv,
    w_send, w_recv, own_send, own_recv, pass_send, pass_recv, out_send, out_recv,
    end_send, end_recv, c_send, c_recv, p_send, p_recv, q_send, q_recv, f_send, f_recv,
):
    dp = lax.axis_index("dp")
    group = lax.axis_index("mp")
    pair = dp // 2
    core = dp % 2
    rows = tokens.shape[0]
    part = rows // groups
    piece_rows = part // chunks
    shard = q_w.shape[0]
    width = q_w.shape[1] // pairs
    span = 2 * shard
    heads = width // HEAD_DIM
    has_up = pair + 1 < pairs
    has_down = pair > 0
    at_end = (pair == 0) | (pair == pairs - 1)
    beside_end = (pair == 1) | (pair == pairs - 2)
    inner = jnp.where(pair < pairs // 2, pair + 1, pair - 1)
    outer = jnp.where(pair < pairs // 2, pair - 1, pair + 1)

    def at_pair(other):
        return (other * 2 + core, group)

    partner = (pair * 2 + (1 - core), group)

    def at_group(other):
        return (dp, other)

    def remote(source, target, send, recv, device):
        return pltpu.make_async_remote_copy(
            src_ref=source, dst_ref=target, send_sem=send, recv_sem=recv,
            device_id=device, device_id_type=MESH,
        )

    def quarter_of(owner):
        return pl.ds(pl.multiple_of(owner * part, part), part)

    token_quarters = []
    for j in range(groups):
        place = quarter_of((group + j) % groups)
        token_quarters.append(
            pltpu.make_async_copy(tokens.at[place, :], raw.at[place, :], local_sem.at[j])
        )
        token_quarters[j].start()

    projections = (q_w, k_w, v_w)

    def columns(other, h, t):
        start = pl.multiple_of(other * width + h * HEAD_DIM, HEAD_DIM)
        return projections[t].at[:, pl.ds(start, HEAD_DIM)]

    def slot(h, block, side, t):
        return weights.at[h, block, side, :, pl.ds(t * HEAD_DIM, HEAD_DIM)]

    greeted = pltpu.get_barrier_semaphore()
    for step in range(1, pairs):
        pl.semaphore_signal(
            greeted, inc=1, device_id=at_pair((pair + step) % pairs), device_id_type=MESH
        )
    for step in range(1, groups):
        pl.semaphore_signal(
            greeted, inc=1, device_id=at_group((group + step) % groups), device_id_type=MESH
        )
    pl.semaphore_signal(greeted, inc=1, device_id=partner, device_id_type=MESH)

    locals_ = [pltpu.make_async_copy(out_w, out_rows.at[core], local_sem.at[groups])]
    for h in range(heads):
        for t in range(3):
            locals_.append(
                pltpu.make_async_copy(
                    columns(pair, h, t), slot(h, pair, core, t),
                    local_sem.at[groups + 1 + 3 * h + t],
                )
            )
    for copy in locals_:
        copy.start()

    def normalise(first_row, count):
        @pl.loop(0, count // 16)
        def _(step):
            place = pl.ds(pl.multiple_of(first_row + step * 16, 16), 16)
            values = raw[place, :].astype(jnp.float32)
            average = jnp.mean(values, axis=-1, keepdims=True)
            centred = values - average
            variance = jnp.mean(centred * centred, axis=-1, keepdims=True)
            scaled = centred * lax.rsqrt(variance + epsilon) * ln_gain[...]
            normed[pair, place, :] = scaled.astype(jnp.bfloat16)

    token_quarters[0].wait()
    normalise(group * part, part)

    def piece(block, owner, k):
        start = pl.multiple_of(owner * part + k * piece_rows, 16)
        return normed.at[block, pl.ds(start, piece_rows), :]

    def z_hop(block, k, up):
        there = piece(block, group, k)
        return remote(
            there, there, token_send.at[0 if up else 1, block], token_recv.at[block, k],
            at_pair(pair + 1 if up else pair - 1),
        )

    beside = group + 1 - 2 * (group % 2)
    across = (group + 2) % 4
    first = jnp.where(core == 0, beside, across)
    second = jnp.where(core == 0, across, beside)
    opposite = 3 - group

    def peer_copy(block, owner, place, k, other):
        there = piece(block, owner, k)
        return remote(
            there, there, peer_send.at[block, place], peer_recv.at[block, owner, k], at_group(other)
        )

    def weight_to(other, h, t):
        return remote(
            columns(other, h, t), slot(h, pair, core, t),
            w_send.at[other, h], w_recv.at[pair, h, t], at_pair(other),
        )

    def send_weights(up, plan):
        for h, distance in plan:
            other = pair + distance if up else pair - distance

            @pl.when(other < pairs if up else other >= 0)
            def _():
                for t in range(3):
                    weight_to(other, h, t).start()

    def own_weight(h, t):
        return remote(
            columns(pair, h, t), slot(h, pair, core, t), own_send, own_recv, partner
        )

    def out_over():
        return remote(out_w, out_rows.at[core], out_send, out_recv, partner)

    with jax.named_scope("greet"):
        pl.semaphore_wait(greeted, pairs + groups - 1)

    @pl.loop(0, chunks)
    def _(k):
        @pl.when(has_up)
        def _():
            z_hop(pair, k, True).start()

        @pl.when(has_down)
        def _():
            z_hop(pair, k, False).start()

    def end_over():
        return remote(out_w, end_rows.at[core], end_send.at[0], end_recv.at[0], at_pair(inner))

    def end_in(side, device, at):
        there = end_rows.at[side]
        return remote(there, there, end_send.at[at], end_recv.at[at], device)

    for at, up in ((0, True), (pairs - 1, False)):
        @pl.when(pair == at)
        def _():
            send_weights(up, [(h, 1) for h in range(heads)])
            send_weights(up, [(0, distance) for distance in range(2, pairs)])
            end_over().start()

    for h in range(heads):
        for t in range(3):
            own_weight(h, t).start()
    out_over().start()
    for j in range(1, groups):
        token_quarters[j].wait()

    def relay(block, k, up):
        with jax.named_scope("relaywait"):
            z_hop(block, k, up).wait_recv()

        @pl.when(has_up if up else has_down)
        def _():
            z_hop(block, k, up).start()

        peer_copy(block, group, 0, k, first).start()
        peer_copy(block, group, 1, k, second).start()

    others = rows - part
    for distance in range(1, pairs):
        @pl.loop(0, chunks)
        def _(k):
            @pl.when(pair - distance >= 0)
            def _():
                relay(pair - distance, k, True)

            @pl.when(pair + distance < pairs)
            def _():
                relay(pair + distance, k, False)

            if distance == 1:
                for j in range(1, groups):
                    normalise(((group + j) % groups) * part + k * piece_rows, piece_rows)

        @pl.when(has_up & (pair == distance))
        def _():
            send_weights(True, [(h, d) for h in range(heads) for d in range(1, pairs - 1)])

        @pl.when(has_down & (pair == pairs - 1 - distance))
        def _():
            send_weights(False, [(h, d) for h in range(heads) for d in range(1, pairs - 1)])

    def cross_tokens(block, k):
        with jax.named_scope("crosswait"):
            peer_copy(block, first, 0, k, first).wait_recv()
        peer_copy(block, first, 2, k, second).start()

    for distance in range(1, pairs):
        @pl.loop(0, chunks)
        def _(k):
            @pl.when(pair - distance >= 0)
            def _():
                cross_tokens(pair - distance, k)

            @pl.when(pair + distance < pairs)
            def _():
                cross_tokens(pair + distance, k)


    def pass_weights(h):
        for distance in range(1, pairs):
            for up in (True, False):
                other = pair - distance if up else pair + distance

                @pl.when(other >= 0 if up else other < pairs)
                def _():
                    for t in range(3):
                        there = slot(h, other, core, t)
                        with jax.named_scope("wwait"):
                            remote(
                                there, there, w_send.at[other, h], w_recv.at[other, h, t], partner
                            ).wait_recv()
                        remote(there, there, pass_send.at[h], pass_recv.at[h], partner).start()

    def all_passed(h):
        there = weights.at[h, pl.ds(0, pairs - 1), 1 - core]
        return remote(there, there, pass_send.at[h], pass_recv.at[h], partner)

    def all_own():
        there = weights.at[:, pair, 1 - core]
        return remote(there, there, own_send, own_recv, partner)

    pass_weights(0)
    for copy in locals_:
        copy.wait()
    all_own().wait_recv()
    for distance in range(1, pairs):
        for below in (True, False):
            block = pair - distance if below else pair + distance

            @pl.when(block >= 0 if below else block < pairs)
            def _():
                with jax.named_scope("tokwait"):
                    @pl.loop(0, chunks)
                    def _(k):
                        peer_copy(block, second, 0, k, second).wait_recv()
                        peer_copy(block, opposite, 0, k, second).wait_recv()

    def head_layer_norm(values, scale_gain):
        average = jnp.mean(values, axis=-1, keepdims=True)
        centred = values - average
        variance = jnp.mean(centred * centred, axis=-1, keepdims=True)
        return (centred * lax.rsqrt(variance + epsilon) * scale_gain).astype(jnp.bfloat16)

    def head_place(block, h):
        return pl.ds(pl.multiple_of(block * width + h * HEAD_DIM, HEAD_DIM), HEAD_DIM)

    def context_hop(block, image, h, up):
        there = context.at[image, :, head_place(block, h)]
        return remote(
            there, there,
            c_send.at[0 if up else 1, block, h], c_recv.at[block, image, h],
            at_pair(pair + 1 if up else pair - 1),
        )

    def inside(image):
        return (image > 0) & (image < pairs - 1)

    def outside(image):
        return (image == 0) | (image == pairs - 1)

    def onward(image, up):
        if up:
            return has_up & ~((pair == pairs - 2) & inside(image))
        return has_down & ~((pair == 1) & inside(image))

    def awaited(block, image, up):
        if up:
            return (block >= 0) & ~((pair == pairs - 1) & inside(image))
        return (block < pairs) & ~((pair == 0) & inside(image))

    def send_context(image, h, across_middle, to_end):
        for up in (True, False):
            crossing = pair < pairs // 2 if up else pair >= pairs // 2
            wanted = (crossing & across_middle) | (~crossing & to_end)

            @pl.when(onward(image, up) & wanted)
            def _():
                context_hop(pair, image, h, up).start()

    def cross_context(image, h):
        for up in (True, False):
            @pl.when((pair == 1) if up else (pair == pairs - 2))
            def _():
                with jax.named_scope("crossctx"):
                    context_hop(outer, image, h, up).wait_recv()
                context_hop(outer, image, h, up).start()

    def pass_context(image, h, distance):
        for up in (True, False):
            block = pair - distance if up else pair + distance

            @pl.when(awaited(block, image, up) & ~(beside_end & (block == outer)))
            def _():
                with jax.named_scope("ctxwait%d" % distance):
                    context_hop(block, image, h, up).wait_recv()

                @pl.when(onward(image, up))
                def _():
                    context_hop(block, image, h, up).start()

    def attend_head(image, h):
        lanes = slice(h * HEAD_DIM, (h + 1) * HEAD_DIM)
        with jax.named_scope("attend"):
            total = jnp.dot(
                normed[image], weights[h].reshape(pairs * span, 3 * HEAD_DIM),
                preferred_element_type=jnp.float32,
            )
            queries = head_layer_norm(total[:, :HEAD_DIM], q_gain[pair, :, lanes])
            key_rows = head_layer_norm(total[:, HEAD_DIM : 2 * HEAD_DIM], k_gain[pair, :, lanes])
            value_rows = total[:, 2 * HEAD_DIM :].astype(jnp.bfloat16)
            scores = lax.dot_general(
                queries, key_rows, (((1,), (1,)), ((), ())), preferred_element_type=jnp.float32
            ) * (1.0 / math.sqrt(HEAD_DIM))
            highest = jnp.max(scores, axis=-1, keepdims=True)
            spread = jnp.exp(scores - highest)
            probs = (spread / jnp.sum(spread, axis=-1, keepdims=True)).astype(jnp.bfloat16)
            mixed = jnp.dot(probs, value_rows, preferred_element_type=jnp.float32)
            context[image, :, head_place(pair, h)] = mixed.astype(jnp.bfloat16)

    def image_at(step):
        return step + 1 - 2 * (step % 2)

    def all_weights(h):
        with jax.named_scope("passedwait"):
            all_passed(h).wait_recv()

    all_weights(0)

    @pl.loop(0, pairs)
    def _(step):
        image = image_at(step)
        attend_head(image, 0)
        send_context(image, 0, at_end | (step < 2), True)

    for at, up in ((0, True), (pairs - 1, False)):
        @pl.when(pair == at)
        def _():
            send_weights(up, [(h, d) for h in range(1, heads) for d in range(pairs - 1, 1, -1)])

    with jax.named_scope("sends"):
        for distance in range(pairs):
            for up in (True, False):
                if distance == 0 and not up:
                    continue
                block = pair - distance if up else pair + distance

                @pl.when(block >= 0 if up else block < pairs)
                def _():
                    quarter = normed.at[block, quarter_of(group), :]
                    for way, there in ((0, has_up), (1, has_down)):
                        if distance > 0 and way != (0 if up else 1):
                            continue

                        @pl.when(there)
                        def _():
                            remote(
                                quarter, quarter, token_send.at[way, block],
                                token_recv.at[block, 0], partner,
                            ).wait_send()

                    if distance > 0:
                        for place in range(3):
                            remote(
                                quarter, quarter, peer_send.at[block, place],
                                peer_recv.at[block, 0, 0], partner,
                            ).wait_send()
        all_own().wait_send()
        out_back = remote(out_rows.at[1 - core], out_rows.at[1 - core], out_send, out_recv, partner)
        out_back.wait_recv()
        out_back.wait_send()


    @pl.when(beside_end)
    def _():
        end_in(core, partner, 0).wait_recv()
        end_in(core, partner, 1).start()

    def partial_to(unit, c, at, owner):
        return remote(
            partial.at[unit, c, quarter_of(owner), :], arrived.at[unit, c, at],
            p_send.at[unit], p_recv.at[unit, c], at_group(first),
        )

    def partials(unit, c):
        there = arrived.at[unit, c, pl.ds(0, 2)]
        return remote(there, there, p_send.at[unit], p_recv.at[unit, c], partner)

    def half_to(unit, c):
        return remote(
            halves.at[unit, c], arrived.at[unit, c, 2], q_send.at[unit], q_recv.at[unit, c],
            at_group(second),
        )

    def half_in(unit, c):
        there = arrived.at[unit, c, 2]
        return remote(there, there, q_send.at[unit], q_recv.at[unit, c], partner)

    def final_to(unit, c, image, span_of):
        return remote(summed.at[unit, c], final.at[span_of, c], f_send, f_recv, at_pair(image))

    def finals(count):
        there = final.at[pl.ds(0, count)]
        return remote(there, there, f_send, f_recv, partner)

    def project(unit, image, rows_of):
        for c in range(2):
            with jax.named_scope("outproj"):
                product = lax.dot_general(
                    context[image], rows_of[c], (((1,), (1,)), ((), ())),
                    preferred_element_type=jnp.float32,
                )
                partial[unit, c] = product.astype(jnp.bfloat16)
            partial_to(unit, c, 0, first).start()
            partial_to(unit, c, 1, opposite).start()

    def add_halves(unit, c):
        with jax.named_scope("partwait"):
            partials(unit, c).wait_recv()
        total = partial[unit, c, quarter_of(second), :].astype(jnp.float32)
        total = total + arrived[unit, c, 1].astype(jnp.float32)
        halves[unit, c] = total.astype(jnp.bfloat16)
        half_to(unit, c).start()

    def add_up(unit, c, image, span_of):
        with jax.named_scope("halfwait"):
            half_in(unit, c).wait_recv()
        total = partial[unit, c, quarter_of(group), :].astype(jnp.float32)
        for at in (0, 2):
            total = total + arrived[unit, c, at].astype(jnp.float32)
        total = total.astype(jnp.bfloat16)

        @pl.when(image != pair)
        def _():
            summed[unit, c] = total
            final_to(unit, c, image, span_of).start()

        @pl.when(image == pair)
        def _():
            final[span_of, c] = total

    def for_units(image, act):
        @pl.when(~at_end | outside(image))
        def _():
            act(image, pair)

        @pl.when(beside_end & inside(image))
        def _():
            act(pairs + image - 1, outer)

    def halve(image):
        def act(unit, span_of):
            for c in range(2):
                add_halves(unit, c)
        for_units(image, act)

    def finish(image):
        def act(unit, span_of):
            for c in range(2):
                add_up(unit, c, image, span_of)
        for_units(image, act)


    for step in range(2):
        cross_context(image_at(step), 0)
    pass_weights(heads - 1)
    all_weights(heads - 1)

    lag = 2

    @pl.loop(0, pairs + lag)
    def _(step):
        @pl.when(step < pairs)
        def _():
            image = image_at(step)
            attend_head(image, heads - 1)
            send_context(image, heads - 1, True, True)
            cross_context(image, heads - 1)

            @pl.when(step + 2 < pairs)
            def _():
                after = image_at(step + 2)

                @pl.when(~at_end)
                def _():
                    send_context(after, 0, True, False)
                cross_context(after, 0)

        @pl.when(step >= lag)
        def _():
            image = image_at(step - lag)
            for distance in range(1, pairs):
                for h in range(heads):
                    pass_context(image, h, distance)

            @pl.when(~at_end | outside(image))
            def _():
                project(image, image, out_rows)

            @pl.when(beside_end & inside(image))
            def _():
                @pl.when(image == image_at(0))
                def _():
                    end_in(1 - core, partner, 1).wait_recv()

                project(pairs + image - 1, image, end_rows)

        @pl.when(step > lag)
        def _():
            halve(image_at(step - lag - 1))

        @pl.when(step > lag + 1)
        def _():
            finish(image_at(step - lag - 2))

    def wait_partials(image):
        def act(unit, span_of):
            there = partial.at[unit, :, pl.ds(0, 2 * part), :]
            remote(there, there, p_send.at[unit], p_recv.at[unit, 0], partner).wait_send()
            there = halves.at[unit]
            remote(there, there, q_send.at[unit], q_recv.at[unit, 0], partner).wait_send()
        for_units(image, act)

    with jax.named_scope("sends2"):
        for h in range(heads):
            own = weights.at[h, pl.ds(0, pairs - 1), core]
            remote(own, own, pass_send.at[h], pass_recv.at[h], partner).wait_send()
        for distance in range(1, pairs):
            for below in (True, False):
                other = pair - distance if below else pair + distance

                @pl.when(other >= 0 if below else other < pairs)
                def _():
                    for h in range(heads):
                        there = weights.at[h, pair, core]
                        remote(
                            there, there, w_send.at[other, h], w_recv.at[other, h, 0], partner
                        ).wait_send()

        @pl.when(at_end)
        def _():
            end_over().wait_send()

        @pl.when(beside_end)
        def _():
            end_in(core, partner, 1).wait_send()

        for distance in range(pairs):
            for up in (True, False):
                block = pair - distance if up else pair + distance
                thin = (pair == pairs - 2) if up else (pair == 1)

                @pl.when((block >= 0 if up else block < pairs) & (has_up if up else has_down))
                def _():
                    for h in range(heads):
                        def sent(count):
                            there = context.at[pl.ds(0, count), :, head_place(block, h)]
                            return remote(
                                there, there, c_send.at[0 if up else 1, block, h],
                                c_recv.at[block, 0, h], partner,
                            )

                        @pl.when(thin)
                        def _():
                            sent(2).wait_send()

                        @pl.when(~thin)
                        def _():
                            sent(pairs).wait_send()

        @pl.loop(0, pairs - 2)
        def _(step):
            wait_partials(image_at(step))

    finish(image_at(pairs - 2))
    last = image_at(pairs - 1)

    @pl.when(beside_end)
    def _():
        ends = [(last, pair, c) for c in range(2)] + [(pairs + last - 1, outer, c) for c in range(2)]
        for k in range(len(ends) + 1):
            if k < len(ends):
                add_halves(ends[k][0], ends[k][2])
            if k > 0:
                add_up(ends[k - 1][0], ends[k - 1][2], last, ends[k - 1][1])

    wait_partials(image_at(pairs - 2))
    wait_partials(last)

    with jax.named_scope("finalwait"):
        @pl.when(at_end)
        def _():
            finals(pairs - 1).wait_recv()

        @pl.when(~at_end)
        def _():
            finals(pairs - 2).wait_recv()
    for p in range(pairs):
        for c in range(2):
            start = (2 * p + c) * shard
            result[:, start : start + shard] = final[p, c]
    with jax.named_scope("sends4"):
        @pl.when(at_end)
        def _():
            finals(1).wait_send()

        @pl.when(~at_end)
        def _():
            finals(pairs).wait_send()


def exchanged_heads(pairs, groups, tokens, ln_gain, q_w, k_w, v_w, q_gain, k_gain, out_w):
    rows, features = tokens.shape
    shard, local_width = q_w.shape
    width = local_width // pairs
    heads = width // HEAD_DIM
    part = rows // groups
    chunks = min(CHUNKS, part // 16)
    units = 2 * pairs - 2
    dma = pltpu.SemaphoreType.DMA
    in_hbm = pl.BlockSpec(memory_space=pl.ANY)
    in_vmem = pl.BlockSpec(memory_space=pltpu.VMEM)
    bf16 = jnp.bfloat16
    return pl.pallas_call(
        functools.partial(exchange_kernel, pairs, groups, chunks),
        out_shape=jax.ShapeDtypeStruct((part, features), bf16),
        in_specs=[in_hbm, in_vmem, in_hbm, in_hbm, in_hbm, in_vmem, in_vmem, in_hbm],
        out_specs=in_vmem,
        scratch_shapes=[
            pltpu.VMEM((rows, features), bf16),
            pltpu.VMEM((pairs, rows, features), bf16),
            pltpu.VMEM((heads, pairs, 2, shard, 3 * HEAD_DIM), bf16),
            pltpu.VMEM((2, shard, local_width), bf16),
            pltpu.VMEM((2, shard, local_width), bf16),
            pltpu.VMEM((pairs, rows, local_width), bf16),
            pltpu.VMEM((units, 2, rows, shard), bf16),
            pltpu.VMEM((units, 2, 3, part, shard), bf16),
            pltpu.VMEM((units, 2, part, shard), bf16),
            pltpu.VMEM((units, 2, part, shard), bf16),
            pltpu.VMEM((pairs, 2, part, shard), bf16),
            dma((groups + 1 + 3 * heads,)), dma((2, pairs)), dma((pairs, chunks)),
            dma((pairs, 3)), dma((pairs, groups, chunks)),
            dma((pairs, heads)), dma((pairs, heads, 3)), dma, dma,
            dma((heads,)), dma((heads,)), dma, dma,
            dma((2,)), dma((2,)), dma((2, pairs, heads)), dma((pairs, pairs, heads)),
            dma((units,)), dma((units, 2)), dma((units,)), dma((units, 2)), dma, dma,
        ],
        compiler_params=pltpu.CompilerParams(
            collective_id=0, has_side_effects=True, vmem_limit_bytes=60 * 1024 * 1024
        ),
    )(
        tokens, ln_gain.reshape(1, features), q_w, k_w, v_w,
        q_gain.reshape(pairs, 1, width), k_gain.reshape(pairs, 1, width), out_w,
    )


def on_device(tokens, ln_gain, q_w, k_w, v_w, q_gain, k_gain, out_w):
    devices = lax.axis_size("dp")
    groups = lax.axis_size("mp")
    pairs = devices // 2
    fits = (
        devices % 2 == 0
        and groups == 4
        and q_w.shape[1] % (pairs * HEAD_DIM) == 0
        and q_w.shape[0] % 128 == 0
        and tokens.shape[0] == IMG_TOKENS
        and tokens.shape[0] % (16 * groups) == 0
        and pairs == 4
        and q_w.shape[1] == 2 * pairs * HEAD_DIM
    )
    if fits:
        return exchanged_heads(pairs, groups, tokens, ln_gain, q_w, k_w, v_w, q_gain, k_gain, out_w)
    return gathered_weights(tokens, ln_gain, q_w, k_w, v_w, q_gain, k_gain, out_w)


def solution(mesh):
    in_specs = (
        P("dp", None),
        P(),
        P("dp", "mp"),
        P("dp", "mp"),
        P("dp", "mp"),
        P("mp"),
        P("mp"),
        P("dp", "mp"),
    )
    out_specs = P(("dp", "mp"), None)
    return jax.shard_map(
        on_device, mesh=mesh, in_specs=in_specs, out_specs=out_specs, check_vma=False
    )
```

```python
import functools
import math

import jax
import jax.numpy as jnp
from jax import lax
from jax.experimental import pallas as pl
from jax.experimental.pallas import tpu as pltpu
from jax.sharding import PartitionSpec as P

HEAD_DIM = 128
IMG_TOKENS = 256


epsilon = 1e-06


def layer_norm(values, scale_gain):
    average = jnp.mean(values, axis=-1, keepdims=True)
    centred = values - average
    variance = jnp.mean(centred * centred, axis=-1, keepdims=True)
    return centred * lax.rsqrt(variance + epsilon) * scale_gain


def head_norm(projected, scale_gain):
    heads_count = projected.shape[1] // HEAD_DIM
    shaped = projected.reshape(projected.shape[0], heads_count, HEAD_DIM)
    normed = layer_norm(shaped, scale_gain.reshape(heads_count, HEAD_DIM))
    return normed.reshape(projected.shape).astype(jnp.bfloat16)


def attend(queries, key_rows, value_rows):
    scores = jnp.einsum(
        "bqhd,bkhd->bhqk", queries, key_rows, preferred_element_type=jnp.float32
    ) * (1.0 / math.sqrt(HEAD_DIM))
    highest = jnp.max(scores, axis=-1, keepdims=True)
    weights = jnp.exp(scores - highest)
    probs = (weights / jnp.sum(weights, axis=-1, keepdims=True)).astype(jnp.bfloat16)
    context = jnp.einsum("bhqk,bkhd->bqhd", probs, value_rows, preferred_element_type=jnp.float32)
    return context.astype(jnp.bfloat16)


def place_three(holder, pieces, offset, local_width):
    holder = lax.dynamic_update_slice(holder, pieces[0], (offset, 0))
    holder = lax.dynamic_update_slice(holder, pieces[1], (offset, local_width))
    return lax.dynamic_update_slice(holder, pieces[2], (offset, 2 * local_width))


def gathered_weights(tokens, ln_gain, q_weight, k_weight, v_weight, q_gain, k_gain, out_weight):
    normed = layer_norm(tokens.astype(jnp.float32), ln_gain).astype(jnp.bfloat16)
    token_count = normed.shape[0]
    local_width = q_weight.shape[1]
    feature_count = normed.shape[1]
    stacked = jnp.zeros((feature_count, 3 * local_width), jnp.bfloat16)
    projections = place_three(
        stacked,
        (
            lax.all_gather(q_weight, "dp", axis=0, tiled=True),
            lax.all_gather(k_weight, "dp", axis=0, tiled=True),
            lax.all_gather(v_weight, "dp", axis=0, tiled=True),
        ),
        jnp.int32(0),
        local_width,
    )
    combined = jnp.dot(normed, projections, preferred_element_type=jnp.float32)
    queries = combined[:, :local_width]
    key_rows = combined[:, local_width : 2 * local_width]
    value_cast = combined[:, 2 * local_width :].astype(jnp.bfloat16)
    query_normed = head_norm(queries, q_gain)
    key_normed = head_norm(key_rows, k_gain)
    images = token_count // IMG_TOKENS
    shaped = (images, IMG_TOKENS, local_width // HEAD_DIM, HEAD_DIM)
    context = attend(
        query_normed.reshape(shaped), key_normed.reshape(shaped), value_cast.reshape(shaped)
    )
    context = context.reshape(token_count, local_width)
    out_full = lax.all_gather(out_weight, "dp", axis=0, tiled=True)
    return lax.psum_scatter(
        lax.dot_general(
            context, out_full, (((1,), (1,)), ((), ())), preferred_element_type=jnp.float32
        ).astype(jnp.bfloat16),
        "mp",
        scatter_dimension=0,
        tiled=True,
    )


MESH = pl.DeviceIdType.MESH

CHUNKS = 4


def exchange_kernel(
    pairs, groups, chunks, tokens, ln_gain, q_w, k_w, v_w, q_gain, k_gain, out_w, result,
    raw, normed, weights, out_rows, end_rows, staged, context, kept, partial, arrived, summed, final,
    local_sem, token_send, token_recv, peer_send, peer_recv,
    w_send, w_recv, own_send, own_recv, pass_send, pass_recv, out_send, out_recv, side_send, side_recv,
    end_send, end_recv, x_send, x_recv, c_send, c_recv, p_send, p_recv, f_send, f_recv,
):
    dp = lax.axis_index("dp")
    group = lax.axis_index("mp")
    pair = dp // 2
    core = dp % 2
    rows = tokens.shape[0]
    part = rows // groups
    piece_rows = part // chunks
    shard = q_w.shape[0]
    width = q_w.shape[1] // pairs
    span = 2 * shard
    heads = width // HEAD_DIM
    has_up = pair + 1 < pairs
    has_down = pair > 0
    at_end = (pair == 0) | (pair == pairs - 1)
    beside_end = (pair == 1) | (pair == pairs - 2)
    inner = jnp.where(pair < pairs // 2, pair + 1, pair - 1)
    outer = jnp.where(pair < pairs // 2, pair - 1, pair + 1)

    def at_pair(other):
        return (other * 2 + core, group)

    partner = (pair * 2 + (1 - core), group)

    def at_group(other):
        return (dp, other)

    def remote(source, target, send, recv, device):
        return pltpu.make_async_remote_copy(
            src_ref=source, dst_ref=target, send_sem=send, recv_sem=recv,
            device_id=device, device_id_type=MESH,
        )

    def quarter_of(owner):
        return pl.ds(pl.multiple_of(owner * part, part), part)

    token_quarters = []
    for j in range(groups):
        place = quarter_of((group + j) % groups)
        token_quarters.append(
            pltpu.make_async_copy(tokens.at[place, :], raw.at[place, :], local_sem.at[j])
        )
        token_quarters[j].start()

    projections = (q_w, k_w, v_w)

    def columns(other, h, t):
        start = pl.multiple_of(other * width + h * HEAD_DIM, HEAD_DIM)
        return projections[t].at[:, pl.ds(start, HEAD_DIM)]

    def slot(h, block, side, t):
        return weights.at[h, block, side, :, pl.ds(t * HEAD_DIM, HEAD_DIM)]

    greeted = pltpu.get_barrier_semaphore()
    for step in range(1, pairs):
        pl.semaphore_signal(
            greeted, inc=1, device_id=at_pair((pair + step) % pairs), device_id_type=MESH
        )
    for step in range(1, groups):
        pl.semaphore_signal(
            greeted, inc=1, device_id=at_group((group + step) % groups), device_id_type=MESH
        )
    pl.semaphore_signal(greeted, inc=1, device_id=partner, device_id_type=MESH)
    beside = group + 1 - 2 * (group % 2)
    across = (group + 2) % 4
    pl.semaphore_signal(
        greeted, inc=1,
        device_id=(pair * 2 + 1 - core, jnp.where(core == 0, beside, across)), device_id_type=MESH,
    )

    locals_ = [pltpu.make_async_copy(out_w, out_rows.at[0, core], local_sem.at[groups])]
    for h in range(heads):
        for t in range(3):
            locals_.append(
                pltpu.make_async_copy(
                    columns(pair, h, t), slot(h, pair, core, t), local_sem.at[groups + 1],
                )
            )
    for copy in locals_:
        copy.start()

    def normalise(first_row, count):
        @pl.loop(0, count // 16)
        def _(step):
            place = pl.ds(pl.multiple_of(first_row + step * 16, 16), 16)
            values = raw[place, :].astype(jnp.float32)
            average = jnp.mean(values, axis=-1, keepdims=True)
            centred = values - average
            variance = jnp.mean(centred * centred, axis=-1, keepdims=True)
            scaled = centred * lax.rsqrt(variance + epsilon) * ln_gain[...]
            normed[pair, place, :] = scaled.astype(jnp.bfloat16)

    token_quarters[0].wait()
    normalise(group * part, part)

    def piece(block, owner, k):
        start = pl.multiple_of(owner * part + k * piece_rows, 16)
        return normed.at[block, pl.ds(start, piece_rows), :]

    def z_hop(block, k, up):
        there = piece(block, group, k)
        return remote(
            there, there, token_send.at[0 if up else 1], token_recv.at[block, k],
            at_pair(pair + 1 if up else pair - 1),
        )

    first = jnp.where(core == 0, beside, across)
    second = jnp.where(core == 0, across, beside)
    opposite = 3 - group

    def peer_copy(block, owner, place, k, other):
        there = piece(block, owner, k)
        return remote(
            there, there, peer_send, peer_recv.at[block, place, k if place == 0 else 0], at_group(other)
        )

    def weight_to(other, h, t):
        return remote(
            columns(other, h, t), slot(h, pair, core, t),
            w_send, w_recv.at[pair, h, t], at_pair(other),
        )

    def send_weights(up, plan):
        for h, distance in plan:
            other = pair + distance if up else pair - distance

            @pl.when(other < pairs if up else other >= 0)
            def _():
                for t in range(3):
                    weight_to(other, h, t).start()

    def own_weight(h, t):
        return remote(
            columns(pair, h, t), slot(h, pair, core, t), own_send, own_recv, partner
        )

    def out_over():
        return remote(out_w, out_rows.at[0, core], out_send, out_recv, partner)

    sides = ((pair * 2, beside), (pair * 2 + 1, across))

    def rows_aside(to):
        return remote(out_w, out_rows.at[1, core], side_send, side_recv.at[core], sides[to])

    with jax.named_scope("greet"):
        pl.semaphore_wait(greeted, pairs + groups)

    @pl.loop(0, chunks)
    def _(k):
        @pl.when(has_up)
        def _():
            z_hop(pair, k, True).start()

        @pl.when(has_down)
        def _():
            z_hop(pair, k, False).start()

    def end_over():
        return remote(out_w, end_rows.at[0, core], end_send.at[0], end_recv.at[0], at_pair(inner))

    def end_in(side, way, at, recv, device):
        return remote(
            end_rows.at[0, side], end_rows.at[way, side], end_send.at[at], end_recv.at[recv], device
        )

    for at, up in ((0, True), (pairs - 1, False)):
        @pl.when(pair == at)
        def _():
            send_weights(up, [(h, 1) for h in range(heads)])
            send_weights(up, [(0, distance) for distance in range(2, pairs)])
            end_over().start()
            send_weights(up, [(h, d) for h in range(1, heads) for d in range(pairs - 1, 1, -1)])

    for h in range(heads):
        for t in range(3):
            own_weight(h, t).start()
    out_over().start()
    for j in range(1, groups):
        token_quarters[j].wait()

    def relay(block, k, up):
        with jax.named_scope("relaywait"):
            z_hop(block, k, up).wait_recv()

        @pl.when(has_up if up else has_down)
        def _():
            z_hop(block, k, up).start()

        peer_copy(block, group, 0, k, first).start()
        peer_copy(block, group, 1, k, second).start()

    others = rows - part
    for distance in range(1, pairs):
        @pl.loop(0, chunks)
        def _(k):
            @pl.when(pair - distance >= 0)
            def _():
                relay(pair - distance, k, True)

            @pl.when(pair + distance < pairs)
            def _():
                relay(pair + distance, k, False)

            if distance == 1:
                for j in range(1, groups):
                    normalise(((group + j) % groups) * part + k * piece_rows, piece_rows)

        @pl.when(has_up & (pair == distance))
        def _():
            send_weights(True, [(h, d) for h in range(heads) for d in range(1, pairs - 1)])

        @pl.when(has_down & (pair == pairs - 1 - distance))
        def _():
            send_weights(False, [(h, d) for h in range(heads) for d in range(1, pairs - 1)])

    def cross_tokens(block, k):
        with jax.named_scope("crosswait"):
            peer_copy(block, first, 0, k, first).wait_recv()
        peer_copy(block, first, 2, k, second).start()

    for distance in range(1, pairs):
        @pl.loop(0, chunks)
        def _(k):
            @pl.when(pair - distance >= 0)
            def _():
                cross_tokens(pair - distance, k)

            @pl.when(pair + distance < pairs)
            def _():
                cross_tokens(pair + distance, k)


    def pass_weights(h):
        for distance in range(1, pairs):
            for up in (True, False):
                other = pair - distance if up else pair + distance

                @pl.when(other >= 0 if up else other < pairs)
                def _():
                    for t in range(3):
                        there = slot(h, other, core, t)
                        with jax.named_scope("wwait"):
                            remote(
                                there, there, w_send, w_recv.at[other, h, t], partner
                            ).wait_recv()
                        remote(there, there, pass_send, pass_recv.at[h], partner).start()

    def all_passed(h):
        there = weights.at[h, pl.ds(0, pairs - 1), 1 - core]
        return remote(there, there, pass_send, pass_recv.at[h], partner)

    def all_own():
        there = weights.at[:, pair, 1 - core]
        return remote(there, there, own_send, own_recv, partner)

    pass_weights(0)
    locals_[0].wait()
    there = weights.at[:, pair, core]
    pltpu.make_async_copy(there, there, local_sem.at[groups + 1]).wait()
    all_own().wait_recv()
    for distance in range(1, pairs):
        for below in (True, False):
            block = pair - distance if below else pair + distance

            @pl.when(block >= 0 if below else block < pairs)
            def _():
                with jax.named_scope("tokwait"):
                    for place, owner in ((1, second), (2, opposite)):
                        there = normed.at[block, quarter_of(owner), :]
                        remote(
                            there, there, peer_send, peer_recv.at[block, place, 0], partner
                        ).wait_recv()

    for to in range(2):
        rows_aside(to).start()

    def head_layer_norm(values, scale_gain):
        average = jnp.mean(values, axis=-1, keepdims=True)
        centred = values - average
        variance = jnp.mean(centred * centred, axis=-1, keepdims=True)
        return (centred * lax.rsqrt(variance + epsilon) * scale_gain).astype(jnp.bfloat16)

    def head_place(block, h):
        return pl.ds(pl.multiple_of(block * width + h * HEAD_DIM, HEAD_DIM), HEAD_DIM)

    def context_hop(block, image, h, up):
        there = context.at[image, :, :, :, head_place(block, h)]
        return remote(
            there, there,
            c_send.at[0 if up else 1], c_recv.at[block, image, h],
            at_pair(pair + 1 if up else pair - 1),
        )

    def inside(image):
        return (image > 0) & (image < pairs - 1)

    def outside(image):
        return (image == 0) | (image == pairs - 1)

    def onward(image, up):
        if up:
            return has_up & ~((pair == pairs - 2) & inside(image))
        return has_down & ~((pair == 1) & inside(image))

    def awaited(block, image, up):
        if up:
            return (block >= 0) & ~((pair == pairs - 1) & inside(image))
        return (block < pairs) & ~((pair == 0) & inside(image))

    def send_context(image, h, across_middle, to_end):
        for up in (True, False):
            crossing = pair < pairs // 2 if up else pair >= pairs // 2
            wanted = (crossing & across_middle) | (~crossing & to_end)

            @pl.when(onward(image, up) & wanted)
            def _():
                context_hop(pair, image, h, up).start()

    def cross_context(image, h):
        for up in (True, False):
            @pl.when((pair == 1) if up else (pair == pairs - 2))
            def _():
                with jax.named_scope("crossctx"):
                    context_hop(outer, image, h, up).wait_recv()
                context_hop(outer, image, h, up).start()

    def pass_context(image, h, distance):
        for up in (True, False):
            block = pair - distance if up else pair + distance

            @pl.when(awaited(block, image, up) & ~(beside_end & (block == outer)))
            def _():
                with jax.named_scope("ctxwait%d" % distance):
                    context_hop(block, image, h, up).wait_recv()

                @pl.when(onward(image, up))
                def _():
                    context_hop(block, image, h, up).start()

    def half_over(image, h, at, owner):
        return remote(
            staged.at[image, h, quarter_of(owner), :],
            context.at[image, 1, at, :, head_place(pair, h)],
            x_send, x_recv.at[image, h], at_group(first),
        )

    def half_in(image, h):
        there = context.at[image, 1, :, :, head_place(pair, h)]
        with jax.named_scope("halfin"):
            remote(there, there, x_send, x_recv.at[image, h], partner).wait_recv()

    def attend_head(image, h):
        lanes = slice(h * HEAD_DIM, (h + 1) * HEAD_DIM)
        with jax.named_scope("attend"):
            total = jnp.dot(
                normed[image], weights[h].reshape(pairs * span, 3 * HEAD_DIM),
                preferred_element_type=jnp.float32,
            )
            queries = head_layer_norm(total[:, :HEAD_DIM], q_gain[pair, :, lanes])
            key_rows = head_layer_norm(total[:, HEAD_DIM : 2 * HEAD_DIM], k_gain[pair, :, lanes])
            value_rows = total[:, 2 * HEAD_DIM :].astype(jnp.bfloat16)
            scores = lax.dot_general(
                queries, key_rows, (((1,), (1,)), ((), ())), preferred_element_type=jnp.float32
            ) * (1.0 / math.sqrt(HEAD_DIM))
            highest = jnp.max(scores, axis=-1, keepdims=True)
            spread = jnp.exp(scores - highest)
            probs = (spread / jnp.sum(spread, axis=-1, keepdims=True)).astype(jnp.bfloat16)
            mixed = jnp.dot(probs, value_rows, preferred_element_type=jnp.float32)
            staged[image, h] = mixed.astype(jnp.bfloat16)

        for at, owner in enumerate((first, opposite)):
            half_over(image, h, at, owner).start()
        for at, owner in enumerate((group, second)):
            context[image, 0, at, :, head_place(pair, h)] = staged[image, h, quarter_of(owner), :]

    def image_at(step):
        return step ^ (step // 2)

    def all_weights(h):
        with jax.named_scope("passedwait"):
            all_passed(h).wait_recv()

    all_weights(0)

    @pl.loop(0, pairs)
    def _(step):
        attend_head(image_at(step), 0)

    with jax.named_scope("sends"):
        for at in range(pairs):
            @pl.when(pair == at)
            def _():
                for way, blocks in ((0, at + 1 if at + 1 < pairs else 0), (1, pairs - at if at > 0 else 0)):
                    if blocks > 0:
                        there = normed.at[pl.ds(0, blocks), pl.ds(0, part), :]
                        remote(
                            there, there, token_send.at[way], token_recv.at[0, 0], partner
                        ).wait_send()
        there = normed.at[pl.ds(0, pairs - 1), pl.ds(0, 3 * part), :]
        remote(there, there, peer_send, peer_recv.at[0, 0, 0], partner).wait_send()
        all_own().wait_send()
        out_back = remote(out_rows.at[0, 1 - core], out_rows.at[0, 1 - core], out_send, out_recv, partner)
        out_back.wait_recv()
        out_back.wait_send()


    def end_part(side, k, way, recv, device):
        place = pl.ds(k * (shard // 2), shard // 2)
        return remote(
            end_rows.at[0, side, place, :], end_rows.at[way, side, place, :],
            end_send.at[2], end_recv.at[recv], device,
        )

    def end_aside(k):
        for to in range(2):
            end_part(core, k, 1, 2 + 2 * core + k, sides[to]).start()

    @pl.when(beside_end)
    def _():
        end_in(core, 0, 0, 0, partner).wait_recv()
        end_in(core, 0, 1, 1, partner).start()
        end_aside(0)

    def partial_to(unit, c):
        return remote(
            partial.at[unit, c], arrived.at[unit, c], p_send, p_recv.at[unit, c], at_group(second)
        )

    def final_to(unit, c, image, span_of):
        return remote(summed.at[unit, c], final.at[span_of, c], f_send, f_recv, at_pair(image))

    def finals(count):
        there = final.at[pl.ds(0, count)]
        return remote(there, there, f_send, f_recv, partner)

    def project(unit, image, rows_of):
        with jax.named_scope("outproj"):
            total = None
            for j in range(2):
                product = lax.dot_general(
                    context[image, j].reshape(2 * part, pairs * width), rows_of[j].reshape(span, pairs * width),
                    (((1,), (1,)), ((), ())), preferred_element_type=jnp.float32,
                )
                total = product if total is None else total + product
            for c in range(2):
                kept[unit, c] = total[:part, c * shard : (c + 1) * shard]
                partial[unit, c] = total[part:, c * shard : (c + 1) * shard].astype(jnp.bfloat16)
        for c in range(2):
            partial_to(unit, c).start()

    def add_up(unit, c, image, span_of):
        with jax.named_scope("partwait"):
            partial_to(unit, c).wait_recv()
        total = (kept[unit, c] + arrived[unit, c].astype(jnp.float32)).astype(jnp.bfloat16)

        @pl.when(image != pair)
        def _():
            summed[unit, c] = total
            final_to(unit, c, image, span_of).start()

        @pl.when(image == pair)
        def _():
            final[span_of, c] = total

    def own_unit(image):
        return ~at_end | outside(image)

    def extra_unit(image):
        return beside_end & inside(image)

    def finish(image, extra):
        @pl.when(extra_unit(image) if extra else own_unit(image))
        def _():
            for c in range(2):
                add_up(pairs + image - 1 if extra else image, c, image, outer if extra else pair)

    for to in range(2):
        remote(out_w, out_rows.at[1, to], side_send, side_recv.at[to], partner).wait_recv()
    for step in range(pairs):
        half_in(image_at(step), 0)
        send_context(image_at(step), 0, at_end | (step < 3), True)
    pass_weights(heads - 1)
    all_weights(heads - 1)

    def pass_most(image):
        for h in range(heads):
            pass_context(image, h, 1)
        pass_context(image, 0, 2)

    def pass_rest(image):
        pass_context(image, 1, 2)
        for h in range(heads):
            pass_context(image, h, 3)

    lag = 4

    @pl.loop(0, pairs + lag)
    def _(step):
        @pl.when(step < pairs)
        def _():
            attend_head(image_at(step), heads - 1)

        @pl.when((step > 0) & (step <= pairs))
        def _():
            image = image_at(step - 1)
            half_in(image, heads - 1)
            send_context(image, heads - 1, at_end | (step < 3), True)

            @pl.when(step < pairs)
            def _():
                cross_context(image, 0)

            @pl.when((step == 1) & ~at_end)
            def _():
                send_context(image_at(pairs - 1), 0, True, False)

            @pl.when((step == pairs) & beside_end)
            def _():
                end_aside(1)

        @pl.when(step >= lag)
        def _():
            image = image_at(step - lag)

            @pl.when(step == lag)
            def _():
                cross_context(image_at(0), heads - 1)

            @pl.when(step < lag + 2)
            def _():
                pass_most(image)

            @pl.when(step < pairs + lag - 1)
            def _():
                cross_context(image_at(step - lag + 1), heads - 1)

            @pl.when((step < lag + 2) & ~at_end)
            def _():
                send_context(image_at(step - lag + 2), heads - 1, True, False)

            @pl.when(step == lag + 1)
            def _():
                cross_context(image_at(pairs - 1), 0)
            pass_rest(image)

            @pl.when((step > lag) & (step < pairs + lag - 1))
            def _():
                pass_most(image_at(step - lag + 1))

            @pl.when(own_unit(image))
            def _():
                project(image, image, out_rows)

            @pl.when(extra_unit(image))
            def _():
                @pl.when(step == lag + 1)
                def _():
                    end_in(1 - core, 0, 1, 1, partner).wait_recv()
                    with jax.named_scope("endrows"):
                        for side in range(2):
                            for k in range(2):
                                end_part(side, k, 1, 2 + 2 * side + k, partner).wait_recv()

                project(pairs + image - 1, image, end_rows)

        @pl.when(step == lag + 2)
        def _():
            for early in range(2):
                for extra in (False, True):
                    finish(image_at(early), extra)

    for step in range(2, pairs):
        for extra in (False, True):
            finish(image_at(step), extra)

    with jax.named_scope("sends2"):
        others = weights.at[:, pl.ds(0, pairs - 1), core]
        remote(others, others, pass_send, pass_recv.at[0], partner).wait_send()
        remote(others, others, w_send, w_recv.at[0, 0, 0], partner).wait_send()

        @pl.when(at_end)
        def _():
            end_over().wait_send()

        @pl.when(beside_end)
        def _():
            end_in(core, 0, 1, 1, partner).wait_send()
            both = end_rows.at[0]
            remote(both, both, end_send.at[2], end_recv.at[2], partner).wait_send()

        def sent(way, images, blocks):
            there = context.at[pl.ds(0, images), :, :, :, pl.ds(0, blocks * width)]
            return remote(there, there, c_send.at[way], c_recv.at[0, 0, 0], partner)

        for at, counts in (
            (0, ((0, pairs, 1),)),
            (1, ((0, pairs, 2), (1, 2, pairs - 1))),
            (pairs - 2, ((0, 2, pairs - 1), (1, pairs, 2))),
            (pairs - 1, ((1, pairs, 1),)),
        ):
            @pl.when(pair == at)
            def _():
                for way, images, blocks in counts:
                    sent(way, images, blocks).wait_send()

    with jax.named_scope("sends3"):
        both = out_rows.at[0]
        remote(both, both, side_send, side_recv.at[0], partner).wait_send()
        half = staged.at[:, :, pl.ds(0, 2 * part), :]
        remote(half, half, x_send, x_recv.at[0, 0], partner).wait_send()
        for few, units in ((at_end, 2), (beside_end, 2 * pairs - 2)):
            @pl.when(few)
            def _():
                whole = partial.at[pl.ds(0, units)]
                remote(whole, whole, p_send, p_recv.at[0, 0], partner).wait_send()

    with jax.named_scope("finalwait"):
        @pl.when(at_end)
        def _():
            finals(pairs - 1).wait_recv()

        @pl.when(~at_end)
        def _():
            finals(pairs - 2).wait_recv()
    for p in range(pairs):
        for c in range(2):
            start = (2 * p + c) * shard
            result[:, start : start + shard] = final[p, c]
    with jax.named_scope("sends4"):
        @pl.when(at_end)
        def _():
            finals(1).wait_send()

        @pl.when(~at_end)
        def _():
            finals(pairs).wait_send()


def exchanged_heads(pairs, groups, tokens, ln_gain, q_w, k_w, v_w, q_gain, k_gain, out_w):
    rows, features = tokens.shape
    shard, local_width = q_w.shape
    width = local_width // pairs
    heads = width // HEAD_DIM
    part = rows // groups
    chunks = min(CHUNKS, part // 16)
    units = 2 * pairs - 2
    dma = pltpu.SemaphoreType.DMA
    in_hbm = pl.BlockSpec(memory_space=pl.ANY)
    in_vmem = pl.BlockSpec(memory_space=pltpu.VMEM)
    bf16 = jnp.bfloat16
    return pl.pallas_call(
        functools.partial(exchange_kernel, pairs, groups, chunks),
        out_shape=pltpu.VMEM((part, features), bf16),
        in_specs=[in_hbm, in_vmem, in_hbm, in_hbm, in_hbm, in_vmem, in_vmem, in_hbm],
        out_specs=in_vmem,
        scratch_shapes=[
            pltpu.VMEM((rows, features), bf16),
            pltpu.VMEM((pairs, rows, features), bf16),
            pltpu.VMEM((heads, pairs, 2, shard, 3 * HEAD_DIM), bf16),
            pltpu.VMEM((2, 2, shard, local_width), bf16),
            pltpu.VMEM((2, 2, shard, local_width), bf16),
            pltpu.VMEM((pairs, heads, rows, HEAD_DIM), bf16),
            pltpu.VMEM((pairs, 2, 2, part, local_width), bf16),
            pltpu.VMEM((units, 2, part, shard), jnp.float32),
            pltpu.VMEM((units, 2, part, shard), bf16),
            pltpu.VMEM((units, 2, part, shard), bf16),
            pltpu.VMEM((units, 2, part, shard), bf16),
            pltpu.VMEM((pairs, 2, part, shard), bf16),
            dma((groups + 2,)), dma((2,)), dma((pairs, chunks)), dma, dma((pairs, 3, chunks)),
            dma, dma((pairs, heads, 3)), dma, dma, dma, dma((heads,)), dma, dma, dma, dma((2,)),
            dma((3,)), dma((6,)), dma, dma((pairs, heads)), dma((2,)), dma((pairs, pairs, heads)),
            dma, dma((units, 2)), dma, dma,
        ],
        compiler_params=pltpu.CompilerParams(
            collective_id=0, has_side_effects=True, vmem_limit_bytes=60 * 1024 * 1024
        ),
    )(
        tokens, ln_gain.reshape(1, features), q_w, k_w, v_w,
        q_gain.reshape(pairs, 1, width), k_gain.reshape(pairs, 1, width), out_w,
    )


def on_device(tokens, ln_gain, q_w, k_w, v_w, q_gain, k_gain, out_w):
    devices = lax.axis_size("dp")
    groups = lax.axis_size("mp")
    pairs = devices // 2
    fits = (
        devices % 2 == 0
        and groups == 4
        and q_w.shape[1] % (pairs * HEAD_DIM) == 0
        and q_w.shape[0] % 128 == 0
        and tokens.shape[0] == IMG_TOKENS
        and tokens.shape[0] % (16 * groups) == 0
        and pairs == 4
        and q_w.shape[1] == 2 * pairs * HEAD_DIM
    )
    if fits:
        return exchanged_heads(pairs, groups, tokens, ln_gain, q_w, k_w, v_w, q_gain, k_gain, out_w)
    return gathered_weights(tokens, ln_gain, q_w, k_w, v_w, q_gain, k_gain, out_w)


def solution(mesh):
    in_specs = (
        P("dp", None),
        P(),
        P("dp", "mp"),
        P("dp", "mp"),
        P("dp", "mp"),
        P("mp"),
        P("mp"),
        P("dp", "mp"),
    )
    out_specs = P(("dp", "mp"), None)
    return jax.shard_map(
        on_device, mesh=mesh, in_specs=in_specs, out_specs=out_specs, check_vma=False
    )
```

```python
import functools
import math

import jax
import jax.numpy as jnp
from jax import lax
from jax.experimental import pallas as pl
from jax.experimental.pallas import tpu as pltpu
from jax.sharding import PartitionSpec as P

HEAD_DIM = 128
IMG_TOKENS = 256


epsilon = 1e-06


def layer_norm(values, scale_gain):
    average = jnp.mean(values, axis=-1, keepdims=True)
    centred = values - average
    variance = jnp.mean(centred * centred, axis=-1, keepdims=True)
    return centred * lax.rsqrt(variance + epsilon) * scale_gain


def head_norm(projected, scale_gain):
    heads_count = projected.shape[1] // HEAD_DIM
    shaped = projected.reshape(projected.shape[0], heads_count, HEAD_DIM)
    normed = layer_norm(shaped, scale_gain.reshape(heads_count, HEAD_DIM))
    return normed.reshape(projected.shape).astype(jnp.bfloat16)


def attend(queries, key_rows, value_rows):
    scores = jnp.einsum(
        "bqhd,bkhd->bhqk", queries, key_rows, preferred_element_type=jnp.float32
    ) * (1.0 / math.sqrt(HEAD_DIM))
    highest = jnp.max(scores, axis=-1, keepdims=True)
    weights = jnp.exp(scores - highest)
    probs = (weights / jnp.sum(weights, axis=-1, keepdims=True)).astype(jnp.bfloat16)
    context = jnp.einsum("bhqk,bkhd->bqhd", probs, value_rows, preferred_element_type=jnp.float32)
    return context.astype(jnp.bfloat16)


def place_three(holder, pieces, offset, local_width):
    holder = lax.dynamic_update_slice(holder, pieces[0], (offset, 0))
    holder = lax.dynamic_update_slice(holder, pieces[1], (offset, local_width))
    return lax.dynamic_update_slice(holder, pieces[2], (offset, 2 * local_width))


def gathered_weights(tokens, ln_gain, q_weight, k_weight, v_weight, q_gain, k_gain, out_weight):
    normed = layer_norm(tokens.astype(jnp.float32), ln_gain).astype(jnp.bfloat16)
    token_count = normed.shape[0]
    local_width = q_weight.shape[1]
    feature_count = normed.shape[1]
    stacked = jnp.zeros((feature_count, 3 * local_width), jnp.bfloat16)
    projections = place_three(
        stacked,
        (
            lax.all_gather(q_weight, "dp", axis=0, tiled=True),
            lax.all_gather(k_weight, "dp", axis=0, tiled=True),
            lax.all_gather(v_weight, "dp", axis=0, tiled=True),
        ),
        jnp.int32(0),
        local_width,
    )
    combined = jnp.dot(normed, projections, preferred_element_type=jnp.float32)
    queries = combined[:, :local_width]
    key_rows = combined[:, local_width : 2 * local_width]
    value_cast = combined[:, 2 * local_width :].astype(jnp.bfloat16)
    query_normed = head_norm(queries, q_gain)
    key_normed = head_norm(key_rows, k_gain)
    images = token_count // IMG_TOKENS
    shaped = (images, IMG_TOKENS, local_width // HEAD_DIM, HEAD_DIM)
    context = attend(
        query_normed.reshape(shaped), key_normed.reshape(shaped), value_cast.reshape(shaped)
    )
    context = context.reshape(token_count, local_width)
    out_full = lax.all_gather(out_weight, "dp", axis=0, tiled=True)
    return lax.psum_scatter(
        lax.dot_general(
            context, out_full, (((1,), (1,)), ((), ())), preferred_element_type=jnp.float32
        ).astype(jnp.bfloat16),
        "mp",
        scatter_dimension=0,
        tiled=True,
    )


MESH = pl.DeviceIdType.MESH

CHUNKS = 4


def exchange_kernel(
    pairs, groups, chunks, tokens, ln_gain, q_w, k_w, v_w, q_gain, k_gain, out_w, result,
    raw, normed, weights, own_rows, out_rows, end_rows, staged, context, kept, partial, arrived, summed, final,
    local_sem, token_send, token_recv, peer_send, first_recv, peer_recv,
    w_send, w_recv, own_send, own_recv, pass_send, pass_recv, out_send, out_recv, side_send, side_recv,
    end_send, end_recv, x_send, x_recv, c_send, c_recv, p_send, p_recv, f_send, f_recv,
):
    dp = lax.axis_index("dp")
    group = lax.axis_index("mp")
    pair = dp // 2
    core = dp % 2
    rows = tokens.shape[0]
    part = rows // groups
    piece_rows = part // chunks
    shard = q_w.shape[0]
    width = q_w.shape[1] // pairs
    span = 2 * shard
    heads = width // HEAD_DIM
    has_up = pair + 1 < pairs
    has_down = pair > 0
    at_end = (pair == 0) | (pair == pairs - 1)
    beside_end = (pair == 1) | (pair == pairs - 2)
    inner = jnp.where(pair < pairs // 2, pair + 1, pair - 1)
    outer = jnp.where(pair < pairs // 2, pair - 1, pair + 1)

    def at_pair(other):
        return (other * 2 + core, group)

    partner = (pair * 2 + (1 - core), group)

    def at_group(other):
        return (dp, other)

    def remote(source, target, send, recv, device):
        return pltpu.make_async_remote_copy(
            src_ref=source, dst_ref=target, send_sem=send, recv_sem=recv,
            device_id=device, device_id_type=MESH,
        )

    def quarter_of(owner):
        return pl.ds(pl.multiple_of(owner * part, part), part)

    token_quarters = []
    for j in range(groups):
        place = quarter_of((group + j) % groups)
        token_quarters.append(
            pltpu.make_async_copy(tokens.at[place, :], raw.at[place, :], local_sem.at[j])
        )
        token_quarters[j].start()

    projections = (q_w, k_w, v_w)

    def columns(other, h, t):
        start = pl.multiple_of(other * width + h * HEAD_DIM, HEAD_DIM)
        return projections[t].at[:, pl.ds(start, HEAD_DIM)]

    def slot(h, block, side, t):
        return weights.at[h, block, side, :, pl.ds(t * HEAD_DIM, HEAD_DIM)]

    greeted = pltpu.get_barrier_semaphore()
    for step in range(1, pairs):
        pl.semaphore_signal(
            greeted, inc=1, device_id=at_pair((pair + step) % pairs), device_id_type=MESH
        )
    for step in range(1, groups):
        pl.semaphore_signal(
            greeted, inc=1, device_id=at_group((group + step) % groups), device_id_type=MESH
        )
    pl.semaphore_signal(greeted, inc=1, device_id=partner, device_id_type=MESH)
    beside = group + 1 - 2 * (group % 2)
    across = (group + 2) % 4
    pl.semaphore_signal(
        greeted, inc=1,
        device_id=(pair * 2 + 1 - core, jnp.where(core == 0, beside, across)), device_id_type=MESH,
    )

    locals_ = [pltpu.make_async_copy(out_w, own_rows, local_sem.at[groups])]
    for h in range(heads):
        for t in range(3):
            locals_.append(
                pltpu.make_async_copy(
                    columns(pair, h, t), slot(h, pair, core, t), local_sem.at[groups + 1],
                )
            )
    for copy in locals_:
        copy.start()

    def normalise(first_row, count):
        @pl.loop(0, count // 16)
        def _(step):
            place = pl.ds(pl.multiple_of(first_row + step * 16, 16), 16)
            values = raw[place, :].astype(jnp.float32)
            average = jnp.mean(values, axis=-1, keepdims=True)
            centred = values - average
            variance = jnp.mean(centred * centred, axis=-1, keepdims=True)
            scaled = centred * lax.rsqrt(variance + epsilon) * ln_gain[...]
            normed[pair, place, :] = scaled.astype(jnp.bfloat16)

    token_quarters[0].wait()
    normalise(group * part, part)

    def piece(block, owner, k):
        start = pl.multiple_of(owner * part + k * piece_rows, 16)
        return normed.at[block, pl.ds(start, piece_rows), :]

    def z_hop(block, k, up):
        there = piece(block, group, k)
        return remote(
            there, there, token_send.at[0 if up else 1], token_recv.at[block, k],
            at_pair(pair + 1 if up else pair - 1),
        )

    first = jnp.where(core == 0, beside, across)
    second = jnp.where(core == 0, across, beside)
    opposite = 3 - group

    def peer_copy(block, owner, place, k, other):
        there = piece(block, owner, k)
        return remote(
            there, there, peer_send, first_recv.at[block, k] if place == 0 else peer_recv.at[block, place - 1], at_group(other)
        )

    def weight_to(other, h, t):
        return remote(
            columns(other, h, t), slot(h, pair, core, t),
            w_send, w_recv.at[pair, h, t], at_pair(other),
        )

    def send_weights(up, plan):
        for h, distance in plan:
            other = pair + distance if up else pair - distance

            @pl.when(other < pairs if up else other >= 0)
            def _():
                for t in range(3):
                    weight_to(other, h, t).start()

    def own_weight(h, t):
        return remote(
            columns(pair, h, t), slot(h, pair, core, t), own_send, own_recv, partner
        )

    def side_of(rows_of, way, side, k=None):
        lanes = pl.ds(pl.multiple_of(side * shard, 128), shard)
        if k is None:
            return rows_of.at[way, :, lanes]
        depth = pairs * width // 2
        return rows_of.at[way, pl.ds(k * depth, depth), lanes]

    def transpose_rows():
        @pl.loop(0, pairs * width // 128)
        def _(k):
            place = pl.ds(pl.multiple_of(k * 128, 128), 128)
            lanes = pl.ds(pl.multiple_of(core * shard, 128), shard)
            out_rows[0, place, lanes] = jnp.transpose(own_rows[:, place])

    def out_over(side):
        there = side_of(out_rows, 0, side)
        return remote(there, there, out_send, out_recv, partner)

    sides = ((pair * 2, beside), (pair * 2 + 1, across))

    def rows_aside(side, k, device):
        return remote(
            side_of(out_rows, 0, side, k), side_of(out_rows, 1, side, k),
            side_send, side_recv.at[side, k], device,
        )

    with jax.named_scope("greet"):
        pl.semaphore_wait(greeted, pairs + groups)

    @pl.loop(0, chunks)
    def _(k):
        @pl.when(has_up)
        def _():
            z_hop(pair, k, True).start()

        @pl.when(has_down)
        def _():
            z_hop(pair, k, False).start()

    def end_over(side):
        return remote(
            side_of(out_rows, 0, side), side_of(end_rows, 0, side),
            end_send.at[0], end_recv.at[0], at_pair(inner),
        )

    def end_pass(side):
        there = side_of(end_rows, 0, side)
        return remote(there, there, end_send.at[1], end_recv.at[1], partner)

    def end_part(side, k, device):
        return remote(
            side_of(end_rows, 0, side, k), side_of(end_rows, 1, side, k),
            end_send.at[2], end_recv.at[2 + 2 * side + k], device,
        )

    for at, up in ((0, True), (pairs - 1, False)):
        @pl.when(pair == at)
        def _():
            send_weights(up, [(h, 1) for h in range(heads)])
            send_weights(up, [(0, distance) for distance in range(2, pairs)])

    for h in range(heads):
        for t in range(3):
            own_weight(h, t).start()
    for j in range(1, groups):
        token_quarters[j].wait()

    def relay(block, k, up):
        with jax.named_scope("relaywait"):
            z_hop(block, k, up).wait_recv()

        @pl.when(has_up if up else has_down)
        def _():
            z_hop(block, k, up).start()

        peer_copy(block, group, 0, k, first).start()
        peer_copy(block, group, 1, k, second).start()

    others = rows - part
    for distance in range(1, pairs):
        @pl.loop(0, chunks)
        def _(k):
            @pl.when(pair - distance >= 0)
            def _():
                relay(pair - distance, k, True)

            @pl.when(pair + distance < pairs)
            def _():
                relay(pair + distance, k, False)

            if distance == 1:
                for j in range(1, groups):
                    normalise(((group + j) % groups) * part + k * piece_rows, piece_rows)

        if distance == 1:
            with jax.named_scope("transpose"):
                locals_[0].wait()
                transpose_rows()
            out_over(core).start()
            for at, up in ((0, True), (pairs - 1, False)):
                @pl.when(pair == at)
                def _():
                    end_over(core).start()
                    send_weights(up, [(h, d) for h in range(1, heads) for d in range(pairs - 1, 1, -1)])

        @pl.when(has_up & (pair == distance))
        def _():
            send_weights(True, [(h, d) for h in range(heads) for d in range(1, pairs - 1)])

        @pl.when(has_down & (pair == pairs - 1 - distance))
        def _():
            send_weights(False, [(h, d) for h in range(heads) for d in range(1, pairs - 1)])

    def cross_tokens(block, k):
        with jax.named_scope("crosswait"):
            peer_copy(block, first, 0, k, first).wait_recv()
        peer_copy(block, first, 2, k, second).start()

    for distance in range(1, pairs):
        @pl.loop(0, chunks)
        def _(k):
            @pl.when(pair - distance >= 0)
            def _():
                cross_tokens(pair - distance, k)

            @pl.when(pair + distance < pairs)
            def _():
                cross_tokens(pair + distance, k)


    def pass_weights(h):
        for distance in range(1, pairs):
            for up in (True, False):
                other = pair - distance if up else pair + distance

                @pl.when(other >= 0 if up else other < pairs)
                def _():
                    for t in range(3):
                        there = slot(h, other, core, t)
                        with jax.named_scope("wwait"):
                            remote(
                                there, there, w_send, w_recv.at[other, h, t], partner
                            ).wait_recv()
                        remote(there, there, pass_send, pass_recv.at[h], partner).start()

    def all_passed(h):
        there = weights.at[h, pl.ds(0, pairs - 1), 1 - core]
        return remote(there, there, pass_send, pass_recv.at[h], partner)

    def all_own():
        there = weights.at[:, pair, 1 - core]
        return remote(there, there, own_send, own_recv, partner)

    pass_weights(0)
    there = weights.at[:, pair, core]
    pltpu.make_async_copy(there, there, local_sem.at[groups + 1]).wait()
    all_own().wait_recv()
    for distance in range(1, pairs):
        for below in (True, False):
            block = pair - distance if below else pair + distance

            @pl.when(block >= 0 if below else block < pairs)
            def _():
                with jax.named_scope("tokwait"):
                    for place, owner in ((1, second), (2, opposite)):
                        there = normed.at[block, quarter_of(owner), :]
                        remote(
                            there, there, peer_send, peer_recv.at[block, place - 1], partner
                        ).wait_recv()

    for to in range(2):
        rows_aside(core, 0, sides[to]).start()

    def head_layer_norm(values, scale_gain):
        average = jnp.mean(values, axis=-1, keepdims=True)
        centred = values - average
        variance = jnp.mean(centred * centred, axis=-1, keepdims=True)
        return (centred * lax.rsqrt(variance + epsilon) * scale_gain).astype(jnp.bfloat16)

    def head_place(block, h):
        return pl.ds(pl.multiple_of(block * width + h * HEAD_DIM, HEAD_DIM), HEAD_DIM)

    def context_hop(block, image, h, up):
        there = context.at[image, :, :, :, head_place(block, h)]
        return remote(
            there, there,
            c_send.at[0 if up else 1], c_recv.at[block, image, h],
            at_pair(pair + 1 if up else pair - 1),
        )

    def inside(image):
        return (image > 0) & (image < pairs - 1)

    def outside(image):
        return (image == 0) | (image == pairs - 1)

    def onward(image, up):
        if up:
            return has_up & ~((pair == pairs - 2) & inside(image))
        return has_down & ~((pair == 1) & inside(image))

    def awaited(block, image, up):
        if up:
            return (block >= 0) & ~((pair == pairs - 1) & inside(image))
        return (block < pairs) & ~((pair == 0) & inside(image))

    def send_context(image, h, across_middle, to_end):
        for up in (True, False):
            crossing = pair < pairs // 2 if up else pair >= pairs // 2
            wanted = (crossing & across_middle) | (~crossing & to_end)

            @pl.when(onward(image, up) & wanted)
            def _():
                context_hop(pair, image, h, up).start()

    def cross_context(image, h):
        for up in (True, False):
            @pl.when((pair == 1) if up else (pair == pairs - 2))
            def _():
                with jax.named_scope("crossctx"):
                    context_hop(outer, image, h, up).wait_recv()
                context_hop(outer, image, h, up).start()

    def pass_context(image, h, distance):
        for up in (True, False):
            block = pair - distance if up else pair + distance

            @pl.when(awaited(block, image, up) & ~(beside_end & (block == outer)))
            def _():
                with jax.named_scope("ctxwait%d" % distance):
                    context_hop(block, image, h, up).wait_recv()

                @pl.when(onward(image, up))
                def _():
                    context_hop(block, image, h, up).start()

    def half_over(image, h, at, owner):
        return remote(
            staged.at[image, h, quarter_of(owner), :],
            context.at[image, 1, at, :, head_place(pair, h)],
            x_send, x_recv.at[image, h], at_group(first),
        )

    def half_in(image, h):
        there = context.at[image, 1, :, :, head_place(pair, h)]
        with jax.named_scope("halfin"):
            remote(there, there, x_send, x_recv.at[image, h], partner).wait_recv()

    def attend_head(image, h):
        lanes = slice(h * HEAD_DIM, (h + 1) * HEAD_DIM)
        with jax.named_scope("attend"):
            total = jnp.dot(
                normed[image], weights[h].reshape(pairs * span, 3 * HEAD_DIM),
                preferred_element_type=jnp.float32,
            )
            queries = head_layer_norm(total[:, :HEAD_DIM], q_gain[pair, :, lanes])
            key_rows = head_layer_norm(total[:, HEAD_DIM : 2 * HEAD_DIM], k_gain[pair, :, lanes])
            value_rows = total[:, 2 * HEAD_DIM :].astype(jnp.bfloat16)
            scores = lax.dot_general(
                queries, key_rows, (((1,), (1,)), ((), ())), preferred_element_type=jnp.float32
            ) * (1.0 / math.sqrt(HEAD_DIM))
            highest = jnp.max(scores, axis=-1, keepdims=True)
            spread = jnp.exp(scores - highest)
            probs = (spread / jnp.sum(spread, axis=-1, keepdims=True)).astype(jnp.bfloat16)
            mixed = jnp.dot(probs, value_rows, preferred_element_type=jnp.float32)
            staged[image, h] = mixed.astype(jnp.bfloat16)

        for at, owner in enumerate((first, opposite)):
            half_over(image, h, at, owner).start()
        for at, owner in enumerate((group, second)):
            context[image, 0, at, :, head_place(pair, h)] = staged[image, h, quarter_of(owner), :]

    lower = pair < pairs // 2
    homely = jnp.where(lower, 1, pairs - 2)
    foreign = pairs - 1 - homely

    def image_at(step):
        if isinstance(step, int):
            return (0, pairs - 1, homely, foreign)[step]
        return jnp.where(step < 2, step * (pairs - 1), jnp.where(step == 2, homely, foreign))

    def projected_at(step):
        if isinstance(step, int):
            return (0, pairs - 1, foreign, homely)[step]
        return jnp.where(step < 2, step * (pairs - 1), jnp.where(step == 2, foreign, homely))

    def all_weights(h):
        with jax.named_scope("passedwait"):
            all_passed(h).wait_recv()

    all_weights(0)

    @pl.loop(0, pairs)
    def _(step):
        attend_head(image_at(step), 0)

    for to in range(2):
        rows_aside(core, 1, sides[to]).start()

    with jax.named_scope("sends"):
        for at in range(pairs):
            @pl.when(pair == at)
            def _():
                for way, blocks in ((0, at + 1 if at + 1 < pairs else 0), (1, pairs - at if at > 0 else 0)):
                    if blocks > 0:
                        there = normed.at[pl.ds(0, blocks), pl.ds(0, part), :]
                        remote(
                            there, there, token_send.at[way], token_recv.at[0, 0], partner
                        ).wait_send()
        there = normed.at[pl.ds(0, pairs - 1), pl.ds(0, 3 * part), :]
        remote(there, there, peer_send, peer_recv.at[0, 0], partner).wait_send()
        all_own().wait_send()
        out_over(1 - core).wait_recv()
        out_over(core).wait_send()


    def end_aside(k):
        for to in range(2):
            end_part(core, k, sides[to]).start()

    @pl.when(beside_end)
    def _():
        end_over(core).wait_recv()
        end_pass(core).start()
        end_aside(0)

    def partial_to(unit, c):
        return remote(
            partial.at[unit, c], arrived.at[unit, c], p_send, p_recv.at[unit, c], at_group(second)
        )

    def final_to(unit, c, image, span_of):
        return remote(summed.at[unit, c], final.at[span_of, c], f_send, f_recv, at_pair(image))

    def finals(count):
        there = final.at[pl.ds(0, count)]
        return remote(there, there, f_send, f_recv, partner)

    def project(unit, image, rows_of):
        with jax.named_scope("outproj"):
            total = None
            for j in range(2):
                product = lax.dot_general(
                    context[image, j].reshape(2 * part, pairs * width), rows_of[j],
                    (((1,), (0,)), ((), ())), preferred_element_type=jnp.float32,
                )
                total = product if total is None else total + product
            for c in range(2):
                kept[unit, c] = total[:part, c * shard : (c + 1) * shard]
                partial[unit, c] = total[part:, c * shard : (c + 1) * shard].astype(jnp.bfloat16)
        for c in range(2):
            partial_to(unit, c).start()

    def add_up(unit, c, image, span_of):
        with jax.named_scope("partwait"):
            partial_to(unit, c).wait_recv()
        total = (kept[unit, c] + arrived[unit, c].astype(jnp.float32)).astype(jnp.bfloat16)

        @pl.when(image != pair)
        def _():
            summed[unit, c] = total
            final_to(unit, c, image, span_of).start()

        @pl.when(image == pair)
        def _():
            final[span_of, c] = total

    def own_unit(image):
        return ~at_end | outside(image)

    def extra_unit(image):
        return beside_end & inside(image)

    def finish(image, extra):
        @pl.when(extra_unit(image) if extra else own_unit(image))
        def _():
            for c in range(2):
                add_up(pairs + image - 1 if extra else image, c, image, outer if extra else pair)

    for step in range(pairs):
        half_in(image_at(step), 0)
        send_context(image_at(step), 0, at_end | (step < 3), True)
    pass_weights(heads - 1)
    all_weights(heads - 1)

    def pass_most(image):
        for h in range(heads):
            pass_context(image, h, 1)
        pass_context(image, 0, 2)

    def pass_rest(image):
        pass_context(image, 1, 2)
        for h in range(heads):
            pass_context(image, h, 3)

    lag = 4

    @pl.loop(0, pairs + lag)
    def _(step):
        @pl.when(step < pairs)
        def _():
            attend_head(image_at(step), heads - 1)

        @pl.when((step > 0) & (step <= pairs))
        def _():
            image = image_at(step - 1)
            half_in(image, heads - 1)
            send_context(image, heads - 1, at_end | (step < 3), True)

            @pl.when(step < pairs)
            def _():
                cross_context(image, 0)

            @pl.when((step == 1) & ~at_end)
            def _():
                send_context(image_at(pairs - 1), 0, True, False)

            @pl.when((step == pairs) & beside_end)
            def _():
                end_aside(1)

        @pl.when(step >= lag)
        def _():
            image = projected_at(step - lag)

            @pl.when(step == lag)
            def _():
                cross_context(image_at(0), heads - 1)

            @pl.when(step < lag + 2)
            def _():
                pass_most(image)

            @pl.when(step < pairs + lag - 1)
            def _():
                cross_context(image_at(step - lag + 1), heads - 1)

            @pl.when((step < lag + 2) & ~at_end)
            def _():
                send_context(image_at(step - lag + 2), heads - 1, True, False)

            @pl.when(step == lag + 1)
            def _():
                cross_context(image_at(pairs - 1), 0)

            @pl.when(step == lag + 3)
            def _():
                for early in range(2):
                    finish(projected_at(early), False)

            pass_rest(image)

            @pl.when((step > lag) & (step < pairs + lag - 1))
            def _():
                pass_most(projected_at(step - lag + 1))

            @pl.when(own_unit(image))
            def _():
                @pl.when(step == lag)
                def _():
                    for side in range(2):
                        for k in range(2):
                            rows_aside(side, k, partner).wait_recv()

                project(image, image, out_rows)

            @pl.when(extra_unit(image))
            def _():
                @pl.when(step == lag + 2)
                def _():
                    end_pass(1 - core).wait_recv()
                    with jax.named_scope("endrows"):
                        for side in range(2):
                            for k in range(2):
                                end_part(side, k, partner).wait_recv()

                project(pairs + image - 1, image, end_rows)

    for step in range(2, pairs):
        for extra in (False, True):
            finish(projected_at(step), extra)

    with jax.named_scope("sends2"):
        others = weights.at[:, pl.ds(0, pairs - 1), core]
        remote(others, others, pass_send, pass_recv.at[0], partner).wait_send()
        remote(others, others, w_send, w_recv.at[0, 0, 0], partner).wait_send()

        @pl.when(at_end)
        def _():
            end_over(core).wait_send()

        @pl.when(beside_end)
        def _():
            end_pass(core).wait_send()
            both = end_rows.at[0]
            remote(both, both, end_send.at[2], end_recv.at[2], partner).wait_send()

        def sent(way, images, blocks):
            there = context.at[pl.ds(0, images), :, :, :, pl.ds(0, blocks * width)]
            return remote(there, there, c_send.at[way], c_recv.at[0, 0, 0], partner)

        for at, counts in (
            (0, ((0, pairs, 1),)),
            (1, ((0, pairs, 2), (1, 2, pairs - 1))),
            (pairs - 2, ((0, 2, pairs - 1), (1, pairs, 2))),
            (pairs - 1, ((1, pairs, 1),)),
        ):
            @pl.when(pair == at)
            def _():
                for way, images, blocks in counts:
                    sent(way, images, blocks).wait_send()

    with jax.named_scope("sends3"):
        both = out_rows.at[0]
        remote(both, both, side_send, side_recv.at[0], partner).wait_send()
        half = staged.at[:, :, pl.ds(0, 2 * part), :]
        remote(half, half, x_send, x_recv.at[0, 0], partner).wait_send()
        for few, units in ((at_end, 2), (beside_end, 2 * pairs - 2)):
            @pl.when(few)
            def _():
                whole = partial.at[pl.ds(0, units)]
                remote(whole, whole, p_send, p_recv.at[0, 0], partner).wait_send()

    with jax.named_scope("finalwait"):
        @pl.when(at_end)
        def _():
            finals(pairs - 1).wait_recv()

        @pl.when(~at_end)
        def _():
            finals(pairs - 2).wait_recv()
    for p in range(pairs):
        for c in range(2):
            start = (2 * p + c) * shard
            result[:, start : start + shard] = final[p, c]
    with jax.named_scope("sends4"):
        @pl.when(at_end)
        def _():
            finals(1).wait_send()

        @pl.when(~at_end)
        def _():
            finals(pairs).wait_send()


def exchanged_heads(pairs, groups, tokens, ln_gain, q_w, k_w, v_w, q_gain, k_gain, out_w):
    rows, features = tokens.shape
    shard, local_width = q_w.shape
    width = local_width // pairs
    heads = width // HEAD_DIM
    part = rows // groups
    chunks = min(CHUNKS, part // 16)
    units = 2 * pairs - 2
    dma = pltpu.SemaphoreType.DMA
    in_hbm = pl.BlockSpec(memory_space=pl.ANY)
    in_vmem = pl.BlockSpec(memory_space=pltpu.VMEM)
    bf16 = jnp.bfloat16
    return pl.pallas_call(
        functools.partial(exchange_kernel, pairs, groups, chunks),
        out_shape=pltpu.VMEM((part, features), bf16),
        in_specs=[in_hbm, in_vmem, in_hbm, in_hbm, in_hbm, in_vmem, in_vmem, in_hbm],
        out_specs=in_vmem,
        scratch_shapes=[
            pltpu.VMEM((rows, features), bf16),
            pltpu.VMEM((pairs, rows, features), bf16),
            pltpu.VMEM((heads, pairs, 2, shard, 3 * HEAD_DIM), bf16),
            pltpu.VMEM((shard, local_width), bf16),
            pltpu.VMEM((2, local_width, 2 * shard), bf16),
            pltpu.VMEM((2, local_width, 2 * shard), bf16),
            pltpu.VMEM((pairs, heads, rows, HEAD_DIM), bf16),
            pltpu.VMEM((pairs, 2, 2, part, local_width), bf16),
            pltpu.VMEM((units, 2, part, shard), jnp.float32),
            pltpu.VMEM((units, 2, part, shard), bf16),
            pltpu.VMEM((units, 2, part, shard), bf16),
            pltpu.VMEM((units, 2, part, shard), bf16),
            pltpu.VMEM((pairs, 2, part, shard), bf16),
            dma((groups + 2,)), dma((2,)), dma((pairs, chunks)), dma, dma((pairs, chunks)), dma((pairs, 2)),
            dma, dma((pairs, heads, 3)), dma, dma, dma, dma((heads,)), dma, dma, dma, dma((2, 2)),
            dma((3,)), dma((6,)), dma, dma((pairs, heads)), dma((2,)), dma((pairs, pairs, heads)),
            dma, dma((units, 2)), dma, dma,
        ],
        compiler_params=pltpu.CompilerParams(
            collective_id=0, has_side_effects=True, vmem_limit_bytes=60 * 1024 * 1024
        ),
    )(
        tokens, ln_gain.reshape(1, features), q_w, k_w, v_w,
        q_gain.reshape(pairs, 1, width), k_gain.reshape(pairs, 1, width), out_w,
    )


def on_device(tokens, ln_gain, q_w, k_w, v_w, q_gain, k_gain, out_w):
    devices = lax.axis_size("dp")
    groups = lax.axis_size("mp")
    pairs = devices // 2
    fits = (
        devices % 2 == 0
        and groups == 4
        and q_w.shape[1] % (pairs * HEAD_DIM) == 0
        and q_w.shape[0] % 128 == 0
        and tokens.shape[0] == IMG_TOKENS
        and tokens.shape[0] % (16 * groups) == 0
        and pairs == 4
        and q_w.shape[1] == 2 * pairs * HEAD_DIM
    )
    if fits:
        return exchanged_heads(pairs, groups, tokens, ln_gain, q_w, k_w, v_w, q_gain, k_gain, out_w)
    return gathered_weights(tokens, ln_gain, q_w, k_w, v_w, q_gain, k_gain, out_w)


def solution(mesh):
    in_specs = (
        P("dp", None),
        P(),
        P("dp", "mp"),
        P("dp", "mp"),
        P("dp", "mp"),
        P("mp"),
        P("mp"),
        P("dp", "mp"),
    )
    out_specs = P(("dp", "mp"), None)
    return jax.shard_map(
        on_device, mesh=mesh, in_specs=in_specs, out_specs=out_specs, check_vma=False
    )
```

```python
import functools
import math

import jax
import jax.numpy as jnp
from jax import lax
from jax.experimental import pallas as pl
from jax.experimental.pallas import tpu as pltpu
from jax.sharding import PartitionSpec as P

HEAD_DIM = 128
IMG_TOKENS = 256


epsilon = 1e-06


def layer_norm(values, scale_gain):
    average = jnp.mean(values, axis=-1, keepdims=True)
    centred = values - average
    variance = jnp.mean(centred * centred, axis=-1, keepdims=True)
    return centred * lax.rsqrt(variance + epsilon) * scale_gain


def head_norm(projected, scale_gain):
    heads_count = projected.shape[1] // HEAD_DIM
    shaped = projected.reshape(projected.shape[0], heads_count, HEAD_DIM)
    normed = layer_norm(shaped, scale_gain.reshape(heads_count, HEAD_DIM))
    return normed.reshape(projected.shape).astype(jnp.bfloat16)


def attend(queries, key_rows, value_rows):
    scores = jnp.einsum(
        "bqhd,bkhd->bhqk", queries, key_rows, preferred_element_type=jnp.float32
    ) * (1.0 / math.sqrt(HEAD_DIM))
    highest = jnp.max(scores, axis=-1, keepdims=True)
    weights = jnp.exp(scores - highest)
    probs = (weights / jnp.sum(weights, axis=-1, keepdims=True)).astype(jnp.bfloat16)
    context = jnp.einsum("bhqk,bkhd->bqhd", probs, value_rows, preferred_element_type=jnp.float32)
    return context.astype(jnp.bfloat16)


def place_three(holder, pieces, offset, local_width):
    holder = lax.dynamic_update_slice(holder, pieces[0], (offset, 0))
    holder = lax.dynamic_update_slice(holder, pieces[1], (offset, local_width))
    return lax.dynamic_update_slice(holder, pieces[2], (offset, 2 * local_width))


def gathered_weights(tokens, ln_gain, q_weight, k_weight, v_weight, q_gain, k_gain, out_weight):
    normed = layer_norm(tokens.astype(jnp.float32), ln_gain).astype(jnp.bfloat16)
    token_count = normed.shape[0]
    local_width = q_weight.shape[1]
    feature_count = normed.shape[1]
    stacked = jnp.zeros((feature_count, 3 * local_width), jnp.bfloat16)
    projections = place_three(
        stacked,
        (
            lax.all_gather(q_weight, "dp", axis=0, tiled=True),
            lax.all_gather(k_weight, "dp", axis=0, tiled=True),
            lax.all_gather(v_weight, "dp", axis=0, tiled=True),
        ),
        jnp.int32(0),
        local_width,
    )
    combined = jnp.dot(normed, projections, preferred_element_type=jnp.float32)
    queries = combined[:, :local_width]
    key_rows = combined[:, local_width : 2 * local_width]
    value_cast = combined[:, 2 * local_width :].astype(jnp.bfloat16)
    query_normed = head_norm(queries, q_gain)
    key_normed = head_norm(key_rows, k_gain)
    images = token_count // IMG_TOKENS
    shaped = (images, IMG_TOKENS, local_width // HEAD_DIM, HEAD_DIM)
    context = attend(
        query_normed.reshape(shaped), key_normed.reshape(shaped), value_cast.reshape(shaped)
    )
    context = context.reshape(token_count, local_width)
    out_full = lax.all_gather(out_weight, "dp", axis=0, tiled=True)
    return lax.psum_scatter(
        lax.dot_general(
            context, out_full, (((1,), (1,)), ((), ())), preferred_element_type=jnp.float32
        ).astype(jnp.bfloat16),
        "mp",
        scatter_dimension=0,
        tiled=True,
    )


MESH = pl.DeviceIdType.MESH

CHUNKS = 4


def exchange_kernel(
    pairs, groups, chunks, tokens, ln_gain, q_w, k_w, v_w, q_gain, k_gain, out_w, result,
    raw, normed, weights, own_rows, out_rows, end_rows, staged, context, kept, partial, arrived, summed, final,
    local_sem, token_send, token_recv, peer_send, first_recv, peer_recv,
    w_send, w_recv, own_send, own_recv, pass_send, pass_recv, out_send, out_recv, side_send, side_recv,
    end_send, end_recv, x_send, x_recv, c_send, c_recv, p_send, p_recv, f_send, f_recv,
):
    dp = lax.axis_index("dp")
    group = lax.axis_index("mp")
    pair = dp // 2
    core = dp % 2
    rows = tokens.shape[0]
    part = rows // groups
    piece_rows = part // chunks
    shard = q_w.shape[0]
    width = q_w.shape[1] // pairs
    span = 2 * shard
    heads = width // HEAD_DIM
    has_up = pair + 1 < pairs
    has_down = pair > 0
    at_end = (pair == 0) | (pair == pairs - 1)
    beside_end = (pair == 1) | (pair == pairs - 2)
    inner = jnp.where(pair < pairs // 2, pair + 1, pair - 1)
    outer = jnp.where(pair < pairs // 2, pair - 1, pair + 1)

    def at_pair(other):
        return (other * 2 + core, group)

    partner = (pair * 2 + (1 - core), group)

    def at_group(other):
        return (dp, other)

    def remote(source, target, send, recv, device):
        return pltpu.make_async_remote_copy(
            src_ref=source, dst_ref=target, send_sem=send, recv_sem=recv,
            device_id=device, device_id_type=MESH,
        )

    def quarter_of(owner):
        return pl.ds(pl.multiple_of(owner * part, part), part)

    token_quarters = []
    for j in range(groups):
        place = quarter_of((group + j) % groups)
        token_quarters.append(
            pltpu.make_async_copy(tokens.at[place, :], raw.at[place, :], local_sem.at[j])
        )
        token_quarters[j].start()

    projections = (q_w, k_w, v_w)

    def columns(other, h, t):
        start = pl.multiple_of(other * width + h * HEAD_DIM, HEAD_DIM)
        return projections[t].at[:, pl.ds(start, HEAD_DIM)]

    def slot(h, block, side, t):
        return weights.at[h, block, side, :, pl.ds(t * HEAD_DIM, HEAD_DIM)]

    greeted = pltpu.get_barrier_semaphore()
    for step in range(1, pairs):
        pl.semaphore_signal(
            greeted, inc=1, device_id=at_pair((pair + step) % pairs), device_id_type=MESH
        )
    for step in range(1, groups):
        pl.semaphore_signal(
            greeted, inc=1, device_id=at_group((group + step) % groups), device_id_type=MESH
        )
    pl.semaphore_signal(greeted, inc=1, device_id=partner, device_id_type=MESH)
    beside = group + 1 - 2 * (group % 2)
    across = (group + 2) % 4
    pl.semaphore_signal(
        greeted, inc=1,
        device_id=(pair * 2 + 1 - core, jnp.where(core == 0, beside, across)), device_id_type=MESH,
    )

    locals_ = [pltpu.make_async_copy(out_w, own_rows, local_sem.at[groups])]
    for h in range(heads):
        for t in range(3):
            locals_.append(
                pltpu.make_async_copy(
                    columns(pair, h, t), slot(h, pair, core, t), local_sem.at[groups + 1],
                )
            )
    for copy in locals_:
        copy.start()

    def normalise(first_row, count):
        @pl.loop(0, count // 16)
        def _(step):
            place = pl.ds(pl.multiple_of(first_row + step * 16, 16), 16)
            values = raw[place, :].astype(jnp.float32)
            average = jnp.mean(values, axis=-1, keepdims=True)
            centred = values - average
            variance = jnp.mean(centred * centred, axis=-1, keepdims=True)
            scaled = centred * lax.rsqrt(variance + epsilon) * ln_gain[...]
            normed[pair, place, :] = scaled.astype(jnp.bfloat16)

    token_quarters[0].wait()
    normalise(group * part, part)

    def piece(block, owner, k):
        start = pl.multiple_of(owner * part + k * piece_rows, 16)
        return normed.at[block, pl.ds(start, piece_rows), :]

    def z_hop(block, k, up):
        there = piece(block, group, k)
        return remote(
            there, there, token_send.at[0 if up else 1], token_recv.at[block, k],
            at_pair(pair + 1 if up else pair - 1),
        )

    first = jnp.where(core == 0, beside, across)
    second = jnp.where(core == 0, across, beside)
    opposite = 3 - group

    def peer_copy(block, owner, place, k, other):
        there = piece(block, owner, k)
        return remote(
            there, there, peer_send, first_recv.at[block, k] if place == 0 else peer_recv.at[block, place - 1], at_group(other)
        )

    def weight_to(other, h, t):
        return remote(
            columns(other, h, t), slot(h, pair, core, t),
            w_send, w_recv.at[pair, h, t], at_pair(other),
        )

    def send_weights(up, plan):
        for h, distance in plan:
            other = pair + distance if up else pair - distance

            @pl.when(other < pairs if up else other >= 0)
            def _():
                for t in range(3):
                    weight_to(other, h, t).start()

    def own_weight(h, t):
        return remote(
            columns(pair, h, t), slot(h, pair, core, t), own_send, own_recv, partner
        )

    def side_of(rows_of, way, side, k=None):
        lanes = pl.ds(pl.multiple_of(side * shard, 128), shard)
        if k is None:
            return rows_of.at[way, :, lanes]
        depth = pairs * width // 2
        return rows_of.at[way, pl.ds(k * depth, depth), lanes]

    def transpose_rows():
        @pl.loop(0, pairs * width // 128)
        def _(k):
            place = pl.ds(pl.multiple_of(k * 128, 128), 128)
            lanes = pl.ds(pl.multiple_of(core * shard, 128), shard)
            out_rows[0, place, lanes] = jnp.transpose(own_rows[:, place])

    def out_over(side):
        there = side_of(out_rows, 0, side)
        return remote(there, there, out_send, out_recv, partner)

    sides = ((pair * 2, beside), (pair * 2 + 1, across))

    def rows_aside(side, k, device):
        return remote(
            side_of(out_rows, 0, side, k), side_of(out_rows, 1, side, k),
            side_send, side_recv.at[side, k], device,
        )

    with jax.named_scope("greet"):
        pl.semaphore_wait(greeted, pairs + groups)

    @pl.loop(0, chunks)
    def _(k):
        @pl.when(has_up)
        def _():
            z_hop(pair, k, True).start()

        @pl.when(has_down)
        def _():
            z_hop(pair, k, False).start()

    def end_over(side):
        return remote(
            side_of(out_rows, 0, side), side_of(end_rows, 0, side),
            end_send.at[0], end_recv.at[0], at_pair(inner),
        )

    def end_pass(side):
        there = side_of(end_rows, 0, side)
        return remote(there, there, end_send.at[1], end_recv.at[1], partner)

    def end_part(side, k, device):
        return remote(
            side_of(end_rows, 0, side, k), side_of(end_rows, 1, side, k),
            end_send.at[2], end_recv.at[2 + 2 * side + k], device,
        )

    for at, up in ((0, True), (pairs - 1, False)):
        @pl.when(pair == at)
        def _():
            send_weights(up, [(h, 1) for h in range(heads)])
            send_weights(up, [(0, distance) for distance in range(2, pairs)])

    for h in range(heads):
        for t in range(3):
            own_weight(h, t).start()
    for j in range(1, groups):
        token_quarters[j].wait()

    def relay(block, k, up):
        with jax.named_scope("relaywait"):
            z_hop(block, k, up).wait_recv()

        @pl.when(has_up if up else has_down)
        def _():
            z_hop(block, k, up).start()

        peer_copy(block, group, 0, k, first).start()
        peer_copy(block, group, 1, k, second).start()

    others = rows - part
    for distance in range(1, pairs):
        @pl.loop(0, chunks)
        def _(k):
            @pl.when(pair - distance >= 0)
            def _():
                relay(pair - distance, k, True)

            @pl.when(pair + distance < pairs)
            def _():
                relay(pair + distance, k, False)

            if distance == 1:
                for j in range(1, groups):
                    normalise(((group + j) % groups) * part + k * piece_rows, piece_rows)

        if distance == 1:
            with jax.named_scope("transpose"):
                locals_[0].wait()
                transpose_rows()
            out_over(core).start()
            for at, up in ((0, True), (pairs - 1, False)):
                @pl.when(pair == at)
                def _():
                    end_over(core).start()
                    send_weights(up, [(h, d) for h in range(1, heads) for d in range(pairs - 1, 1, -1)])

        @pl.when(has_up & (pair == distance))
        def _():
            send_weights(True, [(h, d) for h in range(heads) for d in range(1, pairs - 1)])

        @pl.when(has_down & (pair == pairs - 1 - distance))
        def _():
            send_weights(False, [(h, d) for h in range(heads) for d in range(1, pairs - 1)])

    def cross_tokens(block, k):
        with jax.named_scope("crosswait"):
            peer_copy(block, first, 0, k, first).wait_recv()
        peer_copy(block, first, 2, k, second).start()

    for distance in range(1, pairs):
        @pl.loop(0, chunks)
        def _(k):
            @pl.when(pair - distance >= 0)
            def _():
                cross_tokens(pair - distance, k)

            @pl.when(pair + distance < pairs)
            def _():
                cross_tokens(pair + distance, k)


    def pass_weights(h):
        for distance in range(1, pairs):
            for up in (True, False):
                other = pair - distance if up else pair + distance

                @pl.when(other >= 0 if up else other < pairs)
                def _():
                    for t in range(3):
                        there = slot(h, other, core, t)
                        with jax.named_scope("wwait"):
                            remote(
                                there, there, w_send, w_recv.at[other, h, t], partner
                            ).wait_recv()
                        remote(there, there, pass_send, pass_recv.at[h], partner).start()

    def all_passed(h):
        there = weights.at[h, pl.ds(0, pairs - 1), 1 - core]
        return remote(there, there, pass_send, pass_recv.at[h], partner)

    def all_own():
        there = weights.at[:, pair, 1 - core]
        return remote(there, there, own_send, own_recv, partner)

    pass_weights(0)
    there = weights.at[:, pair, core]
    pltpu.make_async_copy(there, there, local_sem.at[groups + 1]).wait()
    all_own().wait_recv()
    for distance in range(1, pairs):
        for below in (True, False):
            block = pair - distance if below else pair + distance

            @pl.when(block >= 0 if below else block < pairs)
            def _():
                with jax.named_scope("tokwait"):
                    for place, owner in ((1, second), (2, opposite)):
                        there = normed.at[block, quarter_of(owner), :]
                        remote(
                            there, there, peer_send, peer_recv.at[block, place - 1], partner
                        ).wait_recv()

    for to in range(2):
        rows_aside(core, 0, sides[to]).start()

    def head_layer_norm(values, scale_gain):
        average = jnp.mean(values, axis=-1, keepdims=True)
        centred = values - average
        variance = jnp.mean(centred * centred, axis=-1, keepdims=True)
        return (centred * lax.rsqrt(variance + epsilon) * scale_gain).astype(jnp.bfloat16)

    def head_place(block, h):
        return pl.ds(pl.multiple_of(block * width + h * HEAD_DIM, HEAD_DIM), HEAD_DIM)

    def context_hop(block, image, h, up):
        there = context.at[image, :, :, :, head_place(block, h)]
        return remote(
            there, there,
            c_send.at[0 if up else 1], c_recv.at[block, image, h],
            at_pair(pair + 1 if up else pair - 1),
        )

    def inside(image):
        return (image > 0) & (image < pairs - 1)

    def outside(image):
        return (image == 0) | (image == pairs - 1)

    def onward(image, up):
        if up:
            return has_up & ~((pair == pairs - 2) & inside(image))
        return has_down & ~((pair == 1) & inside(image))

    def awaited(block, image, up):
        if up:
            return (block >= 0) & ~((pair == pairs - 1) & inside(image))
        return (block < pairs) & ~((pair == 0) & inside(image))

    def send_context(image, h, across_middle, to_end):
        for up in (True, False):
            crossing = pair < pairs // 2 if up else pair >= pairs // 2
            wanted = (crossing & across_middle) | (~crossing & to_end)

            @pl.when(onward(image, up) & wanted)
            def _():
                context_hop(pair, image, h, up).start()

    def cross_context(image, h):
        for up in (True, False):
            @pl.when((pair == 1) if up else (pair == pairs - 2))
            def _():
                with jax.named_scope("crossctx"):
                    context_hop(outer, image, h, up).wait_recv()
                context_hop(outer, image, h, up).start()

    def pass_context(image, h, distance):
        for up in (True, False):
            block = pair - distance if up else pair + distance

            @pl.when(awaited(block, image, up) & ~(beside_end & (block == outer)))
            def _():
                with jax.named_scope("ctxwait%d" % distance):
                    context_hop(block, image, h, up).wait_recv()

                @pl.when(onward(image, up))
                def _():
                    context_hop(block, image, h, up).start()

    def half_over(image, h, at, owner):
        return remote(
            staged.at[image, h, quarter_of(owner), :],
            context.at[image, 1, at, :, head_place(pair, h)],
            x_send, x_recv.at[image, h], at_group(first),
        )

    def half_in(image, h):
        there = context.at[image, 1, :, :, head_place(pair, h)]
        with jax.named_scope("halfin"):
            remote(there, there, x_send, x_recv.at[image, h], partner).wait_recv()

    def attend_head(image, h):
        lanes = slice(h * HEAD_DIM, (h + 1) * HEAD_DIM)
        with jax.named_scope("attend"):
            total = jnp.dot(
                normed[image], weights[h].reshape(pairs * span, 3 * HEAD_DIM),
                preferred_element_type=jnp.float32,
            )
            queries = head_layer_norm(total[:, :HEAD_DIM], q_gain[pair, :, lanes])
            key_rows = head_layer_norm(total[:, HEAD_DIM : 2 * HEAD_DIM], k_gain[pair, :, lanes])
            value_rows = total[:, 2 * HEAD_DIM :].astype(jnp.bfloat16)
            scores = lax.dot_general(
                queries, key_rows, (((1,), (1,)), ((), ())), preferred_element_type=jnp.float32
            ) * (1.0 / math.sqrt(HEAD_DIM))
            highest = jnp.max(scores, axis=-1, keepdims=True)
            spread = jnp.exp(scores - highest)
            probs = (spread / jnp.sum(spread, axis=-1, keepdims=True)).astype(jnp.bfloat16)
            mixed = jnp.dot(probs, value_rows, preferred_element_type=jnp.float32)
            staged[image, h] = mixed.astype(jnp.bfloat16)

        for at, owner in enumerate((first, opposite)):
            half_over(image, h, at, owner).start()
        for at, owner in enumerate((group, second)):
            context[image, 0, at, :, head_place(pair, h)] = staged[image, h, quarter_of(owner), :]

    lower = pair < pairs // 2
    homely = jnp.where(lower, 1, pairs - 2)
    foreign = pairs - 1 - homely

    def image_at(step):
        if isinstance(step, int):
            return (0, pairs - 1, homely, foreign)[step]
        return jnp.where(step < 2, step * (pairs - 1), jnp.where(step == 2, homely, foreign))

    def projected_at(step):
        if isinstance(step, int):
            return (0, pairs - 1, foreign, homely)[step]
        return jnp.where(step < 2, step * (pairs - 1), jnp.where(step == 2, foreign, homely))

    def all_weights(h):
        with jax.named_scope("passedwait"):
            all_passed(h).wait_recv()

    all_weights(0)

    @pl.loop(0, pairs)
    def _(step):
        attend_head(image_at(step), 0)

    for to in range(2):
        rows_aside(core, 1, sides[to]).start()

    with jax.named_scope("sends"):
        for at in range(pairs):
            @pl.when(pair == at)
            def _():
                for way, blocks in ((0, at + 1 if at + 1 < pairs else 0), (1, pairs - at if at > 0 else 0)):
                    if blocks > 0:
                        there = normed.at[pl.ds(0, blocks), pl.ds(0, part), :]
                        remote(
                            there, there, token_send.at[way], token_recv.at[0, 0], partner
                        ).wait_send()
        there = normed.at[pl.ds(0, pairs - 1), pl.ds(0, 3 * part), :]
        remote(there, there, peer_send, peer_recv.at[0, 0], partner).wait_send()
        all_own().wait_send()
        out_over(1 - core).wait_recv()
        out_over(core).wait_send()


    def end_aside(k):
        for to in range(2):
            end_part(core, k, sides[to]).start()

    @pl.when(beside_end)
    def _():
        end_over(core).wait_recv()
        end_pass(core).start()
        end_aside(0)

    def partial_to(unit, c):
        return remote(
            partial.at[unit, c], arrived.at[unit, c], p_send, p_recv.at[unit, c], at_group(second)
        )

    def final_to(unit, c, image, span_of):
        return remote(summed.at[unit, c], final.at[span_of, c], f_send, f_recv, at_pair(image))

    def finals(count):
        there = final.at[pl.ds(0, count)]
        return remote(there, there, f_send, f_recv, partner)

    def project(unit, image, rows_of):
        with jax.named_scope("outproj"):
            total = None
            for j in range(2):
                product = lax.dot_general(
                    context[image, j].reshape(2 * part, pairs * width), rows_of[j],
                    (((1,), (0,)), ((), ())), preferred_element_type=jnp.float32,
                )
                total = product if total is None else total + product
            for c in range(2):
                kept[unit, c] = total[:part, c * shard : (c + 1) * shard]
                partial[unit, c] = total[part:, c * shard : (c + 1) * shard].astype(jnp.bfloat16)
        for c in range(2):
            partial_to(unit, c).start()

    def add_up(unit, c, image, span_of):
        with jax.named_scope("partwait"):
            partial_to(unit, c).wait_recv()
        total = (kept[unit, c] + arrived[unit, c].astype(jnp.float32)).astype(jnp.bfloat16)

        @pl.when(image != pair)
        def _():
            summed[unit, c] = total
            final_to(unit, c, image, span_of).start()

        @pl.when(image == pair)
        def _():
            final[span_of, c] = total

    def own_unit(image):
        return ~at_end | outside(image)

    def extra_unit(image):
        return beside_end & inside(image)

    def finish(image, extra):
        @pl.when(extra_unit(image) if extra else own_unit(image))
        def _():
            for c in range(2):
                add_up(pairs + image - 1 if extra else image, c, image, outer if extra else pair)

    for step in range(pairs):
        half_in(image_at(step), 0)
        send_context(image_at(step), 0, at_end | (step < 3), True)
    pass_weights(heads - 1)
    all_weights(heads - 1)

    def pass_most(image):
        for h in range(heads):
            pass_context(image, h, 1)
        pass_context(image, 0, 2)

    def pass_rest(image):
        pass_context(image, 1, 2)
        for h in range(heads):
            pass_context(image, h, 3)

    lag = 4

    @pl.loop(0, pairs + lag)
    def _(step):
        @pl.when(step < pairs)
        def _():
            attend_head(image_at(step), heads - 1)

        @pl.when((step > 0) & (step <= pairs))
        def _():
            image = image_at(step - 1)
            half_in(image, heads - 1)
            send_context(image, heads - 1, at_end | (step < 3), True)

            @pl.when(step < pairs)
            def _():
                cross_context(image, 0)

            @pl.when((step == 1) & ~at_end)
            def _():
                send_context(image_at(pairs - 1), 0, True, False)

            for at, (turn, h, distance) in enumerate(((0, 0, 1), (1, 0, 1), (0, 0, 2))):
                @pl.when((step == at + 1) & beside_end)
                def _():
                    pass_context(image_at(turn), h, distance)

            @pl.when((step == pairs) & beside_end)
            def _():
                end_aside(1)

        @pl.when(step >= lag)
        def _():
            image = projected_at(step - lag)

            @pl.when(step == lag)
            def _():
                cross_context(image_at(0), heads - 1)

            @pl.when(step == lag + 3)
            def _():
                for early in range(2):
                    finish(projected_at(early), False)

            @pl.when(at_end | (step > lag + 1))
            def _():
                pass_most(image)

            @pl.when((step == lag) & beside_end)
            def _():
                pass_context(image_at(0), 1, 1)
                cross_context(image_at(1), heads - 1)
                send_context(image_at(2), heads - 1, True, False)
                pass_context(image_at(1), 1, 1)
                pass_context(image_at(1), 0, 2)
                cross_context(image_at(2), heads - 1)
                send_context(image_at(3), heads - 1, True, False)
                cross_context(image_at(3), 0)

            @pl.when(step == lag + 1)
            def _():
                cross_context(image_at(pairs - 1), heads - 1)

            @pl.when(step == lag + 3)
            def _():
                finish(projected_at(2), False)

            pass_rest(image)

            @pl.when(own_unit(image))
            def _():
                @pl.when(step == lag)
                def _():
                    for side in range(2):
                        for k in range(2):
                            rows_aside(side, k, partner).wait_recv()

                project(image, image, out_rows)

            @pl.when(extra_unit(image))
            def _():
                @pl.when(step == lag + 2)
                def _():
                    end_pass(1 - core).wait_recv()
                    with jax.named_scope("endrows"):
                        for side in range(2):
                            for k in range(2):
                                end_part(side, k, partner).wait_recv()

                project(pairs + image - 1, image, end_rows)

    finish(projected_at(2), True)
    for extra in (False, True):
        finish(projected_at(3), extra)

    with jax.named_scope("sends2"):
        others = weights.at[:, pl.ds(0, pairs - 1), core]
        remote(others, others, pass_send, pass_recv.at[0], partner).wait_send()
        remote(others, others, w_send, w_recv.at[0, 0, 0], partner).wait_send()

        @pl.when(at_end)
        def _():
            end_over(core).wait_send()

        @pl.when(beside_end)
        def _():
            end_pass(core).wait_send()
            both = end_rows.at[0]
            remote(both, both, end_send.at[2], end_recv.at[2], partner).wait_send()

        def sent(way, images, blocks):
            there = context.at[pl.ds(0, images), :, :, :, pl.ds(0, blocks * width)]
            return remote(there, there, c_send.at[way], c_recv.at[0, 0, 0], partner)

        for at, counts in (
            (0, ((0, pairs, 1),)),
            (1, ((0, pairs, 2), (1, 2, pairs - 1))),
            (pairs - 2, ((0, 2, pairs - 1), (1, pairs, 2))),
            (pairs - 1, ((1, pairs, 1),)),
        ):
            @pl.when(pair == at)
            def _():
                for way, images, blocks in counts:
                    sent(way, images, blocks).wait_send()

    with jax.named_scope("sends3"):
        both = out_rows.at[0]
        remote(both, both, side_send, side_recv.at[0], partner).wait_send()
        half = staged.at[:, :, pl.ds(0, 2 * part), :]
        remote(half, half, x_send, x_recv.at[0, 0], partner).wait_send()
        for few, units in ((at_end, 2), (beside_end, 2 * pairs - 2)):
            @pl.when(few)
            def _():
                whole = partial.at[pl.ds(0, units)]
                remote(whole, whole, p_send, p_recv.at[0, 0], partner).wait_send()

    with jax.named_scope("finalwait"):
        @pl.when(at_end)
        def _():
            finals(pairs - 1).wait_recv()

        @pl.when(~at_end)
        def _():
            finals(pairs - 2).wait_recv()
    for p in range(pairs):
        for c in range(2):
            start = (2 * p + c) * shard
            result[:, start : start + shard] = final[p, c]
    with jax.named_scope("sends4"):
        @pl.when(at_end)
        def _():
            finals(1).wait_send()

        @pl.when(~at_end)
        def _():
            finals(pairs).wait_send()


def exchanged_heads(pairs, groups, tokens, ln_gain, q_w, k_w, v_w, q_gain, k_gain, out_w):
    rows, features = tokens.shape
    shard, local_width = q_w.shape
    width = local_width // pairs
    heads = width // HEAD_DIM
    part = rows // groups
    chunks = min(CHUNKS, part // 16)
    units = 2 * pairs - 2
    dma = pltpu.SemaphoreType.DMA
    in_hbm = pl.BlockSpec(memory_space=pl.ANY)
    in_vmem = pl.BlockSpec(memory_space=pltpu.VMEM)
    bf16 = jnp.bfloat16
    return pl.pallas_call(
        functools.partial(exchange_kernel, pairs, groups, chunks),
        out_shape=pltpu.VMEM((part, features), bf16),
        in_specs=[in_hbm, in_vmem, in_hbm, in_hbm, in_hbm, in_vmem, in_vmem, in_hbm],
        out_specs=in_vmem,
        scratch_shapes=[
            pltpu.VMEM((rows, features), bf16),
            pltpu.VMEM((pairs, rows, features), bf16),
            pltpu.VMEM((heads, pairs, 2, shard, 3 * HEAD_DIM), bf16),
            pltpu.VMEM((shard, local_width), bf16),
            pltpu.VMEM((2, local_width, 2 * shard), bf16),
            pltpu.VMEM((2, local_width, 2 * shard), bf16),
            pltpu.VMEM((pairs, heads, rows, HEAD_DIM), bf16),
            pltpu.VMEM((pairs, 2, 2, part, local_width), bf16),
            pltpu.VMEM((units, 2, part, shard), jnp.float32),
            pltpu.VMEM((units, 2, part, shard), bf16),
            pltpu.VMEM((units, 2, part, shard), bf16),
            pltpu.VMEM((units, 2, part, shard), bf16),
            pltpu.VMEM((pairs, 2, part, shard), bf16),
            dma((groups + 2,)), dma((2,)), dma((pairs, chunks)), dma, dma((pairs, chunks)), dma((pairs, 2)),
            dma, dma((pairs, heads, 3)), dma, dma, dma, dma((heads,)), dma, dma, dma, dma((2, 2)),
            dma((3,)), dma((6,)), dma, dma((pairs, heads)), dma((2,)), dma((pairs, pairs, heads)),
            dma, dma((units, 2)), dma, dma,
        ],
        compiler_params=pltpu.CompilerParams(
            collective_id=0, has_side_effects=True, vmem_limit_bytes=60 * 1024 * 1024
        ),
    )(
        tokens, ln_gain.reshape(1, features), q_w, k_w, v_w,
        q_gain.reshape(pairs, 1, width), k_gain.reshape(pairs, 1, width), out_w,
    )


def on_device(tokens, ln_gain, q_w, k_w, v_w, q_gain, k_gain, out_w):
    devices = lax.axis_size("dp")
    groups = lax.axis_size("mp")
    pairs = devices // 2
    fits = (
        devices % 2 == 0
        and groups == 4
        and q_w.shape[1] % (pairs * HEAD_DIM) == 0
        and q_w.shape[0] % 128 == 0
        and tokens.shape[0] == IMG_TOKENS
        and tokens.shape[0] % (16 * groups) == 0
        and pairs == 4
        and q_w.shape[1] == 2 * pairs * HEAD_DIM
    )
    if fits:
        return exchanged_heads(pairs, groups, tokens, ln_gain, q_w, k_w, v_w, q_gain, k_gain, out_w)
    return gathered_weights(tokens, ln_gain, q_w, k_w, v_w, q_gain, k_gain, out_w)


def solution(mesh):
    in_specs = (
        P("dp", None),
        P(),
        P("dp", "mp"),
        P("dp", "mp"),
        P("dp", "mp"),
        P("mp"),
        P("mp"),
        P("dp", "mp"),
    )
    out_specs = P(("dp", "mp"), None)
    return jax.shard_map(
        on_device, mesh=mesh, in_specs=in_specs, out_specs=out_specs, check_vma=False
    )
```

```python
import functools
import math

import jax
import jax.numpy as jnp
from jax import lax
from jax.experimental import pallas as pl
from jax.experimental.pallas import tpu as pltpu
from jax.sharding import PartitionSpec as P

HEAD_DIM = 128
IMG_TOKENS = 256


epsilon = 1e-06


def layer_norm(values, scale_gain):
    average = jnp.mean(values, axis=-1, keepdims=True)
    centred = values - average
    variance = jnp.mean(centred * centred, axis=-1, keepdims=True)
    return centred * lax.rsqrt(variance + epsilon) * scale_gain


def head_norm(projected, scale_gain):
    heads_count = projected.shape[1] // HEAD_DIM
    shaped = projected.reshape(projected.shape[0], heads_count, HEAD_DIM)
    normed = layer_norm(shaped, scale_gain.reshape(heads_count, HEAD_DIM))
    return normed.reshape(projected.shape).astype(jnp.bfloat16)


def attend(queries, key_rows, value_rows):
    scores = jnp.einsum(
        "bqhd,bkhd->bhqk", queries, key_rows, preferred_element_type=jnp.float32
    ) * (1.0 / math.sqrt(HEAD_DIM))
    highest = jnp.max(scores, axis=-1, keepdims=True)
    weights = jnp.exp(scores - highest)
    probs = (weights / jnp.sum(weights, axis=-1, keepdims=True)).astype(jnp.bfloat16)
    context = jnp.einsum("bhqk,bkhd->bqhd", probs, value_rows, preferred_element_type=jnp.float32)
    return context.astype(jnp.bfloat16)


def place_three(holder, pieces, offset, local_width):
    holder = lax.dynamic_update_slice(holder, pieces[0], (offset, 0))
    holder = lax.dynamic_update_slice(holder, pieces[1], (offset, local_width))
    return lax.dynamic_update_slice(holder, pieces[2], (offset, 2 * local_width))


def gathered_weights(tokens, ln_gain, q_weight, k_weight, v_weight, q_gain, k_gain, out_weight):
    normed = layer_norm(tokens.astype(jnp.float32), ln_gain).astype(jnp.bfloat16)
    token_count = normed.shape[0]
    local_width = q_weight.shape[1]
    feature_count = normed.shape[1]
    stacked = jnp.zeros((feature_count, 3 * local_width), jnp.bfloat16)
    projections = place_three(
        stacked,
        (
            lax.all_gather(q_weight, "dp", axis=0, tiled=True),
            lax.all_gather(k_weight, "dp", axis=0, tiled=True),
            lax.all_gather(v_weight, "dp", axis=0, tiled=True),
        ),
        jnp.int32(0),
        local_width,
    )
    combined = jnp.dot(normed, projections, preferred_element_type=jnp.float32)
    queries = combined[:, :local_width]
    key_rows = combined[:, local_width : 2 * local_width]
    value_cast = combined[:, 2 * local_width :].astype(jnp.bfloat16)
    query_normed = head_norm(queries, q_gain)
    key_normed = head_norm(key_rows, k_gain)
    images = token_count // IMG_TOKENS
    shaped = (images, IMG_TOKENS, local_width // HEAD_DIM, HEAD_DIM)
    context = attend(
        query_normed.reshape(shaped), key_normed.reshape(shaped), value_cast.reshape(shaped)
    )
    context = context.reshape(token_count, local_width)
    out_full = lax.all_gather(out_weight, "dp", axis=0, tiled=True)
    return lax.psum_scatter(
        lax.dot_general(
            context, out_full, (((1,), (1,)), ((), ())), preferred_element_type=jnp.float32
        ).astype(jnp.bfloat16),
        "mp",
        scatter_dimension=0,
        tiled=True,
    )


MESH = pl.DeviceIdType.MESH

CHUNKS = 4


def exchange_kernel(
    pairs, groups, chunks, tokens, ln_gain_in, q_w, k_w, v_w, q_gain_in, k_gain_in, out_w, result,
    ln_gain, head_gain, raw, normed, weights, own_rows, out_rows, end_rows, staged, context, kept, partial, arrived, summed, final,
    local_sem, token_send, token_recv, peer_send, first_recv, peer_recv,
    w_send, w_recv, own_send, own_recv, pass_send, pass_recv, out_send, out_recv, side_send, side_recv,
    end_send, end_recv, x_send, x_recv, c_send, c_recv, p_send, p_recv, f_send, f_recv,
):
    dp = lax.axis_index("dp")
    group = lax.axis_index("mp")
    pair = dp // 2
    core = dp % 2
    rows = tokens.shape[0]
    part = rows // groups
    piece_rows = part // chunks
    shard = q_w.shape[0]
    width = q_w.shape[1] // pairs
    span = 2 * shard
    heads = width // HEAD_DIM
    has_up = pair + 1 < pairs
    has_down = pair > 0
    at_end = (pair == 0) | (pair == pairs - 1)
    beside_end = (pair == 1) | (pair == pairs - 2)
    inner = jnp.where(pair < pairs // 2, pair + 1, pair - 1)
    outer = jnp.where(pair < pairs // 2, pair - 1, pair + 1)

    def at_pair(other):
        return (other * 2 + core, group)

    partner = (pair * 2 + (1 - core), group)

    def at_group(other):
        return (dp, other)

    def remote(source, target, send, recv, device):
        return pltpu.make_async_remote_copy(
            src_ref=source, dst_ref=target, send_sem=send, recv_sem=recv,
            device_id=device, device_id_type=MESH,
        )

    def quarter_of(owner):
        return pl.ds(pl.multiple_of(owner * part, part), part)

    gain_copy = pltpu.make_async_copy(ln_gain_in, ln_gain, local_sem.at[groups + 2])
    gain_copy.start()
    for at, gain in enumerate((q_gain_in, k_gain_in)):
        pltpu.make_async_copy(gain.at[pair], head_gain.at[at], local_sem.at[groups + 3]).start()
    token_quarters = []
    for j in range(groups):
        place = quarter_of((group + j) % groups)
        token_quarters.append(
            pltpu.make_async_copy(tokens.at[place, :], raw.at[place, :], local_sem.at[j])
        )
        token_quarters[j].start()

    projections = (q_w, k_w, v_w)

    def columns(other, h, t):
        start = pl.multiple_of(other * width + h * HEAD_DIM, HEAD_DIM)
        return projections[t].at[:, pl.ds(start, HEAD_DIM)]

    def slot(h, block, side, t):
        return weights.at[h, block, side, :, pl.ds(t * HEAD_DIM, HEAD_DIM)]

    greeted = pltpu.get_barrier_semaphore()
    for step in range(1, pairs):
        pl.semaphore_signal(
            greeted, inc=1, device_id=at_pair((pair + step) % pairs), device_id_type=MESH
        )
    for step in range(1, groups):
        pl.semaphore_signal(
            greeted, inc=1, device_id=at_group((group + step) % groups), device_id_type=MESH
        )
    pl.semaphore_signal(greeted, inc=1, device_id=partner, device_id_type=MESH)
    beside = group + 1 - 2 * (group % 2)
    across = (group + 2) % 4
    pl.semaphore_signal(
        greeted, inc=1,
        device_id=(pair * 2 + 1 - core, jnp.where(core == 0, beside, across)), device_id_type=MESH,
    )

    locals_ = [pltpu.make_async_copy(out_w, own_rows, local_sem.at[groups])]
    for h in range(heads):
        for t in range(3):
            locals_.append(
                pltpu.make_async_copy(
                    columns(pair, h, t), slot(h, pair, core, t), local_sem.at[groups + 1],
                )
            )
    for copy in locals_:
        copy.start()

    def normalise(first_row, count):
        @pl.loop(0, count // 16)
        def _(step):
            place = pl.ds(pl.multiple_of(first_row + step * 16, 16), 16)
            values = raw[place, :].astype(jnp.float32)
            average = jnp.mean(values, axis=-1, keepdims=True)
            centred = values - average
            variance = jnp.mean(centred * centred, axis=-1, keepdims=True)
            scaled = centred * lax.rsqrt(variance + epsilon) * ln_gain[...]
            normed[pair, place, :] = scaled.astype(jnp.bfloat16)

    gain_copy.wait()
    token_quarters[0].wait()
    normalise(group * part, piece_rows)

    def piece(block, owner, k):
        start = pl.multiple_of(owner * part + k * piece_rows, 16)
        return normed.at[block, pl.ds(start, piece_rows), :]

    def z_hop(block, k, up):
        there = piece(block, group, k)
        return remote(
            there, there, token_send.at[0 if up else 1], token_recv.at[block, k],
            at_pair(pair + 1 if up else pair - 1),
        )

    first = jnp.where(core == 0, beside, across)
    second = jnp.where(core == 0, across, beside)
    opposite = 3 - group

    def peer_copy(block, owner, place, k, other):
        there = piece(block, owner, k)
        return remote(
            there, there, peer_send, first_recv.at[block, k] if place == 0 else peer_recv.at[block, place - 1], at_group(other)
        )

    def weight_to(other, h, t):
        return remote(
            columns(other, h, t), slot(h, pair, core, t),
            w_send, w_recv.at[pair, h, t], at_pair(other),
        )

    def send_weights(up, plan):
        for h, distance in plan:
            other = pair + distance if up else pair - distance

            @pl.when(other < pairs if up else other >= 0)
            def _():
                for t in range(3):
                    weight_to(other, h, t).start()

    def own_weight(h, t):
        return remote(
            columns(pair, h, t), slot(h, pair, core, t), own_send, own_recv, partner
        )

    def side_of(rows_of, way, side, k=None):
        lanes = pl.ds(pl.multiple_of(side * shard, 128), shard)
        if k is None:
            return rows_of.at[way, :, lanes]
        depth = pairs * width // 2
        return rows_of.at[way, pl.ds(k * depth, depth), lanes]

    def transpose_rows():
        @pl.loop(0, pairs * width // 128)
        def _(k):
            place = pl.ds(pl.multiple_of(k * 128, 128), 128)
            lanes = pl.ds(pl.multiple_of(core * shard, 128), shard)
            out_rows[0, place, lanes] = jnp.transpose(own_rows[:, place])

    def out_over(side):
        there = side_of(out_rows, 0, side)
        return remote(there, there, out_send, out_recv, partner)

    sides = ((pair * 2, beside), (pair * 2 + 1, across))

    def rows_aside(side, k, device):
        return remote(
            side_of(out_rows, 0, side, k), side_of(out_rows, 1, side, k),
            side_send, side_recv, device,
        )

    with jax.named_scope("greet"):
        pl.semaphore_wait(greeted, pairs + groups)

    @pl.loop(0, chunks)
    def _(k):
        @pl.when(k > 0)
        def _():
            normalise(group * part + k * piece_rows, piece_rows)

        @pl.when(has_up)
        def _():
            z_hop(pair, k, True).start()

        @pl.when(has_down)
        def _():
            z_hop(pair, k, False).start()

    def end_over(side):
        return remote(
            side_of(out_rows, 0, side), side_of(end_rows, 0, side),
            end_send.at[0], end_recv.at[0], at_pair(inner),
        )

    def end_pass(side):
        there = side_of(end_rows, 0, side)
        return remote(there, there, end_send.at[1], end_recv.at[1], partner)

    def end_part(side, k, device):
        return remote(
            side_of(end_rows, 0, side, k), side_of(end_rows, 1, side, k),
            end_send.at[2], end_recv.at[2], device,
        )

    for at, up in ((0, True), (pairs - 1, False)):
        @pl.when(pair == at)
        def _():
            send_weights(up, [(h, 1) for h in range(heads)])
            send_weights(up, [(0, distance) for distance in range(2, pairs)])

    for h in range(heads):
        for t in range(3):
            own_weight(h, t).start()
    for j in range(1, groups):
        token_quarters[j].wait()
    pltpu.make_async_copy(head_gain, head_gain, local_sem.at[groups + 3]).wait()

    def relay(block, k, up):
        with jax.named_scope("relaywait"):
            z_hop(block, k, up).wait_recv()

        @pl.when(has_up if up else has_down)
        def _():
            z_hop(block, k, up).start()

        peer_copy(block, group, 0, k, first).start()
        peer_copy(block, group, 1, k, second).start()

    others = rows - part
    for distance in range(1, pairs):
        @pl.loop(0, chunks)
        def _(k):
            @pl.when(pair - distance >= 0)
            def _():
                relay(pair - distance, k, True)

            @pl.when(pair + distance < pairs)
            def _():
                relay(pair + distance, k, False)

            if distance == 1:
                for j in range(1, groups):
                    normalise(((group + j) % groups) * part + k * piece_rows, piece_rows)

        if distance == 1:
            with jax.named_scope("transpose"):
                locals_[0].wait()
                transpose_rows()
            out_over(core).start()
            for at, up in ((0, True), (pairs - 1, False)):
                @pl.when(pair == at)
                def _():
                    end_over(core).start()
                    send_weights(up, [(h, d) for h in range(1, heads) for d in range(pairs - 1, 1, -1)])

        @pl.when(has_up & (pair == distance))
        def _():
            send_weights(True, [(h, d) for h in range(heads) for d in range(1, pairs - 1)])

        @pl.when(has_down & (pair == pairs - 1 - distance))
        def _():
            send_weights(False, [(h, d) for h in range(heads) for d in range(1, pairs - 1)])

    def cross_tokens(block, k):
        with jax.named_scope("crosswait"):
            peer_copy(block, first, 0, k, first).wait_recv()
        peer_copy(block, first, 2, k, second).start()

    for distance in range(1, pairs):
        @pl.loop(0, chunks)
        def _(k):
            @pl.when(pair - distance >= 0)
            def _():
                cross_tokens(pair - distance, k)

            @pl.when(pair + distance < pairs)
            def _():
                cross_tokens(pair + distance, k)


    def pass_weights(h):
        for distance in range(1, pairs):
            for up in (True, False):
                other = pair - distance if up else pair + distance

                @pl.when(other >= 0 if up else other < pairs)
                def _():
                    for t in range(3):
                        there = slot(h, other, core, t)
                        with jax.named_scope("wwait"):
                            remote(
                                there, there, w_send, w_recv.at[other, h, t], partner
                            ).wait_recv()
                        remote(there, there, pass_send, pass_recv.at[h], partner).start()

    def all_passed(h):
        there = weights.at[h, pl.ds(0, pairs - 1), 1 - core]
        return remote(there, there, pass_send, pass_recv.at[h], partner)

    def all_own():
        there = weights.at[:, pair, 1 - core]
        return remote(there, there, own_send, own_recv, partner)

    pass_weights(0)
    there = weights.at[:, pair, core]
    pltpu.make_async_copy(there, there, local_sem.at[groups + 1]).wait()
    all_own().wait_recv()
    for distance in range(1, pairs):
        for below in (True, False):
            block = pair - distance if below else pair + distance

            @pl.when(block >= 0 if below else block < pairs)
            def _():
                with jax.named_scope("tokwait"):
                    for place, owner in ((1, second), (2, opposite)):
                        there = normed.at[block, quarter_of(owner), :]
                        remote(
                            there, there, peer_send, peer_recv.at[block, place - 1], partner
                        ).wait_recv()

    for to in range(2):
        rows_aside(core, 0, sides[to]).start()

    def head_layer_norm(values, scale_gain):
        average = jnp.mean(values, axis=-1, keepdims=True)
        centred = values - average
        variance = jnp.mean(centred * centred, axis=-1, keepdims=True)
        return (centred * lax.rsqrt(variance + epsilon) * scale_gain).astype(jnp.bfloat16)

    def head_place(block, h):
        return pl.ds(pl.multiple_of(block * width + h * HEAD_DIM, HEAD_DIM), HEAD_DIM)

    def context_hop(block, image, h, up):
        there = context.at[image, :, :, :, head_place(block, h)]
        return remote(
            there, there,
            c_send.at[0 if up else 1], c_recv.at[block, image, h],
            at_pair(pair + 1 if up else pair - 1),
        )

    def inside(image):
        return (image > 0) & (image < pairs - 1)

    def outside(image):
        return (image == 0) | (image == pairs - 1)

    def onward(image, up):
        if up:
            return has_up & ~((pair == pairs - 2) & inside(image))
        return has_down & ~((pair == 1) & inside(image))

    def awaited(block, image, up):
        if up:
            return (block >= 0) & ~((pair == pairs - 1) & inside(image))
        return (block < pairs) & ~((pair == 0) & inside(image))

    def send_context(image, h, across_middle, to_end):
        for up in (True, False):
            crossing = pair < pairs // 2 if up else pair >= pairs // 2
            wanted = (crossing & across_middle) | (~crossing & to_end)

            @pl.when(onward(image, up) & wanted)
            def _():
                context_hop(pair, image, h, up).start()

    def cross_context(image, h):
        for up in (True, False):
            @pl.when((pair == 1) if up else (pair == pairs - 2))
            def _():
                with jax.named_scope("crossctx"):
                    context_hop(outer, image, h, up).wait_recv()
                context_hop(outer, image, h, up).start()

    def pass_context(image, h, distance):
        for up in (True, False):
            block = pair - distance if up else pair + distance

            @pl.when(awaited(block, image, up) & ~(beside_end & (block == outer)))
            def _():
                with jax.named_scope("ctxwait%d" % distance):
                    context_hop(block, image, h, up).wait_recv()

                @pl.when(onward(image, up))
                def _():
                    context_hop(block, image, h, up).start()

    def half_over(image, h, at, owner):
        return remote(
            staged.at[image, h, quarter_of(owner), :],
            context.at[image, 1, at, :, head_place(pair, h)],
            x_send, x_recv.at[image, h], at_group(first),
        )

    def half_in(image, h):
        there = context.at[image, 1, :, :, head_place(pair, h)]
        with jax.named_scope("halfin"):
            remote(there, there, x_send, x_recv.at[image, h], partner).wait_recv()

    def attend_head(image, h):
        lanes = slice(h * HEAD_DIM, (h + 1) * HEAD_DIM)
        with jax.named_scope("attend"):
            total = jnp.dot(
                normed[image], weights[h].reshape(pairs * span, 3 * HEAD_DIM),
                preferred_element_type=jnp.float32,
            )
            queries = head_layer_norm(total[:, :HEAD_DIM], head_gain[0, :, lanes])
            key_rows = head_layer_norm(total[:, HEAD_DIM : 2 * HEAD_DIM], head_gain[1, :, lanes])
            value_rows = total[:, 2 * HEAD_DIM :].astype(jnp.bfloat16)
            scores = lax.dot_general(
                queries, key_rows, (((1,), (1,)), ((), ())), preferred_element_type=jnp.float32
            ) * (1.0 / math.sqrt(HEAD_DIM))
            highest = jnp.max(scores, axis=-1, keepdims=True)
            spread = jnp.exp(scores - highest)
            probs = (spread / jnp.sum(spread, axis=-1, keepdims=True)).astype(jnp.bfloat16)
            mixed = jnp.dot(probs, value_rows, preferred_element_type=jnp.float32)
            staged[image, h] = mixed.astype(jnp.bfloat16)

        for at, owner in enumerate((first, opposite)):
            half_over(image, h, at, owner).start()
        for at, owner in enumerate((group, second)):
            context[image, 0, at, :, head_place(pair, h)] = staged[image, h, quarter_of(owner), :]

    lower = pair < pairs // 2
    homely = jnp.where(lower, 1, pairs - 2)
    foreign = pairs - 1 - homely

    def image_at(step):
        if isinstance(step, int):
            return (0, pairs - 1, homely, foreign)[step]
        return jnp.where(step < 2, step * (pairs - 1), jnp.where(step == 2, homely, foreign))

    def projected_at(step):
        if isinstance(step, int):
            return (0, pairs - 1, foreign, homely)[step]
        return jnp.where(step < 2, step * (pairs - 1), jnp.where(step == 2, foreign, homely))

    def all_weights(h):
        with jax.named_scope("passedwait"):
            all_passed(h).wait_recv()

    all_weights(0)

    @pl.loop(0, pairs)
    def _(step):
        attend_head(image_at(step), 0)

    for to in range(2):
        rows_aside(core, 1, sides[to]).start()

    with jax.named_scope("sends"):
        for at in range(pairs):
            @pl.when(pair == at)
            def _():
                for way, blocks in ((0, at + 1 if at + 1 < pairs else 0), (1, pairs - at if at > 0 else 0)):
                    if blocks > 0:
                        there = normed.at[pl.ds(0, blocks), pl.ds(0, part), :]
                        remote(
                            there, there, token_send.at[way], token_recv.at[0, 0], partner
                        ).wait_send()
        there = normed.at[pl.ds(0, pairs - 1), pl.ds(0, 3 * part), :]
        remote(there, there, peer_send, peer_recv.at[0, 0], partner).wait_send()
        all_own().wait_send()
        out_over(1 - core).wait_recv()
        out_over(core).wait_send()


    def end_aside(k):
        for to in range(2):
            end_part(core, k, sides[to]).start()

    @pl.when(beside_end)
    def _():
        end_over(core).wait_recv()
        end_pass(core).start()
        end_aside(0)

    def partial_to(unit, c):
        return remote(
            partial.at[unit, c], arrived.at[unit, c], p_send, p_recv.at[unit, c], at_group(second)
        )

    def final_to(unit, c, image, span_of):
        return remote(summed.at[unit, c], final.at[span_of, c], f_send, f_recv, at_pair(image))

    def finals(count):
        there = final.at[pl.ds(0, count)]
        return remote(there, there, f_send, f_recv, partner)

    def project(unit, image, rows_of):
        with jax.named_scope("outproj"):
            total = None
            for j in range(2):
                product = lax.dot_general(
                    context[image, j].reshape(2 * part, pairs * width), rows_of[j],
                    (((1,), (0,)), ((), ())), preferred_element_type=jnp.float32,
                )
                total = product if total is None else total + product
            for c in range(2):
                kept[unit, c] = total[:part, c * shard : (c + 1) * shard]
                partial[unit, c] = total[part:, c * shard : (c + 1) * shard].astype(jnp.bfloat16)
        for c in range(2):
            partial_to(unit, c).start()

    def add_up(unit, c, image, span_of):
        with jax.named_scope("partwait"):
            partial_to(unit, c).wait_recv()
        total = (kept[unit, c] + arrived[unit, c].astype(jnp.float32)).astype(jnp.bfloat16)

        @pl.when(image != pair)
        def _():
            summed[unit, c] = total
            final_to(unit, c, image, span_of).start()

        @pl.when(image == pair)
        def _():
            final[span_of, c] = total

    def own_unit(image):
        return ~at_end | outside(image)

    def extra_unit(image):
        return beside_end & inside(image)

    def finish(image, extra):
        @pl.when(extra_unit(image) if extra else own_unit(image))
        def _():
            for c in range(2):
                add_up(pairs + image - 1 if extra else image, c, image, outer if extra else pair)

    for step in range(pairs):
        half_in(image_at(step), 0)
        send_context(image_at(step), 0, True, True)
    pass_weights(heads - 1)
    all_weights(heads - 1)

    def pass_most(image):
        for h in range(heads):
            pass_context(image, h, 1)
        pass_context(image, 0, 2)

    def pass_rest(image):
        pass_context(image, 1, 2)
        for h in range(heads):
            pass_context(image, h, 3)

    lag = 4

    @pl.loop(0, pairs + lag)
    def _(step):
        @pl.when(step < pairs)
        def _():
            attend_head(image_at(step), heads - 1)

        @pl.when(step == 0)
        def _():
            cross_context(image_at(0), 0)

        @pl.when((step > 0) & (step <= pairs))
        def _():
            image = image_at(step - 1)
            half_in(image, heads - 1)
            send_context(image, heads - 1, at_end | (step < 3), True)

            @pl.when(step < pairs)
            def _():
                cross_context(image_at(step), 0)

            for at, (turn, h, distance) in enumerate(((0, 0, 1), (1, 0, 1), (0, 0, 2))):
                @pl.when((step == at + 1) & beside_end)
                def _():
                    pass_context(image_at(turn), h, distance)

            @pl.when((step == pairs) & beside_end)
            def _():
                end_aside(1)

        @pl.when(step >= lag)
        def _():
            image = projected_at(step - lag)

            @pl.when(step == lag)
            def _():
                cross_context(image_at(0), heads - 1)

            @pl.when(step == lag + 3)
            def _():
                for early in range(2):
                    finish(projected_at(early), False)

            @pl.when(at_end | (step > lag + 1))
            def _():
                pass_most(image)

            @pl.when((step == lag) & beside_end)
            def _():
                pass_context(image_at(0), 1, 1)
                cross_context(image_at(1), heads - 1)
                send_context(image_at(2), heads - 1, True, False)
                pass_context(image_at(1), 1, 1)
                pass_context(image_at(1), 0, 2)
                cross_context(image_at(2), heads - 1)
                send_context(image_at(3), heads - 1, True, False)

            @pl.when(step == lag + 1)
            def _():
                cross_context(image_at(pairs - 1), heads - 1)

            pass_rest(image)

            @pl.when(own_unit(image))
            def _():
                @pl.when(step == lag)
                def _():
                    whole = out_rows.at[1]
                    remote(whole, whole, side_send, side_recv, partner).wait_recv()

                project(image, image, out_rows)

            @pl.when(extra_unit(image))
            def _():
                @pl.when(step == lag + 2)
                def _():
                    end_pass(1 - core).wait_recv()
                    with jax.named_scope("endrows"):
                        whole = end_rows.at[1]
                        remote(whole, whole, end_send.at[2], end_recv.at[2], partner).wait_recv()

                project(pairs + image - 1, image, end_rows)

    for turn in (2, 3):
        for extra in (False, True):
            finish(projected_at(turn), extra)

    with jax.named_scope("sends2"):
        others = weights.at[:, pl.ds(0, pairs - 1), core]
        remote(others, others, pass_send, pass_recv.at[0], partner).wait_send()
        remote(others, others, w_send, w_recv.at[0, 0, 0], partner).wait_send()

        @pl.when(at_end)
        def _():
            end_over(core).wait_send()

        @pl.when(beside_end)
        def _():
            end_pass(core).wait_send()
            both = end_rows.at[0]
            remote(both, both, end_send.at[2], end_recv.at[2], partner).wait_send()

        def sent(way, images, blocks):
            there = context.at[pl.ds(0, images), :, :, :, pl.ds(0, blocks * width)]
            return remote(there, there, c_send.at[way], c_recv.at[0, 0, 0], partner)

        for at, counts in (
            (0, ((0, pairs, 1),)),
            (1, ((0, pairs, 2), (1, 2, pairs - 1))),
            (pairs - 2, ((0, 2, pairs - 1), (1, pairs, 2))),
            (pairs - 1, ((1, pairs, 1),)),
        ):
            @pl.when(pair == at)
            def _():
                for way, images, blocks in counts:
                    sent(way, images, blocks).wait_send()

    with jax.named_scope("sends3"):
        both = out_rows.at[0]
        remote(both, both, side_send, side_recv, partner).wait_send()
        half = staged.at[:, :, pl.ds(0, 2 * part), :]
        remote(half, half, x_send, x_recv.at[0, 0], partner).wait_send()
        for few, units in ((at_end, 2), (beside_end, 2 * pairs - 2)):
            @pl.when(few)
            def _():
                whole = partial.at[pl.ds(0, units)]
                remote(whole, whole, p_send, p_recv.at[0, 0], partner).wait_send()

    with jax.named_scope("finalwait"):
        @pl.when(at_end)
        def _():
            finals(pairs - 1).wait_recv()

        @pl.when(~at_end)
        def _():
            finals(pairs - 2).wait_recv()
    for p in range(pairs):
        for c in range(2):
            start = (2 * p + c) * shard
            result[:, start : start + shard] = final[p, c]
    with jax.named_scope("sends4"):
        @pl.when(at_end)
        def _():
            finals(1).wait_send()

        @pl.when(~at_end)
        def _():
            finals(pairs).wait_send()


def exchanged_heads(pairs, groups, tokens, ln_gain, q_w, k_w, v_w, q_gain, k_gain, out_w):
    rows, features = tokens.shape
    shard, local_width = q_w.shape
    width = local_width // pairs
    heads = width // HEAD_DIM
    part = rows // groups
    chunks = min(CHUNKS, part // 16)
    units = 2 * pairs - 2
    dma = pltpu.SemaphoreType.DMA
    in_hbm = pl.BlockSpec(memory_space=pl.ANY)
    in_vmem = pl.BlockSpec(memory_space=pltpu.VMEM)
    bf16 = jnp.bfloat16
    return pl.pallas_call(
        functools.partial(exchange_kernel, pairs, groups, chunks),
        out_shape=pltpu.VMEM((part, features), bf16),
        in_specs=[in_hbm] * 8,
        out_specs=in_vmem,
        scratch_shapes=[
            pltpu.VMEM((1, features), jnp.float32),
            pltpu.VMEM((2, 1, width), jnp.float32),
            pltpu.VMEM((rows, features), bf16),
            pltpu.VMEM((pairs, rows, features), bf16),
            pltpu.VMEM((heads, pairs, 2, shard, 3 * HEAD_DIM), bf16),
            pltpu.VMEM((shard, local_width), bf16),
            pltpu.VMEM((2, local_width, 2 * shard), bf16),
            pltpu.VMEM((2, local_width, 2 * shard), bf16),
            pltpu.VMEM((pairs, heads, rows, HEAD_DIM), bf16),
            pltpu.VMEM((pairs, 2, 2, part, local_width), bf16),
            pltpu.VMEM((units, 2, part, shard), jnp.float32),
            pltpu.VMEM((units, 2, part, shard), bf16),
            pltpu.VMEM((units, 2, part, shard), bf16),
            pltpu.VMEM((units, 2, part, shard), bf16),
            pltpu.VMEM((pairs, 2, part, shard), bf16),
            dma((groups + 4,)), dma((2,)), dma((pairs, chunks)), dma, dma((pairs, chunks)), dma((pairs, 2)),
            dma, dma((pairs, heads, 3)), dma, dma, dma, dma((heads,)), dma, dma, dma, dma,
            dma((3,)), dma((3,)), dma, dma((pairs, heads)), dma((2,)), dma((pairs, pairs, heads)),
            dma, dma((units, 2)), dma, dma,
        ],
        compiler_params=pltpu.CompilerParams(
            collective_id=0, has_side_effects=True, vmem_limit_bytes=60 * 1024 * 1024
        ),
    )(
        tokens, ln_gain.reshape(1, features), q_w, k_w, v_w,
        q_gain.reshape(pairs, 1, width), k_gain.reshape(pairs, 1, width), out_w,
    )


def on_device(tokens, ln_gain, q_w, k_w, v_w, q_gain, k_gain, out_w):
    devices = lax.axis_size("dp")
    groups = lax.axis_size("mp")
    pairs = devices // 2
    fits = (
        devices % 2 == 0
        and groups == 4
        and q_w.shape[1] % (pairs * HEAD_DIM) == 0
        and q_w.shape[0] % 128 == 0
        and tokens.shape[0] == IMG_TOKENS
        and tokens.shape[0] % (16 * groups) == 0
        and pairs == 4
        and q_w.shape[1] == 2 * pairs * HEAD_DIM
    )
    if fits:
        return exchanged_heads(pairs, groups, tokens, ln_gain, q_w, k_w, v_w, q_gain, k_gain, out_w)
    return gathered_weights(tokens, ln_gain, q_w, k_w, v_w, q_gain, k_gain, out_w)


def solution(mesh):
    in_specs = (
        P("dp", None),
        P(),
        P("dp", "mp"),
        P("dp", "mp"),
        P("dp", "mp"),
        P("mp"),
        P("mp"),
        P("dp", "mp"),
    )
    out_specs = P(("dp", "mp"), None)
    return jax.shard_map(
        on_device, mesh=mesh, in_specs=in_specs, out_specs=out_specs, check_vma=False
    )
```

```python
import functools
import math

import jax
import jax.numpy as jnp
from jax import lax
from jax.experimental import pallas as pl
from jax.experimental.pallas import tpu as pltpu
from jax.sharding import PartitionSpec as P

HEAD_DIM = 128
IMG_TOKENS = 256


epsilon = 1e-06


def layer_norm(values, scale_gain):
    average = jnp.mean(values, axis=-1, keepdims=True)
    centred = values - average
    variance = jnp.mean(centred * centred, axis=-1, keepdims=True)
    return centred * lax.rsqrt(variance + epsilon) * scale_gain


def head_norm(projected, scale_gain):
    heads_count = projected.shape[1] // HEAD_DIM
    shaped = projected.reshape(projected.shape[0], heads_count, HEAD_DIM)
    normed = layer_norm(shaped, scale_gain.reshape(heads_count, HEAD_DIM))
    return normed.reshape(projected.shape).astype(jnp.bfloat16)


def attend(queries, key_rows, value_rows):
    scores = jnp.einsum(
        "bqhd,bkhd->bhqk", queries, key_rows, preferred_element_type=jnp.float32
    ) * (1.0 / math.sqrt(HEAD_DIM))
    highest = jnp.max(scores, axis=-1, keepdims=True)
    weights = jnp.exp(scores - highest)
    probs = (weights / jnp.sum(weights, axis=-1, keepdims=True)).astype(jnp.bfloat16)
    context = jnp.einsum("bhqk,bkhd->bqhd", probs, value_rows, preferred_element_type=jnp.float32)
    return context.astype(jnp.bfloat16)


def place_three(holder, pieces, offset, local_width):
    holder = lax.dynamic_update_slice(holder, pieces[0], (offset, 0))
    holder = lax.dynamic_update_slice(holder, pieces[1], (offset, local_width))
    return lax.dynamic_update_slice(holder, pieces[2], (offset, 2 * local_width))


def gathered_weights(tokens, ln_gain, q_weight, k_weight, v_weight, q_gain, k_gain, out_weight):
    normed = layer_norm(tokens.astype(jnp.float32), ln_gain).astype(jnp.bfloat16)
    token_count = normed.shape[0]
    local_width = q_weight.shape[1]
    feature_count = normed.shape[1]
    stacked = jnp.zeros((feature_count, 3 * local_width), jnp.bfloat16)
    projections = place_three(
        stacked,
        (
            lax.all_gather(q_weight, "dp", axis=0, tiled=True),
            lax.all_gather(k_weight, "dp", axis=0, tiled=True),
            lax.all_gather(v_weight, "dp", axis=0, tiled=True),
        ),
        jnp.int32(0),
        local_width,
    )
    combined = jnp.dot(normed, projections, preferred_element_type=jnp.float32)
    queries = combined[:, :local_width]
    key_rows = combined[:, local_width : 2 * local_width]
    value_cast = combined[:, 2 * local_width :].astype(jnp.bfloat16)
    query_normed = head_norm(queries, q_gain)
    key_normed = head_norm(key_rows, k_gain)
    images = token_count // IMG_TOKENS
    shaped = (images, IMG_TOKENS, local_width // HEAD_DIM, HEAD_DIM)
    context = attend(
        query_normed.reshape(shaped), key_normed.reshape(shaped), value_cast.reshape(shaped)
    )
    context = context.reshape(token_count, local_width)
    out_full = lax.all_gather(out_weight, "dp", axis=0, tiled=True)
    return lax.psum_scatter(
        lax.dot_general(
            context, out_full, (((1,), (1,)), ((), ())), preferred_element_type=jnp.float32
        ).astype(jnp.bfloat16),
        "mp",
        scatter_dimension=0,
        tiled=True,
    )


MESH = pl.DeviceIdType.MESH

CHUNKS = 4


def exchange_kernel(
    pairs, groups, chunks, tokens, ln_gain_in, q_w, k_w, v_w, q_gain_in, k_gain_in, out_w, result,
    ln_gain, head_gain, raw, normed, weights, own_rows, out_rows, end_rows, staged, context, kept, partial, arrived, summed,
    local_sem, token_send, token_recv, peer_send, first_recv, peer_recv,
    w_send, w_recv, own_send, own_recv, pass_send, pass_recv, out_send, out_recv, side_send, side_recv,
    end_send, end_recv, x_send, x_recv, c_send, c_recv, p_send, p_recv, f_send, f_recv,
):
    dp = lax.axis_index("dp")
    group = lax.axis_index("mp")
    pair = dp // 2
    core = dp % 2
    rows = tokens.shape[0]
    part = rows // groups
    piece_rows = part // chunks
    shard = q_w.shape[0]
    width = q_w.shape[1] // pairs
    span = 2 * shard
    heads = width // HEAD_DIM
    has_up = pair + 1 < pairs
    has_down = pair > 0
    at_end = (pair == 0) | (pair == pairs - 1)
    beside_end = (pair == 1) | (pair == pairs - 2)
    inner = jnp.where(pair < pairs // 2, pair + 1, pair - 1)
    outer = jnp.where(pair < pairs // 2, pair - 1, pair + 1)

    def at_pair(other):
        return (other * 2 + core, group)

    partner = (pair * 2 + (1 - core), group)

    def at_group(other):
        return (dp, other)

    def remote(source, target, send, recv, device):
        return pltpu.make_async_remote_copy(
            src_ref=source, dst_ref=target, send_sem=send, recv_sem=recv,
            device_id=device, device_id_type=MESH,
        )

    def quarter_of(owner):
        return pl.ds(pl.multiple_of(owner * part, part), part)

    greeted = pltpu.get_barrier_semaphore()
    for step in range(1, pairs):
        pl.semaphore_signal(
            greeted, inc=1, device_id=at_pair((pair + step) % pairs), device_id_type=MESH
        )
    for step in range(1, groups):
        pl.semaphore_signal(
            greeted, inc=1, device_id=at_group((group + step) % groups), device_id_type=MESH
        )
    pl.semaphore_signal(greeted, inc=1, device_id=partner, device_id_type=MESH)
    beside = group + 1 - 2 * (group % 2)
    across = (group + 2) % 4
    pl.semaphore_signal(
        greeted, inc=1,
        device_id=(pair * 2 + 1 - core, jnp.where(core == 0, beside, across)), device_id_type=MESH,
    )

    gain_copy = pltpu.make_async_copy(ln_gain_in, ln_gain, local_sem.at[groups + 2])
    gain_copy.start()
    for at, gain in enumerate((q_gain_in, k_gain_in)):
        pltpu.make_async_copy(gain.at[pair], head_gain.at[at], local_sem.at[groups + 3]).start()
    token_quarters = []
    for j in range(groups):
        place = quarter_of((group + j) % groups)
        token_quarters.append(
            pltpu.make_async_copy(tokens.at[place, :], raw.at[place, :], local_sem.at[j])
        )
        token_quarters[j].start()

    projections = (q_w, k_w, v_w)

    def columns(other, h, t):
        start = pl.multiple_of(other * width + h * HEAD_DIM, HEAD_DIM)
        return projections[t].at[:, pl.ds(start, HEAD_DIM)]

    def slot(h, block, side, t):
        return weights.at[h, block, side, :, pl.ds(t * HEAD_DIM, HEAD_DIM)]

    locals_ = [pltpu.make_async_copy(out_w, own_rows, local_sem.at[groups])]
    for h in range(heads):
        for t in range(3):
            locals_.append(
                pltpu.make_async_copy(
                    columns(pair, h, t), slot(h, pair, core, t), local_sem.at[groups + 1],
                )
            )
    for copy in locals_:
        copy.start()

    def normalise(first_row, count):
        @pl.loop(0, count // 16)
        def _(step):
            place = pl.ds(pl.multiple_of(first_row + step * 16, 16), 16)
            values = raw[place, :].astype(jnp.float32)
            average = jnp.mean(values, axis=-1, keepdims=True)
            centred = values - average
            variance = jnp.mean(centred * centred, axis=-1, keepdims=True)
            scaled = centred * lax.rsqrt(variance + epsilon) * ln_gain[...]
            normed[pair, place, :] = scaled.astype(jnp.bfloat16)

    gain_copy.wait()
    token_quarters[0].wait()
    normalise(group * part, piece_rows)

    def piece(block, owner, k):
        start = pl.multiple_of(owner * part + k * piece_rows, 16)
        return normed.at[block, pl.ds(start, piece_rows), :]

    def z_hop(block, k, up):
        there = piece(block, group, k)
        return remote(
            there, there, token_send.at[0 if up else 1], token_recv.at[block, k],
            at_pair(pair + 1 if up else pair - 1),
        )

    first = jnp.where(core == 0, beside, across)
    second = jnp.where(core == 0, across, beside)
    opposite = 3 - group

    def peer_copy(block, owner, place, k, other):
        there = piece(block, owner, k)
        return remote(
            there, there, peer_send, first_recv.at[block, k] if place == 0 else peer_recv.at[block, place - 1], at_group(other)
        )

    def weight_to(other, h, t):
        return remote(
            columns(other, h, t), slot(h, pair, core, t),
            w_send, w_recv.at[pair, t if h > 0 else 3], at_pair(other),
        )

    def send_weights(up, plan):
        for h, distance in plan:
            other = pair + distance if up else pair - distance

            @pl.when(other < pairs if up else other >= 0)
            def _():
                for t in range(3):
                    weight_to(other, h, t).start()

    def own_weight(h, t):
        return remote(
            columns(pair, h, t), slot(h, pair, core, t), own_send, own_recv, partner
        )

    def side_of(rows_of, way, side, k=None):
        lanes = pl.ds(pl.multiple_of(side * shard, 128), shard)
        if k is None:
            return rows_of.at[way, :, lanes]
        depth = pairs * width // 2
        return rows_of.at[way, pl.ds(k * depth, depth), lanes]

    def transpose_rows():
        @pl.loop(0, pairs * width // 128)
        def _(k):
            place = pl.ds(pl.multiple_of(k * 128, 128), 128)
            lanes = pl.ds(pl.multiple_of(core * shard, 128), shard)
            out_rows[0, place, lanes] = jnp.transpose(own_rows[:, place])

    def out_over(side):
        there = side_of(out_rows, 0, side)
        return remote(there, there, out_send, out_recv, partner)

    sides = ((pair * 2, beside), (pair * 2 + 1, across))

    def rows_aside(side, k, device):
        return remote(
            side_of(out_rows, 0, side, k), side_of(out_rows, 1, side, k),
            side_send, side_recv, device,
        )

    with jax.named_scope("greet"):
        pl.semaphore_wait(greeted, pairs + groups)

    @pl.loop(0, chunks)
    def _(k):
        @pl.when(k > 0)
        def _():
            normalise(group * part + k * piece_rows, piece_rows)

        @pl.when(has_up)
        def _():
            z_hop(pair, k, True).start()

        @pl.when(has_down)
        def _():
            z_hop(pair, k, False).start()

    def end_over(side):
        return remote(
            side_of(out_rows, 0, side), side_of(end_rows, 0, side),
            end_send.at[0], end_recv.at[0], at_pair(inner),
        )

    def end_pass(side):
        there = side_of(end_rows, 0, side)
        return remote(there, there, end_send.at[1], end_recv.at[1], partner)

    def end_part(side, k, device):
        return remote(
            side_of(end_rows, 0, side, k), side_of(end_rows, 1, side, k),
            end_send.at[2], end_recv.at[2], device,
        )

    for at, up in ((0, True), (pairs - 1, False)):
        @pl.when(pair == at)
        def _():
            send_weights(up, [(h, 1) for h in range(heads)])
            send_weights(up, [(0, distance) for distance in range(2, pairs)])

    for h in range(heads):
        for t in range(3):
            own_weight(h, t).start()
    for j in range(1, groups):
        token_quarters[j].wait()
    pltpu.make_async_copy(head_gain, head_gain, local_sem.at[groups + 3]).wait()

    def relay(block, k, up):
        with jax.named_scope("relaywait"):
            z_hop(block, k, up).wait_recv()

        @pl.when(has_up if up else has_down)
        def _():
            z_hop(block, k, up).start()

        peer_copy(block, group, 0, k, first).start()
        peer_copy(block, group, 1, k, second).start()

    others = rows - part
    for distance in range(1, pairs):
        @pl.loop(0, chunks)
        def _(k):
            @pl.when(pair - distance >= 0)
            def _():
                relay(pair - distance, k, True)

            @pl.when(pair + distance < pairs)
            def _():
                relay(pair + distance, k, False)

            if distance == 1:
                for j in range(1, groups):
                    normalise(((group + j) % groups) * part + k * piece_rows, piece_rows)

        if distance == 1:
            with jax.named_scope("transpose"):
                locals_[0].wait()
                transpose_rows()
            out_over(core).start()
            for at, up in ((0, True), (pairs - 1, False)):
                @pl.when(pair == at)
                def _():
                    end_over(core).start()
                    send_weights(up, [(h, d) for h in range(1, heads) for d in range(pairs - 1, 1, -1)])

        @pl.when(has_up & (pair == distance))
        def _():
            send_weights(True, [(h, d) for h in range(heads) for d in range(1, pairs - 1)])

        @pl.when(has_down & (pair == pairs - 1 - distance))
        def _():
            send_weights(False, [(h, d) for h in range(heads) for d in range(1, pairs - 1)])

    def cross_tokens(block, k):
        with jax.named_scope("crosswait"):
            peer_copy(block, first, 0, k, first).wait_recv()
        peer_copy(block, first, 2, k, second).start()

    for distance in range(1, pairs):
        @pl.loop(0, chunks)
        def _(k):
            @pl.when(pair - distance >= 0)
            def _():
                cross_tokens(pair - distance, k)

            @pl.when(pair + distance < pairs)
            def _():
                cross_tokens(pair + distance, k)


    def pass_weights(h):
        for distance in range(1, pairs):
            for up in (True, False):
                other = pair - distance if up else pair + distance

                @pl.when(other >= 0 if up else other < pairs)
                def _():
                    pieces = [(slot(h, other, core, t), t) for t in range(3)]
                    if h == 0:
                        pieces = [(weights.at[h, other, core], 3)]
                    for there, at in pieces:
                        with jax.named_scope("wwait"):
                            remote(there, there, w_send, w_recv.at[other, at], partner).wait_recv()
                        remote(there, there, pass_send, pass_recv.at[h], partner).start()

    def all_passed(h):
        there = weights.at[h, pl.ds(0, pairs - 1), 1 - core]
        return remote(there, there, pass_send, pass_recv.at[h], partner)

    def all_own():
        there = weights.at[:, pair, 1 - core]
        return remote(there, there, own_send, own_recv, partner)

    pass_weights(0)
    there = weights.at[:, pair, core]
    pltpu.make_async_copy(there, there, local_sem.at[groups + 1]).wait()
    all_own().wait_recv()
    for distance in range(1, pairs):
        for below in (True, False):
            block = pair - distance if below else pair + distance

            @pl.when(block >= 0 if below else block < pairs)
            def _():
                with jax.named_scope("tokwait"):
                    for place, owner in ((1, second), (2, opposite)):
                        there = normed.at[block, quarter_of(owner), :]
                        remote(
                            there, there, peer_send, peer_recv.at[block, place - 1], partner
                        ).wait_recv()

    for to in range(2):
        rows_aside(core, 0, sides[to]).start()

    def head_layer_norm(values, scale_gain):
        average = jnp.mean(values, axis=-1, keepdims=True)
        centred = values - average
        variance = jnp.mean(centred * centred, axis=-1, keepdims=True)
        return (centred * lax.rsqrt(variance + epsilon) * scale_gain).astype(jnp.bfloat16)

    def head_place(block, h):
        return pl.ds(pl.multiple_of(block * width + h * HEAD_DIM, HEAD_DIM), HEAD_DIM)

    def context_hop(block, image, h, up):
        there = context.at[image, :, :, :, head_place(block, h)]
        return remote(
            there, there,
            c_send.at[0 if up else 1], c_recv.at[block, image, h],
            at_pair(pair + 1 if up else pair - 1),
        )

    def inside(image):
        return (image > 0) & (image < pairs - 1)

    def outside(image):
        return (image == 0) | (image == pairs - 1)

    def onward(image, up):
        if up:
            return has_up & ~((pair == pairs - 2) & inside(image))
        return has_down & ~((pair == 1) & inside(image))

    def awaited(block, image, up):
        if up:
            return (block >= 0) & ~((pair == pairs - 1) & inside(image))
        return (block < pairs) & ~((pair == 0) & inside(image))

    def send_context(image, h, across_middle, to_end):
        for up in (True, False):
            crossing = pair < pairs // 2 if up else pair >= pairs // 2
            wanted = (crossing & across_middle) | (~crossing & to_end)

            @pl.when(onward(image, up) & wanted)
            def _():
                context_hop(pair, image, h, up).start()

    def cross_context(image, h):
        for up in (True, False):
            @pl.when((pair == 1) if up else (pair == pairs - 2))
            def _():
                with jax.named_scope("crossctx"):
                    context_hop(outer, image, h, up).wait_recv()
                context_hop(outer, image, h, up).start()

    def pass_context(image, h, distance):
        for up in (True, False):
            block = pair - distance if up else pair + distance

            @pl.when(awaited(block, image, up) & ~(beside_end & (block == outer)))
            def _():
                with jax.named_scope("ctxwait%d" % distance):
                    context_hop(block, image, h, up).wait_recv()

                @pl.when(onward(image, up))
                def _():
                    context_hop(block, image, h, up).start()

    def half_over(image, h, at, owner):
        return remote(
            staged.at[image, h, quarter_of(owner), :],
            context.at[image, 1, at, :, head_place(pair, h)],
            x_send, x_recv.at[image, h], at_group(first),
        )

    def half_in(image, h):
        there = context.at[image, 1, :, :, head_place(pair, h)]
        with jax.named_scope("halfin"):
            remote(there, there, x_send, x_recv.at[image, h], partner).wait_recv()

    def attend_head(image, h):
        lanes = slice(h * HEAD_DIM, (h + 1) * HEAD_DIM)
        with jax.named_scope("attend"):
            total = jnp.dot(
                normed[image], weights[h].reshape(pairs * span, 3 * HEAD_DIM),
                preferred_element_type=jnp.float32,
            )
            queries = head_layer_norm(total[:, :HEAD_DIM], head_gain[0, :, lanes])
            key_rows = head_layer_norm(total[:, HEAD_DIM : 2 * HEAD_DIM], head_gain[1, :, lanes])
            value_rows = total[:, 2 * HEAD_DIM :].astype(jnp.bfloat16)
            scores = lax.dot_general(
                queries, key_rows, (((1,), (1,)), ((), ())), preferred_element_type=jnp.float32
            ) * (1.0 / math.sqrt(HEAD_DIM))
            highest = jnp.max(scores, axis=-1, keepdims=True)
            spread = jnp.exp(scores - highest)
            probs = (spread / jnp.sum(spread, axis=-1, keepdims=True)).astype(jnp.bfloat16)
            mixed = jnp.dot(probs, value_rows, preferred_element_type=jnp.float32)
            staged[image, h] = mixed.astype(jnp.bfloat16)

        for at, owner in enumerate((first, opposite)):
            half_over(image, h, at, owner).start()
        for at, owner in enumerate((group, second)):
            context[image, 0, at, :, head_place(pair, h)] = staged[image, h, quarter_of(owner), :]

    lower = pair < pairs // 2
    homely = jnp.where(lower, 1, pairs - 2)
    foreign = pairs - 1 - homely

    def image_at(step):
        if isinstance(step, int):
            return (0, pairs - 1, homely, foreign)[step]
        return jnp.where(step < 2, step * (pairs - 1), jnp.where(step == 2, homely, foreign))

    def projected_at(step):
        if isinstance(step, int):
            return (0, pairs - 1, foreign, homely)[step]
        return jnp.where(step < 2, step * (pairs - 1), jnp.where(step == 2, foreign, homely))

    def all_weights(h):
        with jax.named_scope("passedwait"):
            all_passed(h).wait_recv()

    all_weights(0)

    @pl.loop(0, pairs)
    def _(step):
        attend_head(image_at(step), 0)

    for to in range(2):
        rows_aside(core, 1, sides[to]).start()

    with jax.named_scope("sends"):
        for at in range(pairs):
            @pl.when(pair == at)
            def _():
                for way, blocks in ((0, at + 1 if at + 1 < pairs else 0), (1, pairs - at if at > 0 else 0)):
                    if blocks > 0:
                        there = normed.at[pl.ds(0, blocks), pl.ds(0, part), :]
                        remote(
                            there, there, token_send.at[way], token_recv.at[0, 0], partner
                        ).wait_send()
        there = normed.at[pl.ds(0, pairs - 1), pl.ds(0, 3 * part), :]
        remote(there, there, peer_send, peer_recv.at[0, 0], partner).wait_send()
        all_own().wait_send()
        out_over(1 - core).wait_recv()
        out_over(core).wait_send()


    def end_aside(k):
        for to in range(2):
            end_part(core, k, sides[to]).start()

    @pl.when(beside_end)
    def _():
        end_over(core).wait_recv()
        end_pass(core).start()
        end_aside(0)

    def partial_to(unit, c):
        return remote(
            partial.at[unit, c], arrived.at[unit, c], p_send, p_recv.at[unit, c], at_group(second)
        )

    def span_place(span_of, c):
        return pl.ds(pl.multiple_of(span_of * span + c * shard, 128), shard)

    def final_to(unit, c, image, span_of):
        return remote(
            summed.at[unit, c], result.at[:, span_place(span_of, c)], f_send, f_recv, at_pair(image)
        )

    def finals(count):
        there = summed.at[pl.ds(0, count)]
        return remote(there, there, f_send, f_recv, partner)

    def project(unit, image, rows_of):
        with jax.named_scope("outproj"):
            total = None
            for j in range(2):
                product = lax.dot_general(
                    context[image, j].reshape(2 * part, pairs * width), rows_of[j],
                    (((1,), (0,)), ((), ())), preferred_element_type=jnp.float32,
                )
                total = product if total is None else total + product
            for c in range(2):
                kept[unit, c] = total[:part, c * shard : (c + 1) * shard]
                partial[unit, c] = total[part:, c * shard : (c + 1) * shard].astype(jnp.bfloat16)
        for c in range(2):
            partial_to(unit, c).start()

    def add_up(unit, c, image, span_of):
        with jax.named_scope("partwait"):
            partial_to(unit, c).wait_recv()
        total = (kept[unit, c] + arrived[unit, c].astype(jnp.float32)).astype(jnp.bfloat16)

        @pl.when(image != pair)
        def _():
            summed[unit, c] = total
            final_to(unit, c, image, span_of).start()

        @pl.when(image == pair)
        def _():
            result[:, span_place(span_of, c)] = total

    def own_unit(image):
        return ~at_end | outside(image)

    def extra_unit(image):
        return beside_end & inside(image)

    def finish(image, extra):
        @pl.when(extra_unit(image) if extra else own_unit(image))
        def _():
            for c in range(2):
                add_up(pairs + image - 1 if extra else image, c, image, outer if extra else pair)

    for step in range(pairs):
        half_in(image_at(step), 0)
        send_context(image_at(step), 0, True, True)
    pass_weights(heads - 1)
    all_weights(heads - 1)

    def pass_most(image):
        for h in range(heads):
            pass_context(image, h, 1)
        pass_context(image, 0, 2)

    def pass_rest(image):
        pass_context(image, 1, 2)
        for h in range(heads):
            pass_context(image, h, 3)

    lag = 4

    @pl.loop(0, pairs + lag)
    def _(step):
        @pl.when(step < pairs)
        def _():
            attend_head(image_at(step), heads - 1)

        @pl.when(step == 0)
        def _():
            cross_context(image_at(0), 0)

        @pl.when((step > 0) & (step <= pairs))
        def _():
            image = image_at(step - 1)
            half_in(image, heads - 1)
            send_context(image, heads - 1, at_end | (step < 3), True)

            @pl.when(step < pairs)
            def _():
                cross_context(image_at(step), 0)

            for at, (turn, h, distance) in enumerate(((0, 0, 1), (1, 0, 1), (0, 0, 2))):
                @pl.when((step == at + 1) & beside_end)
                def _():
                    pass_context(image_at(turn), h, distance)

            @pl.when((step == pairs) & beside_end)
            def _():
                end_aside(1)

        @pl.when(step >= lag)
        def _():
            image = projected_at(step - lag)

            @pl.when(step == lag)
            def _():
                cross_context(image_at(0), heads - 1)

            @pl.when(step == lag + 3)
            def _():
                for early in range(2):
                    finish(projected_at(early), False)

            @pl.when(at_end | (step > lag + 1))
            def _():
                pass_most(image)

            @pl.when((step == lag) & beside_end)
            def _():
                pass_context(image_at(0), 1, 1)
                cross_context(image_at(1), heads - 1)
                send_context(image_at(2), heads - 1, True, False)
                pass_context(image_at(1), 1, 1)
                pass_context(image_at(1), 0, 2)
                cross_context(image_at(2), heads - 1)
                send_context(image_at(3), heads - 1, True, False)

            @pl.when(step == lag + 1)
            def _():
                cross_context(image_at(pairs - 1), heads - 1)

            pass_rest(image)

            @pl.when(own_unit(image))
            def _():
                @pl.when(step == lag)
                def _():
                    whole = out_rows.at[1]
                    remote(whole, whole, side_send, side_recv, partner).wait_recv()

                project(image, image, out_rows)

            @pl.when(extra_unit(image))
            def _():
                @pl.when(step == lag + 2)
                def _():
                    end_pass(1 - core).wait_recv()
                    with jax.named_scope("endrows"):
                        whole = end_rows.at[1]
                        remote(whole, whole, end_send.at[2], end_recv.at[2], partner).wait_recv()

                project(pairs + image - 1, image, end_rows)

    for turn in (2, 3):
        for extra in (False, True):
            finish(projected_at(turn), extra)

    with jax.named_scope("sends2"):
        others = weights.at[:, pl.ds(0, pairs - 1), core]
        remote(others, others, pass_send, pass_recv.at[0], partner).wait_send()
        remote(others, others, w_send, w_recv.at[0, 0], partner).wait_send()

        @pl.when(at_end)
        def _():
            end_over(core).wait_send()

        @pl.when(beside_end)
        def _():
            end_pass(core).wait_send()
            both = end_rows.at[0]
            remote(both, both, end_send.at[2], end_recv.at[2], partner).wait_send()

        def sent(way, images, blocks):
            there = context.at[pl.ds(0, images), :, :, :, pl.ds(0, blocks * width)]
            return remote(there, there, c_send.at[way], c_recv.at[0, 0, 0], partner)

        for at, counts in (
            (0, ((0, pairs, 1),)),
            (1, ((0, pairs, 2), (1, 2, pairs - 1))),
            (pairs - 2, ((0, 2, pairs - 1), (1, pairs, 2))),
            (pairs - 1, ((1, pairs, 1),)),
        ):
            @pl.when(pair == at)
            def _():
                for way, images, blocks in counts:
                    sent(way, images, blocks).wait_send()

    with jax.named_scope("sends3"):
        both = out_rows.at[0]
        remote(both, both, side_send, side_recv, partner).wait_send()
        half = staged.at[:, :, pl.ds(0, 2 * part), :]
        remote(half, half, x_send, x_recv.at[0, 0], partner).wait_send()
        for few, units in ((at_end, 2), (beside_end, 2 * pairs - 2)):
            @pl.when(few)
            def _():
                whole = partial.at[pl.ds(0, units)]
                remote(whole, whole, p_send, p_recv.at[0, 0], partner).wait_send()

    with jax.named_scope("finalwait"):
        @pl.when(at_end)
        def _():
            finals(pairs - 1).wait_recv()

        @pl.when(~at_end)
        def _():
            finals(pairs - 2).wait_recv()
    with jax.named_scope("sends4"):
        @pl.when(at_end)
        def _():
            finals(1).wait_send()

        @pl.when(~at_end)
        def _():
            finals(pairs).wait_send()


def exchanged_heads(pairs, groups, tokens, ln_gain, q_w, k_w, v_w, q_gain, k_gain, out_w):
    rows, features = tokens.shape
    shard, local_width = q_w.shape
    width = local_width // pairs
    heads = width // HEAD_DIM
    part = rows // groups
    chunks = min(CHUNKS, part // 16)
    units = 2 * pairs - 2
    dma = pltpu.SemaphoreType.DMA
    in_hbm = pl.BlockSpec(memory_space=pl.ANY)
    in_vmem = pl.BlockSpec(memory_space=pltpu.VMEM)
    bf16 = jnp.bfloat16
    return pl.pallas_call(
        functools.partial(exchange_kernel, pairs, groups, chunks),
        out_shape=pltpu.VMEM((part, features), bf16),
        in_specs=[in_hbm] * 8,
        out_specs=in_vmem,
        scratch_shapes=[
            pltpu.VMEM((1, features), jnp.float32),
            pltpu.VMEM((2, 1, width), jnp.float32),
            pltpu.VMEM((rows, features), bf16),
            pltpu.VMEM((pairs, rows, features), bf16),
            pltpu.VMEM((heads, pairs, 2, shard, 3 * HEAD_DIM), bf16),
            pltpu.VMEM((shard, local_width), bf16),
            pltpu.VMEM((2, local_width, 2 * shard), bf16),
            pltpu.VMEM((2, local_width, 2 * shard), bf16),
            pltpu.VMEM((pairs, heads, rows, HEAD_DIM), bf16),
            pltpu.VMEM((pairs, 2, 2, part, local_width), bf16),
            pltpu.VMEM((units, 2, part, shard), jnp.float32),
            pltpu.VMEM((units, 2, part, shard), bf16),
            pltpu.VMEM((units, 2, part, shard), bf16),
            pltpu.VMEM((units, 2, part, shard), bf16),
            dma((groups + 4,)), dma((2,)), dma((pairs, chunks)), dma, dma((pairs, chunks)), dma((pairs, 2)),
            dma, dma((pairs, 4)), dma, dma, dma, dma((heads,)), dma, dma, dma, dma,
            dma((3,)), dma((3,)), dma, dma((pairs, heads)), dma((2,)), dma((pairs, pairs, heads)),
            dma, dma((units, 2)), dma, dma,
        ],
        compiler_params=pltpu.CompilerParams(
            collective_id=0, has_side_effects=True, vmem_limit_bytes=60 * 1024 * 1024
        ),
    )(
        tokens, ln_gain.reshape(1, features), q_w, k_w, v_w,
        q_gain.reshape(pairs, 1, width), k_gain.reshape(pairs, 1, width), out_w,
    )


def on_device(tokens, ln_gain, q_w, k_w, v_w, q_gain, k_gain, out_w):
    devices = lax.axis_size("dp")
    groups = lax.axis_size("mp")
    pairs = devices // 2
    fits = (
        devices % 2 == 0
        and groups == 4
        and q_w.shape[1] % (pairs * HEAD_DIM) == 0
        and q_w.shape[0] % 128 == 0
        and tokens.shape[0] == IMG_TOKENS
        and tokens.shape[0] % (16 * groups) == 0
        and pairs == 4
        and q_w.shape[1] == 2 * pairs * HEAD_DIM
    )
    if fits:
        return exchanged_heads(pairs, groups, tokens, ln_gain, q_w, k_w, v_w, q_gain, k_gain, out_w)
    return gathered_weights(tokens, ln_gain, q_w, k_w, v_w, q_gain, k_gain, out_w)


def solution(mesh):
    in_specs = (
        P("dp", None),
        P(),
        P("dp", "mp"),
        P("dp", "mp"),
        P("dp", "mp"),
        P("mp"),
        P("mp"),
        P("dp", "mp"),
    )
    out_specs = P(("dp", "mp"), None)
    return jax.shard_map(
        on_device, mesh=mesh, in_specs=in_specs, out_specs=out_specs, check_vma=False
    )
```

```python
import functools
import math

import jax
import jax.numpy as jnp
from jax import lax
from jax.experimental import pallas as pl
from jax.experimental.pallas import tpu as pltpu
from jax.sharding import PartitionSpec as P

HEAD_DIM = 128
IMG_TOKENS = 256


epsilon = 1e-06


def layer_norm(values, scale_gain):
    average = jnp.mean(values, axis=-1, keepdims=True)
    centred = values - average
    variance = jnp.mean(centred * centred, axis=-1, keepdims=True)
    return centred * lax.rsqrt(variance + epsilon) * scale_gain


def head_norm(projected, scale_gain):
    heads_count = projected.shape[1] // HEAD_DIM
    shaped = projected.reshape(projected.shape[0], heads_count, HEAD_DIM)
    normed = layer_norm(shaped, scale_gain.reshape(heads_count, HEAD_DIM))
    return normed.reshape(projected.shape).astype(jnp.bfloat16)


def attend(queries, key_rows, value_rows):
    scores = jnp.einsum(
        "bqhd,bkhd->bhqk", queries, key_rows, preferred_element_type=jnp.float32
    ) * (1.0 / math.sqrt(HEAD_DIM))
    highest = jnp.max(scores, axis=-1, keepdims=True)
    weights = jnp.exp(scores - highest)
    probs = (weights / jnp.sum(weights, axis=-1, keepdims=True)).astype(jnp.bfloat16)
    context = jnp.einsum("bhqk,bkhd->bqhd", probs, value_rows, preferred_element_type=jnp.float32)
    return context.astype(jnp.bfloat16)


def place_three(holder, pieces, offset, local_width):
    holder = lax.dynamic_update_slice(holder, pieces[0], (offset, 0))
    holder = lax.dynamic_update_slice(holder, pieces[1], (offset, local_width))
    return lax.dynamic_update_slice(holder, pieces[2], (offset, 2 * local_width))


def gathered_weights(tokens, ln_gain, q_weight, k_weight, v_weight, q_gain, k_gain, out_weight):
    normed = layer_norm(tokens.astype(jnp.float32), ln_gain).astype(jnp.bfloat16)
    token_count = normed.shape[0]
    local_width = q_weight.shape[1]
    feature_count = normed.shape[1]
    stacked = jnp.zeros((feature_count, 3 * local_width), jnp.bfloat16)
    projections = place_three(
        stacked,
        (
            lax.all_gather(q_weight, "dp", axis=0, tiled=True),
            lax.all_gather(k_weight, "dp", axis=0, tiled=True),
            lax.all_gather(v_weight, "dp", axis=0, tiled=True),
        ),
        jnp.int32(0),
        local_width,
    )
    combined = jnp.dot(normed, projections, preferred_element_type=jnp.float32)
    queries = combined[:, :local_width]
    key_rows = combined[:, local_width : 2 * local_width]
    value_cast = combined[:, 2 * local_width :].astype(jnp.bfloat16)
    query_normed = head_norm(queries, q_gain)
    key_normed = head_norm(key_rows, k_gain)
    images = token_count // IMG_TOKENS
    shaped = (images, IMG_TOKENS, local_width // HEAD_DIM, HEAD_DIM)
    context = attend(
        query_normed.reshape(shaped), key_normed.reshape(shaped), value_cast.reshape(shaped)
    )
    context = context.reshape(token_count, local_width)
    out_full = lax.all_gather(out_weight, "dp", axis=0, tiled=True)
    return lax.psum_scatter(
        lax.dot_general(
            context, out_full, (((1,), (1,)), ((), ())), preferred_element_type=jnp.float32
        ).astype(jnp.bfloat16),
        "mp",
        scatter_dimension=0,
        tiled=True,
    )


MESH = pl.DeviceIdType.MESH

CHUNKS = 4


def exchange_kernel(
    pairs, groups, chunks, tokens, ln_gain_in, q_w, k_w, v_w, q_gain_in, k_gain_in, out_w, result,
    ln_gain, head_gain, raw, normed, weights, own_rows, out_rows, end_rows, staged, context, kept, partial, arrived, summed,
    local_sem, token_send, token_recv, peer_send, first_recv, peer_recv,
    w_send, w_recv, own_send, own_recv, pass_send, pass_recv, out_send, out_recv, side_send, side_recv,
    end_send, end_recv, x_send, x_recv, c_send, c_recv, p_send, p_recv, f_send, f_recv,
):
    dp = lax.axis_index("dp")
    group = lax.axis_index("mp")
    pair = dp // 2
    core = dp % 2
    rows = tokens.shape[0]
    part = rows // groups
    piece_rows = part // chunks
    shard = q_w.shape[0]
    width = q_w.shape[1] // pairs
    span = 2 * shard
    heads = width // HEAD_DIM
    has_up = pair + 1 < pairs
    has_down = pair > 0
    at_end = (pair == 0) | (pair == pairs - 1)
    beside_end = (pair == 1) | (pair == pairs - 2)
    inner = jnp.where(pair < pairs // 2, pair + 1, pair - 1)
    outer = jnp.where(pair < pairs // 2, pair - 1, pair + 1)

    def at_pair(other):
        return (other * 2 + core, group)

    partner = (pair * 2 + (1 - core), group)

    def at_group(other):
        return (dp, other)

    def remote(source, target, send, recv, device):
        return pltpu.make_async_remote_copy(
            src_ref=source, dst_ref=target, send_sem=send, recv_sem=recv,
            device_id=device, device_id_type=MESH,
        )

    def quarter_of(owner):
        return pl.ds(pl.multiple_of(owner * part, part), part)

    greeted = pltpu.get_barrier_semaphore()
    for step in range(1, pairs):
        pl.semaphore_signal(
            greeted, inc=1, device_id=at_pair((pair + step) % pairs), device_id_type=MESH
        )
    for step in range(1, groups):
        pl.semaphore_signal(
            greeted, inc=1, device_id=at_group((group + step) % groups), device_id_type=MESH
        )
    pl.semaphore_signal(greeted, inc=1, device_id=partner, device_id_type=MESH)
    beside = group + 1 - 2 * (group % 2)
    across = (group + 2) % 4
    pl.semaphore_signal(
        greeted, inc=1,
        device_id=(pair * 2 + 1 - core, jnp.where(core == 0, beside, across)), device_id_type=MESH,
    )

    gain_copy = pltpu.make_async_copy(ln_gain_in, ln_gain, local_sem.at[groups + 2])
    gain_copy.start()
    for at, gain in enumerate((q_gain_in, k_gain_in)):
        pltpu.make_async_copy(gain.at[pair], head_gain.at[at], local_sem.at[groups + 3]).start()
    token_quarters = []
    for j in range(groups):
        place = quarter_of((group + j) % groups)
        token_quarters.append(
            pltpu.make_async_copy(tokens.at[place, :], raw.at[place, :], local_sem.at[j])
        )
        token_quarters[j].start()

    projections = (q_w, k_w, v_w)

    def columns(other, h, t):
        start = pl.multiple_of(other * width + h * HEAD_DIM, HEAD_DIM)
        return projections[t].at[:, pl.ds(start, HEAD_DIM)]

    def slot(h, block, side, t):
        return weights.at[h, block, side, :, pl.ds(t * HEAD_DIM, HEAD_DIM)]

    locals_ = [pltpu.make_async_copy(out_w, own_rows, local_sem.at[groups])]
    for h in range(heads):
        for t in range(3):
            locals_.append(
                pltpu.make_async_copy(
                    columns(pair, h, t), slot(h, pair, core, t), local_sem.at[groups + 1],
                )
            )
    for copy in locals_:
        copy.start()

    def normalise(first_row, count):
        @pl.loop(0, count // 16)
        def _(step):
            place = pl.ds(pl.multiple_of(first_row + step * 16, 16), 16)
            values = raw[place, :].astype(jnp.float32)
            average = jnp.mean(values, axis=-1, keepdims=True)
            centred = values - average
            variance = jnp.mean(centred * centred, axis=-1, keepdims=True)
            scaled = centred * lax.rsqrt(variance + epsilon) * ln_gain[...]
            normed[pair, place, :] = scaled.astype(jnp.bfloat16)

    gain_copy.wait()
    token_quarters[0].wait()
    normalise(group * part, piece_rows)

    def piece(block, owner, k):
        start = pl.multiple_of(owner * part + k * piece_rows, 16)
        return normed.at[block, pl.ds(start, piece_rows), :]

    def z_hop(block, k, up):
        there = piece(block, group, k)
        return remote(
            there, there, token_send.at[0 if up else 1], token_recv.at[block, k],
            at_pair(pair + 1 if up else pair - 1),
        )

    first = jnp.where(core == 0, beside, across)
    second = jnp.where(core == 0, across, beside)
    opposite = 3 - group

    def peer_copy(block, owner, place, k, other):
        there = piece(block, owner, k)
        return remote(
            there, there, peer_send, first_recv.at[block, k] if place == 0 else peer_recv.at[block, place - 1], at_group(other)
        )

    def weight_to(other, h, t):
        return remote(
            columns(other, h, t), slot(h, pair, core, t),
            w_send, w_recv.at[pair, t if h > 0 else 3], at_pair(other),
        )

    def send_weights(up, plan):
        for h, distance in plan:
            other = pair + distance if up else pair - distance

            @pl.when(other < pairs if up else other >= 0)
            def _():
                for t in range(3):
                    weight_to(other, h, t).start()

    def own_weight(h, t):
        return remote(
            columns(pair, h, t), slot(h, pair, core, t), own_send, own_recv, partner
        )

    def side_of(rows_of, way, side, k=None):
        lanes = pl.ds(pl.multiple_of(side * shard, 128), shard)
        if k is None:
            return rows_of.at[way, :, lanes]
        depth = pairs * width // 2
        return rows_of.at[way, pl.ds(k * depth, depth), lanes]

    def transpose_rows():
        @pl.loop(0, pairs * width // 128)
        def _(k):
            place = pl.ds(pl.multiple_of(k * 128, 128), 128)
            lanes = pl.ds(pl.multiple_of(core * shard, 128), shard)
            out_rows[0, place, lanes] = jnp.transpose(own_rows[:, place])

    def out_over(side):
        there = side_of(out_rows, 0, side)
        return remote(there, there, out_send, out_recv, partner)

    sides = ((pair * 2, beside), (pair * 2 + 1, across))

    def rows_aside(side, k, device):
        return remote(
            side_of(out_rows, 0, side, k), side_of(out_rows, 1, side, k),
            side_send, side_recv, device,
        )

    with jax.named_scope("greet"):
        pl.semaphore_wait(greeted, pairs + groups)

    @pl.loop(0, chunks)
    def _(k):
        @pl.when(k > 0)
        def _():
            normalise(group * part + k * piece_rows, piece_rows)

        @pl.when(has_up)
        def _():
            z_hop(pair, k, True).start()

        @pl.when(has_down)
        def _():
            z_hop(pair, k, False).start()

    def end_over(side):
        return remote(
            side_of(out_rows, 0, side), side_of(end_rows, 0, side),
            end_send.at[0], end_recv.at[0], at_pair(inner),
        )

    def end_pass(side):
        there = side_of(end_rows, 0, side)
        return remote(there, there, end_send.at[1], end_recv.at[1], partner)

    def end_part(side, k, device):
        return remote(
            side_of(end_rows, 0, side, k), side_of(end_rows, 1, side, k),
            end_send.at[2], end_recv.at[2], device,
        )

    for at, up in ((0, True), (pairs - 1, False)):
        @pl.when(pair == at)
        def _():
            send_weights(up, [(h, 1) for h in range(heads)])
            send_weights(up, [(0, distance) for distance in range(2, pairs)])

    for h in range(heads):
        for t in range(3):
            own_weight(h, t).start()
    for j in range(1, groups):
        token_quarters[j].wait()
    pltpu.make_async_copy(head_gain, head_gain, local_sem.at[groups + 3]).wait()

    def relay(block, k, up):
        with jax.named_scope("relaywait"):
            z_hop(block, k, up).wait_recv()

        @pl.when(has_up if up else has_down)
        def _():
            z_hop(block, k, up).start()

        peer_copy(block, group, 0, k, first).start()
        peer_copy(block, group, 1, k, second).start()

    others = rows - part
    for distance in range(1, pairs):
        @pl.loop(0, chunks)
        def _(k):
            @pl.when(pair - distance >= 0)
            def _():
                relay(pair - distance, k, True)

            @pl.when(pair + distance < pairs)
            def _():
                relay(pair + distance, k, False)

            if distance == 1:
                for j in range(1, groups):
                    normalise(((group + j) % groups) * part + k * piece_rows, piece_rows)

        if distance == 1:
            with jax.named_scope("transpose"):
                locals_[0].wait()
                transpose_rows()
            out_over(core).start()
            for at, up in ((0, True), (pairs - 1, False)):
                @pl.when(pair == at)
                def _():
                    end_over(core).start()
                    send_weights(up, [(h, d) for h in range(1, heads) for d in range(pairs - 1, 1, -1)])

        @pl.when(has_up & (pair == distance))
        def _():
            send_weights(True, [(h, d) for h in range(heads) for d in range(1, pairs - 1)])

        @pl.when(has_down & (pair == pairs - 1 - distance))
        def _():
            send_weights(False, [(h, d) for h in range(heads) for d in range(1, pairs - 1)])

    def cross_tokens(block, k):
        with jax.named_scope("crosswait"):
            peer_copy(block, first, 0, k, first).wait_recv()
        peer_copy(block, first, 2, k, second).start()

    for distance in range(1, pairs):
        @pl.loop(0, chunks)
        def _(k):
            @pl.when(pair - distance >= 0)
            def _():
                cross_tokens(pair - distance, k)

            @pl.when(pair + distance < pairs)
            def _():
                cross_tokens(pair + distance, k)


    def pass_weights(h):
        for distance in range(1, pairs):
            for up in (True, False):
                other = pair - distance if up else pair + distance

                @pl.when(other >= 0 if up else other < pairs)
                def _():
                    pieces = [(slot(h, other, core, t), t) for t in range(3)]
                    if h == 0:
                        pieces = [(weights.at[h, other, core], 3)]
                    for there, at in pieces:
                        with jax.named_scope("wwait"):
                            remote(there, there, w_send, w_recv.at[other, at], partner).wait_recv()
                        remote(there, there, pass_send, pass_recv.at[h], partner).start()

    def all_passed(h):
        there = weights.at[h, pl.ds(0, pairs - 1), 1 - core]
        return remote(there, there, pass_send, pass_recv.at[h], partner)

    def all_own():
        there = weights.at[:, pair, 1 - core]
        return remote(there, there, own_send, own_recv, partner)

    pass_weights(0)
    there = weights.at[:, pair, core]
    pltpu.make_async_copy(there, there, local_sem.at[groups + 1]).wait()
    all_own().wait_recv()
    for distance in range(1, pairs):
        for below in (True, False):
            block = pair - distance if below else pair + distance

            @pl.when(block >= 0 if below else block < pairs)
            def _():
                with jax.named_scope("tokwait"):
                    for place, owner in ((1, second), (2, opposite)):
                        there = normed.at[block, quarter_of(owner), :]
                        remote(
                            there, there, peer_send, peer_recv.at[block, place - 1], partner
                        ).wait_recv()

    for to in range(2):
        rows_aside(core, 0, sides[to]).start()

    def head_layer_norm(values, scale_gain):
        average = jnp.mean(values, axis=-1, keepdims=True)
        centred = values - average
        variance = jnp.mean(centred * centred, axis=-1, keepdims=True)
        return (centred * lax.rsqrt(variance + epsilon) * scale_gain).astype(jnp.bfloat16)

    def head_place(block, h):
        return pl.ds(pl.multiple_of(block * width + h * HEAD_DIM, HEAD_DIM), HEAD_DIM)

    def context_hop(block, image, h, up):
        there = context.at[image, :, :, :, head_place(block, h)]
        return remote(
            there, there,
            c_send.at[0 if up else 1], c_recv.at[block, image, h],
            at_pair(pair + 1 if up else pair - 1),
        )

    def inside(image):
        return (image > 0) & (image < pairs - 1)

    def outside(image):
        return (image == 0) | (image == pairs - 1)

    def onward(image, up):
        if up:
            return has_up & ~((pair == pairs - 2) & inside(image))
        return has_down & ~((pair == 1) & inside(image))

    def awaited(block, image, up):
        if up:
            return (block >= 0) & ~((pair == pairs - 1) & inside(image))
        return (block < pairs) & ~((pair == 0) & inside(image))

    def send_context(image, h, across_middle, to_end):
        for up in (True, False):
            crossing = pair < pairs // 2 if up else pair >= pairs // 2
            wanted = (crossing & across_middle) | (~crossing & to_end)

            @pl.when(onward(image, up) & wanted)
            def _():
                context_hop(pair, image, h, up).start()

    def cross_context(image, h):
        for up in (True, False):
            @pl.when((pair == 1) if up else (pair == pairs - 2))
            def _():
                with jax.named_scope("crossctx"):
                    context_hop(outer, image, h, up).wait_recv()
                context_hop(outer, image, h, up).start()

    def pass_context(image, h, distance):
        for up in (True, False):
            block = pair - distance if up else pair + distance

            @pl.when(awaited(block, image, up) & ~(beside_end & (block == outer)))
            def _():
                with jax.named_scope("ctxwait%d" % distance):
                    context_hop(block, image, h, up).wait_recv()

                @pl.when(onward(image, up))
                def _():
                    context_hop(block, image, h, up).start()

    def half_over(image, h, at, owner):
        return remote(
            staged.at[image, h, quarter_of(owner), :],
            context.at[image, 1, at, :, head_place(pair, h)],
            x_send, x_recv.at[image, h], at_group(first),
        )

    def half_in(image, h):
        there = context.at[image, 1, :, :, head_place(pair, h)]
        with jax.named_scope("halfin"):
            remote(there, there, x_send, x_recv.at[image, h], partner).wait_recv()

    def attend_head(image, h):
        lanes = slice(h * HEAD_DIM, (h + 1) * HEAD_DIM)
        with jax.named_scope("attend"):
            total = jnp.dot(
                normed[image], weights[h].reshape(pairs * span, 3 * HEAD_DIM),
                preferred_element_type=jnp.float32,
            )
            queries = head_layer_norm(total[:, :HEAD_DIM], head_gain[0, :, lanes])
            key_rows = head_layer_norm(total[:, HEAD_DIM : 2 * HEAD_DIM], head_gain[1, :, lanes])
            value_rows = total[:, 2 * HEAD_DIM :].astype(jnp.bfloat16)
            scores = lax.dot_general(
                queries, key_rows, (((1,), (1,)), ((), ())), preferred_element_type=jnp.float32
            ) * (1.0 / math.sqrt(HEAD_DIM))
            highest = jnp.max(scores, axis=-1, keepdims=True)
            spread = jnp.exp(scores - highest)
            probs = (spread / jnp.sum(spread, axis=-1, keepdims=True)).astype(jnp.bfloat16)
            mixed = jnp.dot(probs, value_rows, preferred_element_type=jnp.float32)
            staged[image, h] = mixed.astype(jnp.bfloat16)

        for at, owner in enumerate((first, opposite)):
            half_over(image, h, at, owner).start()
        for at, owner in enumerate((group, second)):
            context[image, 0, at, :, head_place(pair, h)] = staged[image, h, quarter_of(owner), :]

    lower = pair < pairs // 2
    homely = jnp.where(lower, 1, pairs - 2)
    foreign = pairs - 1 - homely

    def image_at(step):
        if isinstance(step, int):
            return (0, pairs - 1, homely, foreign)[step]
        return jnp.where(step < 2, step * (pairs - 1), jnp.where(step == 2, homely, foreign))

    def projected_at(step):
        if isinstance(step, int):
            return (0, pairs - 1, foreign, homely)[step]
        return jnp.where(step < 2, step * (pairs - 1), jnp.where(step == 2, foreign, homely))

    def all_weights(h):
        with jax.named_scope("passedwait"):
            all_passed(h).wait_recv()

    all_weights(0)

    @pl.loop(0, pairs)
    def _(step):
        attend_head(image_at(step), 0)

    for to in range(2):
        rows_aside(core, 1, sides[to]).start()

    with jax.named_scope("sends"):
        for at in range(pairs):
            @pl.when(pair == at)
            def _():
                for way, blocks in ((0, at + 1 if at + 1 < pairs else 0), (1, pairs - at if at > 0 else 0)):
                    if blocks > 0:
                        there = normed.at[pl.ds(0, blocks), pl.ds(0, part), :]
                        remote(
                            there, there, token_send.at[way], token_recv.at[0, 0], partner
                        ).wait_send()
        there = normed.at[pl.ds(0, pairs - 1), pl.ds(0, 3 * part), :]
        remote(there, there, peer_send, peer_recv.at[0, 0], partner).wait_send()
        all_own().wait_send()
        out_over(1 - core).wait_recv()
        out_over(core).wait_send()


    def end_aside(k):
        for to in range(2):
            end_part(core, k, sides[to]).start()

    @pl.when(beside_end)
    def _():
        end_over(core).wait_recv()
        end_pass(core).start()
        end_aside(0)

    def partial_to(unit, c):
        return remote(
            partial.at[unit, c], arrived.at[unit, c], p_send, p_recv.at[unit, c], at_group(second)
        )

    def span_place(span_of, c):
        return pl.ds(pl.multiple_of(span_of * span + c * shard, 128), shard)

    def final_to(unit, c, image, span_of):
        return remote(
            summed.at[unit, c], result.at[:, span_place(span_of, c)], f_send, f_recv, at_pair(image)
        )

    def finals(count):
        there = summed.at[pl.ds(0, count)]
        return remote(there, there, f_send, f_recv, partner)

    def project(unit, image, rows_of):
        with jax.named_scope("outproj"):
            total = None
            for j in range(2):
                product = lax.dot_general(
                    context[image, j].reshape(2 * part, pairs * width), rows_of[j],
                    (((1,), (0,)), ((), ())), preferred_element_type=jnp.float32,
                )
                total = product if total is None else total + product
            for c in range(2):
                kept[unit, c] = total[:part, c * shard : (c + 1) * shard]
                partial[unit, c] = total[part:, c * shard : (c + 1) * shard].astype(jnp.bfloat16)
        for c in range(2):
            partial_to(unit, c).start()

    def add_up(unit, c, image, span_of):
        with jax.named_scope("partwait"):
            partial_to(unit, c).wait_recv()
        total = (kept[unit, c] + arrived[unit, c].astype(jnp.float32)).astype(jnp.bfloat16)

        @pl.when(image != pair)
        def _():
            summed[unit, c] = total
            final_to(unit, c, image, span_of).start()

        @pl.when(image == pair)
        def _():
            result[:, span_place(span_of, c)] = total

    def own_unit(image):
        return ~at_end | outside(image)

    def extra_unit(image):
        return beside_end & inside(image)

    def finish(image, extra):
        @pl.when(extra_unit(image) if extra else own_unit(image))
        def _():
            for c in range(2):
                add_up(pairs + image - 1 if extra else image, c, image, outer if extra else pair)

    for step in range(pairs):
        half_in(image_at(step), 0)
        send_context(image_at(step), 0, True, True)
    pass_weights(heads - 1)
    all_weights(heads - 1)

    def pass_most(image):
        for h in range(heads):
            pass_context(image, h, 1)
        pass_context(image, 0, 2)

    def pass_rest(image):
        pass_context(image, 1, 2)
        for h in range(heads):
            pass_context(image, h, 3)

    lag = 4

    @pl.loop(0, pairs + lag)
    def _(step):
        @pl.when(step < pairs)
        def _():
            attend_head(image_at(step), heads - 1)

        @pl.when(step == 0)
        def _():
            cross_context(image_at(0), 0)

        @pl.when((step > 0) & (step <= pairs))
        def _():
            image = image_at(step - 1)
            half_in(image, heads - 1)
            send_context(image, heads - 1, at_end | (step < 3), True)

            @pl.when(step < pairs)
            def _():
                cross_context(image_at(step), 0)

            for at, (turn, h, distance) in enumerate(((0, 0, 1), (1, 0, 1), (0, 0, 2))):
                @pl.when((step == at + 1) & beside_end)
                def _():
                    pass_context(image_at(turn), h, distance)

            @pl.when((step == pairs) & beside_end)
            def _():
                end_aside(1)

        @pl.when(step >= lag)
        def _():
            image = projected_at(step - lag)

            @pl.when(step == lag)
            def _():
                cross_context(image_at(0), heads - 1)

            @pl.when(at_end | (step > lag + 1))
            def _():
                pass_most(image)

            @pl.when((step == lag) & beside_end)
            def _():
                pass_context(image_at(0), 1, 1)
                cross_context(image_at(1), heads - 1)
                send_context(image_at(2), heads - 1, True, False)
                pass_context(image_at(1), 1, 1)
                pass_context(image_at(1), 0, 2)
                cross_context(image_at(2), heads - 1)
                send_context(image_at(3), heads - 1, True, False)

            @pl.when(step == lag + 1)
            def _():
                cross_context(image_at(pairs - 1), heads - 1)

            pass_rest(image)

            @pl.when(step == lag + 2)
            def _():
                finish(projected_at(0), False)

            @pl.when(own_unit(image))
            def _():
                @pl.when(step == lag)
                def _():
                    whole = out_rows.at[1]
                    remote(whole, whole, side_send, side_recv, partner).wait_recv()

                project(image, image, out_rows)

            @pl.when(step == lag + 2)
            def _():
                finish(projected_at(1), False)

            @pl.when(extra_unit(image))
            def _():
                @pl.when(step == lag + 2)
                def _():
                    end_pass(1 - core).wait_recv()
                    with jax.named_scope("endrows"):
                        whole = end_rows.at[1]
                        remote(whole, whole, end_send.at[2], end_recv.at[2], partner).wait_recv()

                project(pairs + image - 1, image, end_rows)

    for turn in (2, 3):
        for extra in (False, True):
            finish(projected_at(turn), extra)

    with jax.named_scope("sends2"):
        others = weights.at[:, pl.ds(0, pairs - 1), core]
        remote(others, others, pass_send, pass_recv.at[0], partner).wait_send()
        remote(others, others, w_send, w_recv.at[0, 0], partner).wait_send()

        @pl.when(at_end)
        def _():
            end_over(core).wait_send()

        @pl.when(beside_end)
        def _():
            end_pass(core).wait_send()
            both = end_rows.at[0]
            remote(both, both, end_send.at[2], end_recv.at[2], partner).wait_send()

        def sent(way, images, blocks):
            there = context.at[pl.ds(0, images), :, :, :, pl.ds(0, blocks * width)]
            return remote(there, there, c_send.at[way], c_recv.at[0, 0, 0], partner)

        for at, counts in (
            (0, ((0, pairs, 1),)),
            (1, ((0, pairs, 2), (1, 2, pairs - 1))),
            (pairs - 2, ((0, 2, pairs - 1), (1, pairs, 2))),
            (pairs - 1, ((1, pairs, 1),)),
        ):
            @pl.when(pair == at)
            def _():
                for way, images, blocks in counts:
                    sent(way, images, blocks).wait_send()

    with jax.named_scope("sends3"):
        both = out_rows.at[0]
        remote(both, both, side_send, side_recv, partner).wait_send()
        half = staged.at[:, :, pl.ds(0, 2 * part), :]
        remote(half, half, x_send, x_recv.at[0, 0], partner).wait_send()
        for few, units in ((at_end, 2), (beside_end, 2 * pairs - 2)):
            @pl.when(few)
            def _():
                whole = partial.at[pl.ds(0, units)]
                remote(whole, whole, p_send, p_recv.at[0, 0], partner).wait_send()

    with jax.named_scope("finalwait"):
        @pl.when(at_end)
        def _():
            finals(pairs - 1).wait_recv()

        @pl.when(~at_end)
        def _():
            finals(pairs - 2).wait_recv()
    with jax.named_scope("sends4"):
        @pl.when(at_end)
        def _():
            finals(1).wait_send()

        @pl.when(~at_end)
        def _():
            finals(pairs).wait_send()


def exchanged_heads(pairs, groups, tokens, ln_gain, q_w, k_w, v_w, q_gain, k_gain, out_w):
    rows, features = tokens.shape
    shard, local_width = q_w.shape
    width = local_width // pairs
    heads = width // HEAD_DIM
    part = rows // groups
    chunks = min(CHUNKS, part // 16)
    units = 2 * pairs - 2
    dma = pltpu.SemaphoreType.DMA
    in_hbm = pl.BlockSpec(memory_space=pl.ANY)
    in_vmem = pl.BlockSpec(memory_space=pltpu.VMEM)
    bf16 = jnp.bfloat16
    return pl.pallas_call(
        functools.partial(exchange_kernel, pairs, groups, chunks),
        out_shape=pltpu.VMEM((part, features), bf16),
        in_specs=[in_hbm] * 8,
        out_specs=in_vmem,
        scratch_shapes=[
            pltpu.VMEM((1, features), jnp.float32),
            pltpu.VMEM((2, 1, width), jnp.float32),
            pltpu.VMEM((rows, features), bf16),
            pltpu.VMEM((pairs, rows, features), bf16),
            pltpu.VMEM((heads, pairs, 2, shard, 3 * HEAD_DIM), bf16),
            pltpu.VMEM((shard, local_width), bf16),
            pltpu.VMEM((2, local_width, 2 * shard), bf16),
            pltpu.VMEM((2, local_width, 2 * shard), bf16),
            pltpu.VMEM((pairs, heads, rows, HEAD_DIM), bf16),
            pltpu.VMEM((pairs, 2, 2, part, local_width), bf16),
            pltpu.VMEM((units, 2, part, shard), jnp.float32),
            pltpu.VMEM((units, 2, part, shard), bf16),
            pltpu.VMEM((units, 2, part, shard), bf16),
            pltpu.VMEM((units, 2, part, shard), bf16),
            dma((groups + 4,)), dma((2,)), dma((pairs, chunks)), dma, dma((pairs, chunks)), dma((pairs, 2)),
            dma, dma((pairs, 4)), dma, dma, dma, dma((heads,)), dma, dma, dma, dma,
            dma((3,)), dma((3,)), dma, dma((pairs, heads)), dma((2,)), dma((pairs, pairs, heads)),
            dma, dma((units, 2)), dma, dma,
        ],
        compiler_params=pltpu.CompilerParams(
            collective_id=0, has_side_effects=True, vmem_limit_bytes=60 * 1024 * 1024
        ),
    )(
        tokens, ln_gain.reshape(1, features), q_w, k_w, v_w,
        q_gain.reshape(pairs, 1, width), k_gain.reshape(pairs, 1, width), out_w,
    )


def on_device(tokens, ln_gain, q_w, k_w, v_w, q_gain, k_gain, out_w):
    devices = lax.axis_size("dp")
    groups = lax.axis_size("mp")
    pairs = devices // 2
    fits = (
        devices % 2 == 0
        and groups == 4
        and q_w.shape[1] % (pairs * HEAD_DIM) == 0
        and q_w.shape[0] % 128 == 0
        and tokens.shape[0] == IMG_TOKENS
        and tokens.shape[0] % (16 * groups) == 0
        and pairs == 4
        and q_w.shape[1] == 2 * pairs * HEAD_DIM
    )
    if fits:
        return exchanged_heads(pairs, groups, tokens, ln_gain, q_w, k_w, v_w, q_gain, k_gain, out_w)
    return gathered_weights(tokens, ln_gain, q_w, k_w, v_w, q_gain, k_gain, out_w)


def solution(mesh):
    in_specs = (
        P("dp", None),
        P(),
        P("dp", "mp"),
        P("dp", "mp"),
        P("dp", "mp"),
        P("mp"),
        P("mp"),
        P("dp", "mp"),
    )
    out_specs = P(("dp", "mp"), None)
    return jax.shard_map(
        on_device, mesh=mesh, in_specs=in_specs, out_specs=out_specs, check_vma=False
    )
```

```python
import functools
import math

import jax
import jax.numpy as jnp
from jax import lax
from jax.experimental import pallas as pl
from jax.experimental.pallas import tpu as pltpu
from jax.sharding import PartitionSpec as P

HEAD_DIM = 128
IMG_TOKENS = 256


epsilon = 1e-06


def layer_norm(values, scale_gain):
    average = jnp.mean(values, axis=-1, keepdims=True)
    centred = values - average
    variance = jnp.mean(centred * centred, axis=-1, keepdims=True)
    return centred * lax.rsqrt(variance + epsilon) * scale_gain


def head_norm(projected, scale_gain):
    heads_count = projected.shape[1] // HEAD_DIM
    shaped = projected.reshape(projected.shape[0], heads_count, HEAD_DIM)
    normed = layer_norm(shaped, scale_gain.reshape(heads_count, HEAD_DIM))
    return normed.reshape(projected.shape).astype(jnp.bfloat16)


def attend(queries, key_rows, value_rows):
    scores = jnp.einsum(
        "bqhd,bkhd->bhqk", queries, key_rows, preferred_element_type=jnp.float32
    ) * (1.0 / math.sqrt(HEAD_DIM))
    highest = jnp.max(scores, axis=-1, keepdims=True)
    weights = jnp.exp(scores - highest)
    probs = (weights / jnp.sum(weights, axis=-1, keepdims=True)).astype(jnp.bfloat16)
    context = jnp.einsum("bhqk,bkhd->bqhd", probs, value_rows, preferred_element_type=jnp.float32)
    return context.astype(jnp.bfloat16)


def place_three(holder, pieces, offset, local_width):
    holder = lax.dynamic_update_slice(holder, pieces[0], (offset, 0))
    holder = lax.dynamic_update_slice(holder, pieces[1], (offset, local_width))
    return lax.dynamic_update_slice(holder, pieces[2], (offset, 2 * local_width))


def gathered_weights(tokens, ln_gain, q_weight, k_weight, v_weight, q_gain, k_gain, out_weight):
    normed = layer_norm(tokens.astype(jnp.float32), ln_gain).astype(jnp.bfloat16)
    token_count = normed.shape[0]
    local_width = q_weight.shape[1]
    feature_count = normed.shape[1]
    stacked = jnp.zeros((feature_count, 3 * local_width), jnp.bfloat16)
    projections = place_three(
        stacked,
        (
            lax.all_gather(q_weight, "dp", axis=0, tiled=True),
            lax.all_gather(k_weight, "dp", axis=0, tiled=True),
            lax.all_gather(v_weight, "dp", axis=0, tiled=True),
        ),
        jnp.int32(0),
        local_width,
    )
    combined = jnp.dot(normed, projections, preferred_element_type=jnp.float32)
    queries = combined[:, :local_width]
    key_rows = combined[:, local_width : 2 * local_width]
    value_cast = combined[:, 2 * local_width :].astype(jnp.bfloat16)
    query_normed = head_norm(queries, q_gain)
    key_normed = head_norm(key_rows, k_gain)
    images = token_count // IMG_TOKENS
    shaped = (images, IMG_TOKENS, local_width // HEAD_DIM, HEAD_DIM)
    context = attend(
        query_normed.reshape(shaped), key_normed.reshape(shaped), value_cast.reshape(shaped)
    )
    context = context.reshape(token_count, local_width)
    out_full = lax.all_gather(out_weight, "dp", axis=0, tiled=True)
    return lax.psum_scatter(
        lax.dot_general(
            context, out_full, (((1,), (1,)), ((), ())), preferred_element_type=jnp.float32
        ).astype(jnp.bfloat16),
        "mp",
        scatter_dimension=0,
        tiled=True,
    )


MESH = pl.DeviceIdType.MESH

CHUNKS = 4


def exchange_kernel(
    pairs, groups, chunks, tokens, ln_gain_in, q_w, k_w, v_w, q_gain_in, k_gain_in, out_w, result,
    ln_gain, head_gain, raw, normed, weights, own_rows, out_rows, end_rows, staged, context, kept, partial, arrived, summed,
    local_sem, token_send, token_recv, peer_send, first_recv, peer_recv,
    w_send, w_recv, own_send, own_recv, pass_send, pass_recv, out_send, out_recv, side_send, side_recv,
    end_send, end_recv, x_send, x_recv, c_send, c_recv, p_send, p_recv, f_send, f_recv,
):
    dp = lax.axis_index("dp")
    group = lax.axis_index("mp")
    pair = dp // 2
    core = dp % 2
    rows = tokens.shape[0]
    part = rows // groups
    piece_rows = part // chunks
    shard = q_w.shape[0]
    width = q_w.shape[1] // pairs
    span = 2 * shard
    heads = width // HEAD_DIM
    has_up = pair + 1 < pairs
    has_down = pair > 0
    at_end = (pair == 0) | (pair == pairs - 1)
    beside_end = (pair == 1) | (pair == pairs - 2)
    inner = jnp.where(pair < pairs // 2, pair + 1, pair - 1)
    outer = jnp.where(pair < pairs // 2, pair - 1, pair + 1)

    def at_pair(other):
        return (other * 2 + core, group)

    partner = (pair * 2 + (1 - core), group)

    def at_group(other):
        return (dp, other)

    def remote(source, target, send, recv, device):
        return pltpu.make_async_remote_copy(
            src_ref=source, dst_ref=target, send_sem=send, recv_sem=recv,
            device_id=device, device_id_type=MESH,
        )

    def quarter_of(owner):
        return pl.ds(pl.multiple_of(owner * part, part), part)

    greeted = pltpu.get_barrier_semaphore()
    for step in range(1, pairs):
        pl.semaphore_signal(
            greeted, inc=1, device_id=at_pair((pair + step) % pairs), device_id_type=MESH
        )
    for step in range(1, groups):
        pl.semaphore_signal(
            greeted, inc=1, device_id=at_group((group + step) % groups), device_id_type=MESH
        )
    pl.semaphore_signal(greeted, inc=1, device_id=partner, device_id_type=MESH)
    beside = group + 1 - 2 * (group % 2)
    across = (group + 2) % 4
    pl.semaphore_signal(
        greeted, inc=1,
        device_id=(pair * 2 + 1 - core, jnp.where(core == 0, beside, across)), device_id_type=MESH,
    )

    gain_copy = pltpu.make_async_copy(ln_gain_in, ln_gain, local_sem.at[groups + 2])
    gain_copy.start()
    for at, gain in enumerate((q_gain_in, k_gain_in)):
        pltpu.make_async_copy(gain.at[pair], head_gain.at[at], local_sem.at[groups + 3]).start()
    token_quarters = []
    for j in range(groups):
        place = quarter_of((group + j) % groups)
        token_quarters.append(
            pltpu.make_async_copy(tokens.at[place, :], raw.at[place, :], local_sem.at[j])
        )
        token_quarters[j].start()

    projections = (q_w, k_w, v_w)

    def columns(other, h, t):
        start = pl.multiple_of(other * width + h * HEAD_DIM, HEAD_DIM)
        return projections[t].at[:, pl.ds(start, HEAD_DIM)]

    def slot(h, block, side, t):
        return weights.at[h, block, side, :, pl.ds(t * HEAD_DIM, HEAD_DIM)]

    locals_ = [pltpu.make_async_copy(out_w, own_rows, local_sem.at[groups])]
    for h in range(heads):
        for t in range(3):
            locals_.append(
                pltpu.make_async_copy(
                    columns(pair, h, t), slot(h, pair, core, t), local_sem.at[groups + 1],
                )
            )
    for copy in locals_:
        copy.start()

    def normalise(first_row, count):
        @pl.loop(0, count // 16)
        def _(step):
            place = pl.ds(pl.multiple_of(first_row + step * 16, 16), 16)
            values = raw[place, :].astype(jnp.float32)
            average = jnp.mean(values, axis=-1, keepdims=True)
            centred = values - average
            variance = jnp.mean(centred * centred, axis=-1, keepdims=True)
            scaled = centred * lax.rsqrt(variance + epsilon) * ln_gain[...]
            normed[pair, place, :] = scaled.astype(jnp.bfloat16)

    gain_copy.wait()
    token_quarters[0].wait()
    normalise(group * part, piece_rows)

    def piece(block, owner, k):
        start = pl.multiple_of(owner * part + k * piece_rows, 16)
        return normed.at[block, pl.ds(start, piece_rows), :]

    def z_hop(block, k, up):
        there = piece(block, group, k)
        return remote(
            there, there, token_send.at[0 if up else 1], token_recv.at[block, k],
            at_pair(pair + 1 if up else pair - 1),
        )

    first = jnp.where(core == 0, beside, across)
    second = jnp.where(core == 0, across, beside)
    opposite = 3 - group

    def peer_copy(block, owner, place, k, other):
        there = piece(block, owner, k)
        return remote(
            there, there, peer_send, first_recv.at[block, k] if place == 0 else peer_recv.at[block, place - 1], at_group(other)
        )

    def weight_to(other, h, t):
        return remote(
            columns(other, h, t), slot(h, pair, core, t),
            w_send, w_recv.at[pair, t if h > 0 else 3], at_pair(other),
        )

    def send_weights(up, plan):
        for h, distance in plan:
            other = pair + distance if up else pair - distance

            @pl.when(other < pairs if up else other >= 0)
            def _():
                for t in range(3):
                    weight_to(other, h, t).start()

    def own_weight(h, t):
        return remote(
            columns(pair, h, t), slot(h, pair, core, t), own_send, own_recv, partner
        )

    def side_of(rows_of, way, side, k=None):
        lanes = pl.ds(pl.multiple_of(side * shard, 128), shard)
        if k is None:
            return rows_of.at[way, :, lanes]
        depth = pairs * width // 2
        return rows_of.at[way, pl.ds(k * depth, depth), lanes]

    def transpose_rows():
        @pl.loop(0, pairs * width // 128)
        def _(k):
            place = pl.ds(pl.multiple_of(k * 128, 128), 128)
            lanes = pl.ds(pl.multiple_of(core * shard, 128), shard)
            out_rows[0, place, lanes] = jnp.transpose(own_rows[:, place])

    def out_over(side):
        there = side_of(out_rows, 0, side)
        return remote(there, there, out_send, out_recv, partner)

    sides = ((pair * 2, beside), (pair * 2 + 1, across))

    def rows_aside(side, k, device):
        return remote(
            side_of(out_rows, 0, side, k), side_of(out_rows, 1, side, k),
            side_send, side_recv, device,
        )

    with jax.named_scope("greet"):
        pl.semaphore_wait(greeted, pairs + groups)

    @pl.loop(0, chunks)
    def _(k):
        @pl.when(k > 0)
        def _():
            normalise(group * part + k * piece_rows, piece_rows)

        @pl.when(has_up)
        def _():
            z_hop(pair, k, True).start()

        @pl.when(has_down)
        def _():
            z_hop(pair, k, False).start()

    def end_over(side):
        return remote(
            side_of(out_rows, 0, side), side_of(end_rows, 0, side),
            end_send.at[0], end_recv.at[0], at_pair(inner),
        )

    def end_pass(side):
        there = side_of(end_rows, 0, side)
        return remote(there, there, end_send.at[1], end_recv.at[1], partner)

    def end_part(side, k, device):
        return remote(
            side_of(end_rows, 0, side, k), side_of(end_rows, 1, side, k),
            end_send.at[2], end_recv.at[2], device,
        )

    for at, up in ((0, True), (pairs - 1, False)):
        @pl.when(pair == at)
        def _():
            send_weights(up, [(h, 1) for h in range(heads)])
            send_weights(up, [(0, distance) for distance in range(2, pairs)])

    for h in range(heads):
        for t in range(3):
            own_weight(h, t).start()
    for j in range(1, groups):
        token_quarters[j].wait()
    pltpu.make_async_copy(head_gain, head_gain, local_sem.at[groups + 3]).wait()

    def relay(block, k, up):
        with jax.named_scope("relaywait"):
            z_hop(block, k, up).wait_recv()

        @pl.when(has_up if up else has_down)
        def _():
            z_hop(block, k, up).start()

        peer_copy(block, group, 0, k, first).start()
        peer_copy(block, group, 1, k, second).start()

    others = rows - part
    for distance in range(1, pairs):
        @pl.loop(0, chunks)
        def _(k):
            @pl.when(pair - distance >= 0)
            def _():
                relay(pair - distance, k, True)

            @pl.when(pair + distance < pairs)
            def _():
                relay(pair + distance, k, False)

            if distance == 1:
                for j in range(1, groups):
                    normalise(((group + j) % groups) * part + k * piece_rows, piece_rows)

        if distance == 1:
            with jax.named_scope("transpose"):
                locals_[0].wait()
                transpose_rows()
            out_over(core).start()
            for at, up in ((0, True), (pairs - 1, False)):
                @pl.when(pair == at)
                def _():
                    end_over(core).start()
                    send_weights(up, [(h, d) for h in range(1, heads) for d in range(pairs - 1, 1, -1)])

        @pl.when(has_up & (pair == distance))
        def _():
            send_weights(True, [(h, d) for h in range(heads) for d in range(1, pairs - 1)])

        @pl.when(has_down & (pair == pairs - 1 - distance))
        def _():
            send_weights(False, [(h, d) for h in range(heads) for d in range(1, pairs - 1)])

    def cross_tokens(block, k):
        with jax.named_scope("crosswait"):
            peer_copy(block, first, 0, k, first).wait_recv()
        peer_copy(block, first, 2, k, second).start()

    for distance in range(1, pairs):
        @pl.loop(0, chunks)
        def _(k):
            @pl.when(pair - distance >= 0)
            def _():
                cross_tokens(pair - distance, k)

            @pl.when(pair + distance < pairs)
            def _():
                cross_tokens(pair + distance, k)


    def pass_weights(h):
        for distance in range(1, pairs):
            for up in (True, False):
                other = pair - distance if up else pair + distance

                @pl.when(other >= 0 if up else other < pairs)
                def _():
                    pieces = [(slot(h, other, core, t), t) for t in range(3)]
                    if h == 0:
                        pieces = [(weights.at[h, other, core], 3)]
                    for there, at in pieces:
                        with jax.named_scope("wwait"):
                            remote(there, there, w_send, w_recv.at[other, at], partner).wait_recv()
                        remote(there, there, pass_send, pass_recv.at[h], partner).start()

    def all_passed(h):
        there = weights.at[h, pl.ds(0, pairs - 1), 1 - core]
        return remote(there, there, pass_send, pass_recv.at[h], partner)

    def all_own():
        there = weights.at[:, pair, 1 - core]
        return remote(there, there, own_send, own_recv, partner)

    pass_weights(0)
    there = weights.at[:, pair, core]
    pltpu.make_async_copy(there, there, local_sem.at[groups + 1]).wait()
    all_own().wait_recv()
    for distance in range(1, pairs):
        for below in (True, False):
            block = pair - distance if below else pair + distance

            @pl.when(block >= 0 if below else block < pairs)
            def _():
                with jax.named_scope("tokwait"):
                    for place, owner in ((1, second), (2, opposite)):
                        there = normed.at[block, quarter_of(owner), :]
                        remote(
                            there, there, peer_send, peer_recv.at[block, place - 1], partner
                        ).wait_recv()

    for to in range(2):
        rows_aside(core, 0, sides[to]).start()

    def head_layer_norm(values, scale_gain):
        average = jnp.mean(values, axis=-1, keepdims=True)
        centred = values - average
        variance = jnp.mean(centred * centred, axis=-1, keepdims=True)
        return (centred * lax.rsqrt(variance + epsilon) * scale_gain).astype(jnp.bfloat16)

    def head_place(block, h):
        return pl.ds(pl.multiple_of(block * width + h * HEAD_DIM, HEAD_DIM), HEAD_DIM)

    def context_hop(block, image, h, up):
        there = context.at[image, :, :, :, head_place(block, h)]
        return remote(
            there, there,
            c_send.at[0 if up else 1], c_recv.at[block, image, h],
            at_pair(pair + 1 if up else pair - 1),
        )

    def inside(image):
        return (image > 0) & (image < pairs - 1)

    def outside(image):
        return (image == 0) | (image == pairs - 1)

    def onward(image, up):
        if up:
            return has_up & ~((pair == pairs - 2) & inside(image))
        return has_down & ~((pair == 1) & inside(image))

    def awaited(block, image, up):
        if up:
            return (block >= 0) & ~((pair == pairs - 1) & inside(image))
        return (block < pairs) & ~((pair == 0) & inside(image))

    def send_context(image, h, across_middle, to_end):
        for up in (True, False):
            crossing = pair < pairs // 2 if up else pair >= pairs // 2
            wanted = (crossing & across_middle) | (~crossing & to_end)

            @pl.when(onward(image, up) & wanted)
            def _():
                context_hop(pair, image, h, up).start()

    def cross_context(image, h):
        for up in (True, False):
            @pl.when((pair == 1) if up else (pair == pairs - 2))
            def _():
                with jax.named_scope("crossctx"):
                    context_hop(outer, image, h, up).wait_recv()
                context_hop(outer, image, h, up).start()

    def pass_context(image, h, distance):
        for up in (True, False):
            block = pair - distance if up else pair + distance

            @pl.when(awaited(block, image, up) & ~(beside_end & (block == outer)))
            def _():
                with jax.named_scope("ctxwait%d" % distance):
                    context_hop(block, image, h, up).wait_recv()

                @pl.when(onward(image, up))
                def _():
                    context_hop(block, image, h, up).start()

    def half_over(image, h, at, owner):
        return remote(
            staged.at[image, h, quarter_of(owner), :],
            context.at[image, 1, at, :, head_place(pair, h)],
            x_send, x_recv.at[image if h > 0 else pairs], at_group(first),
        )

    def half_in(image, h):
        there = context.at[image, 1, :, :, head_place(pair, h)]
        with jax.named_scope("halfin"):
            remote(there, there, x_send, x_recv.at[image], partner).wait_recv()

    def attend_head(image, h):
        lanes = slice(h * HEAD_DIM, (h + 1) * HEAD_DIM)
        with jax.named_scope("attend"):
            total = jnp.dot(
                normed[image], weights[h].reshape(pairs * span, 3 * HEAD_DIM),
                preferred_element_type=jnp.float32,
            )
            queries = head_layer_norm(total[:, :HEAD_DIM], head_gain[0, :, lanes])
            key_rows = head_layer_norm(total[:, HEAD_DIM : 2 * HEAD_DIM], head_gain[1, :, lanes])
            value_rows = total[:, 2 * HEAD_DIM :].astype(jnp.bfloat16)
            scores = lax.dot_general(
                queries, key_rows, (((1,), (1,)), ((), ())), preferred_element_type=jnp.float32
            ) * (1.0 / math.sqrt(HEAD_DIM))
            highest = jnp.max(scores, axis=-1, keepdims=True)
            spread = jnp.exp(scores - highest)
            probs = (spread / jnp.sum(spread, axis=-1, keepdims=True)).astype(jnp.bfloat16)
            mixed = jnp.dot(probs, value_rows, preferred_element_type=jnp.float32)
            staged[image, h] = mixed.astype(jnp.bfloat16)

        for at, owner in enumerate((first, opposite)):
            half_over(image, h, at, owner).start()
        for at, owner in enumerate((group, second)):
            context[image, 0, at, :, head_place(pair, h)] = staged[image, h, quarter_of(owner), :]

    lower = pair < pairs // 2
    homely = jnp.where(lower, 1, pairs - 2)
    foreign = pairs - 1 - homely

    def image_at(step):
        if isinstance(step, int):
            return (0, pairs - 1, homely, foreign)[step]
        return jnp.where(step < 2, step * (pairs - 1), jnp.where(step == 2, homely, foreign))

    def projected_at(step):
        if isinstance(step, int):
            return (0, pairs - 1, foreign, homely)[step]
        return jnp.where(step < 2, step * (pairs - 1), jnp.where(step == 2, foreign, homely))

    def all_weights(h):
        with jax.named_scope("passedwait"):
            all_passed(h).wait_recv()

    all_weights(0)

    @pl.loop(0, pairs)
    def _(step):
        attend_head(image_at(step), 0)

    for to in range(2):
        rows_aside(core, 1, sides[to]).start()

    with jax.named_scope("sends"):
        for at in range(pairs):
            @pl.when(pair == at)
            def _():
                for way, blocks in ((0, at + 1 if at + 1 < pairs else 0), (1, pairs - at if at > 0 else 0)):
                    if blocks > 0:
                        there = normed.at[pl.ds(0, blocks), pl.ds(0, part), :]
                        remote(
                            there, there, token_send.at[way], token_recv.at[0, 0], partner
                        ).wait_send()
        there = normed.at[pl.ds(0, pairs - 1), pl.ds(0, 3 * part), :]
        remote(there, there, peer_send, peer_recv.at[0, 0], partner).wait_send()
        all_own().wait_send()
        out_over(1 - core).wait_recv()
        out_over(core).wait_send()


    def end_aside(k):
        for to in range(2):
            end_part(core, k, sides[to]).start()

    @pl.when(beside_end)
    def _():
        end_over(core).wait_recv()
        end_pass(core).start()
        end_aside(0)

    def partial_to(unit, c):
        return remote(
            partial.at[unit, c], arrived.at[unit, c], p_send, p_recv.at[unit, c], at_group(second)
        )

    def span_place(span_of, c):
        return pl.ds(pl.multiple_of(span_of * span + c * shard, 128), shard)

    def final_to(unit, c, image, span_of):
        return remote(
            summed.at[unit, c], result.at[:, span_place(span_of, c)], f_send, f_recv, at_pair(image)
        )

    def finals(count):
        there = summed.at[pl.ds(0, count)]
        return remote(there, there, f_send, f_recv, partner)

    def project(unit, image, rows_of):
        with jax.named_scope("outproj"):
            total = None
            for j in range(2):
                product = lax.dot_general(
                    context[image, j].reshape(2 * part, pairs * width), rows_of[j],
                    (((1,), (0,)), ((), ())), preferred_element_type=jnp.float32,
                )
                total = product if total is None else total + product
            for c in range(2):
                kept[unit, c] = total[:part, c * shard : (c + 1) * shard]
                partial[unit, c] = total[part:, c * shard : (c + 1) * shard].astype(jnp.bfloat16)
        for c in range(2):
            partial_to(unit, c).start()

    def add_up(unit, c, image, span_of):
        with jax.named_scope("partwait"):
            partial_to(unit, c).wait_recv()
        total = (kept[unit, c] + arrived[unit, c].astype(jnp.float32)).astype(jnp.bfloat16)

        @pl.when(image != pair)
        def _():
            summed[unit, c] = total
            final_to(unit, c, image, span_of).start()

        @pl.when(image == pair)
        def _():
            result[:, span_place(span_of, c)] = total

    def own_unit(image):
        return ~at_end | outside(image)

    def extra_unit(image):
        return beside_end & inside(image)

    def finish(image, extra):
        @pl.when(extra_unit(image) if extra else own_unit(image))
        def _():
            for c in range(2):
                add_up(pairs + image - 1 if extra else image, c, image, outer if extra else pair)

    halves_in = context.at[:, 1, :, :, head_place(pair, 0)]
    remote(halves_in, halves_in, x_send, x_recv.at[pairs], partner).wait_recv()
    for step in range(pairs):
        send_context(image_at(step), 0, True, True)
    pass_weights(heads - 1)
    all_weights(heads - 1)

    def pass_most(image):
        for h in range(heads):
            pass_context(image, h, 1)
        pass_context(image, 0, 2)

    def pass_rest(image):
        pass_context(image, 1, 2)
        for h in range(heads):
            pass_context(image, h, 3)

    lag = 4

    @pl.loop(0, pairs + lag)
    def _(step):
        @pl.when(step < pairs)
        def _():
            attend_head(image_at(step), heads - 1)

        @pl.when(step == 0)
        def _():
            cross_context(image_at(0), 0)

        @pl.when((step > 0) & (step <= pairs))
        def _():
            image = image_at(step - 1)
            half_in(image, heads - 1)
            send_context(image, heads - 1, at_end | (step < 3), True)

            @pl.when(step < pairs)
            def _():
                cross_context(image_at(step), 0)

            for at, (turn, h, distance) in enumerate(((0, 0, 1), (1, 0, 1), (0, 0, 2))):
                @pl.when((step == at + 1) & beside_end)
                def _():
                    pass_context(image_at(turn), h, distance)

            @pl.when((step == pairs) & beside_end)
            def _():
                end_aside(1)

        @pl.when(step >= lag)
        def _():
            image = projected_at(step - lag)

            @pl.when(step == lag)
            def _():
                cross_context(image_at(0), heads - 1)

            @pl.when(at_end | (step > lag + 1))
            def _():
                pass_most(image)

            @pl.when((step == lag) & beside_end)
            def _():
                pass_context(image_at(0), 1, 1)
                cross_context(image_at(1), heads - 1)
                send_context(image_at(2), heads - 1, True, False)
                pass_context(image_at(1), 1, 1)
                pass_context(image_at(1), 0, 2)
                cross_context(image_at(2), heads - 1)
                send_context(image_at(3), heads - 1, True, False)

            @pl.when(step == lag + 1)
            def _():
                cross_context(image_at(pairs - 1), heads - 1)

            pass_rest(image)

            @pl.when(step == lag + 2)
            def _():
                finish(projected_at(0), False)

            @pl.when(own_unit(image))
            def _():
                @pl.when(step == lag)
                def _():
                    whole = out_rows.at[1]
                    remote(whole, whole, side_send, side_recv, partner).wait_recv()

                project(image, image, out_rows)

            @pl.when(step == lag + 2)
            def _():
                finish(projected_at(1), False)

            @pl.when(extra_unit(image))
            def _():
                @pl.when(step == lag + 2)
                def _():
                    end_pass(1 - core).wait_recv()
                    with jax.named_scope("endrows"):
                        whole = end_rows.at[1]
                        remote(whole, whole, end_send.at[2], end_recv.at[2], partner).wait_recv()

                project(pairs + image - 1, image, end_rows)

    for turn in (2, 3):
        for extra in (False, True):
            finish(projected_at(turn), extra)

    with jax.named_scope("sends2"):
        others = weights.at[:, pl.ds(0, pairs - 1), core]
        remote(others, others, pass_send, pass_recv.at[0], partner).wait_send()
        remote(others, others, w_send, w_recv.at[0, 0], partner).wait_send()

        @pl.when(at_end)
        def _():
            end_over(core).wait_send()

        @pl.when(beside_end)
        def _():
            end_pass(core).wait_send()
            both = end_rows.at[0]
            remote(both, both, end_send.at[2], end_recv.at[2], partner).wait_send()

        def sent(way, images, blocks):
            there = context.at[pl.ds(0, images), :, :, :, pl.ds(0, blocks * width)]
            return remote(there, there, c_send.at[way], c_recv.at[0, 0, 0], partner)

        for at, counts in (
            (0, ((0, pairs, 1),)),
            (1, ((0, pairs, 2), (1, 2, pairs - 1))),
            (pairs - 2, ((0, 2, pairs - 1), (1, pairs, 2))),
            (pairs - 1, ((1, pairs, 1),)),
        ):
            @pl.when(pair == at)
            def _():
                for way, images, blocks in counts:
                    sent(way, images, blocks).wait_send()

    with jax.named_scope("sends3"):
        both = out_rows.at[0]
        remote(both, both, side_send, side_recv, partner).wait_send()
        half = staged.at[:, :, pl.ds(0, 2 * part), :]
        remote(half, half, x_send, x_recv.at[0], partner).wait_send()
        for few, units in ((at_end, 2), (beside_end, 2 * pairs - 2)):
            @pl.when(few)
            def _():
                whole = partial.at[pl.ds(0, units)]
                remote(whole, whole, p_send, p_recv.at[0, 0], partner).wait_send()

    with jax.named_scope("finalwait"):
        @pl.when(at_end)
        def _():
            finals(pairs - 1).wait_recv()

        @pl.when(~at_end)
        def _():
            finals(pairs - 2).wait_recv()
    with jax.named_scope("sends4"):
        @pl.when(at_end)
        def _():
            finals(1).wait_send()

        @pl.when(~at_end)
        def _():
            finals(pairs).wait_send()


def exchanged_heads(pairs, groups, tokens, ln_gain, q_w, k_w, v_w, q_gain, k_gain, out_w):
    rows, features = tokens.shape
    shard, local_width = q_w.shape
    width = local_width // pairs
    heads = width // HEAD_DIM
    part = rows // groups
    chunks = min(CHUNKS, part // 16)
    units = 2 * pairs - 2
    dma = pltpu.SemaphoreType.DMA
    in_hbm = pl.BlockSpec(memory_space=pl.ANY)
    in_vmem = pl.BlockSpec(memory_space=pltpu.VMEM)
    bf16 = jnp.bfloat16
    return pl.pallas_call(
        functools.partial(exchange_kernel, pairs, groups, chunks),
        out_shape=pltpu.VMEM((part, features), bf16),
        in_specs=[in_hbm] * 8,
        out_specs=in_vmem,
        scratch_shapes=[
            pltpu.VMEM((1, features), jnp.float32),
            pltpu.VMEM((2, 1, width), jnp.float32),
            pltpu.VMEM((rows, features), bf16),
            pltpu.VMEM((pairs, rows, features), bf16),
            pltpu.VMEM((heads, pairs, 2, shard, 3 * HEAD_DIM), bf16),
            pltpu.VMEM((shard, local_width), bf16),
            pltpu.VMEM((2, local_width, 2 * shard), bf16),
            pltpu.VMEM((2, local_width, 2 * shard), bf16),
            pltpu.VMEM((pairs, heads, rows, HEAD_DIM), bf16),
            pltpu.VMEM((pairs, 2, 2, part, local_width), bf16),
            pltpu.VMEM((units, 2, part, shard), jnp.float32),
            pltpu.VMEM((units, 2, part, shard), bf16),
            pltpu.VMEM((units, 2, part, shard), bf16),
            pltpu.VMEM((units, 2, part, shard), bf16),
            dma((groups + 4,)), dma((2,)), dma((pairs, chunks)), dma, dma((pairs, chunks)), dma((pairs, 2)),
            dma, dma((pairs, 4)), dma, dma, dma, dma((heads,)), dma, dma, dma, dma,
            dma((3,)), dma((3,)), dma, dma((pairs + 1,)), dma((2,)), dma((pairs, pairs, heads)),
            dma, dma((units, 2)), dma, dma,
        ],
        compiler_params=pltpu.CompilerParams(
            collective_id=0, has_side_effects=True, vmem_limit_bytes=60 * 1024 * 1024
        ),
    )(
        tokens, ln_gain.reshape(1, features), q_w, k_w, v_w,
        q_gain.reshape(pairs, 1, width), k_gain.reshape(pairs, 1, width), out_w,
    )


def on_device(tokens, ln_gain, q_w, k_w, v_w, q_gain, k_gain, out_w):
    devices = lax.axis_size("dp")
    groups = lax.axis_size("mp")
    pairs = devices // 2
    fits = (
        devices % 2 == 0
        and groups == 4
        and q_w.shape[1] % (pairs * HEAD_DIM) == 0
        and q_w.shape[0] % 128 == 0
        and tokens.shape[0] == IMG_TOKENS
        and tokens.shape[0] % (16 * groups) == 0
        and pairs == 4
        and q_w.shape[1] == 2 * pairs * HEAD_DIM
    )
    if fits:
        return exchanged_heads(pairs, groups, tokens, ln_gain, q_w, k_w, v_w, q_gain, k_gain, out_w)
    return gathered_weights(tokens, ln_gain, q_w, k_w, v_w, q_gain, k_gain, out_w)


def solution(mesh):
    in_specs = (
        P("dp", None),
        P(),
        P("dp", "mp"),
        P("dp", "mp"),
        P("dp", "mp"),
        P("mp"),
        P("mp"),
        P("dp", "mp"),
    )
    out_specs = P(("dp", "mp"), None)
    return jax.shard_map(
        on_device, mesh=mesh, in_specs=in_specs, out_specs=out_specs, check_vma=False
    )
```
